128 devices in a mesh: row: 16 (over z, x_hi, core), col: 8 (over y, x_lo).
Axes of the slice: x: 4 (x_hi: 2, x_lo: 2; x = x_hi * 2 + x_lo), y: 4, z: 4, core: 2. Of those that a mesh axis runs over, the one named last changes fastest.
Arguments:
- tensor_slab: float32 [1024, 262144], P(None, ('row', 'col')), may hold values from 0.25 to 1500, as said below
- left_init: float32 [1024, 128], replicated, may hold values from 0.15 to 1.5
- right_init: float32 [128, 262144], P(None, ('row', 'col')), may hold values from 0.1 to 1
- second_left_init: float32 [65536, 128], P('row'), may hold values from 0.1 to 1
- second_right_init: float32 [128, 512], P(None, 'col'), may hold values from 0.003 to 0.03
Outputs:
- left_out: float32 [1024, 128], replicated
- second_left_out: float32 [65536, 128], P(('row', 'col'))
The draws below stay inside these ranges and needn't reach their ends.
Inputs may be any that keep to these rules, and one draw needn't show every extreme that they name: `tensor_slab`: every entry is positive.
All inputs are finite; a program needn't handle non-finite values.
Results may differ from the reference program's by a relative error of at most 0.0003.
Values sent between devices are 32-bit elements; how exact they have to be, the bound alone decides.
A program may use at most 128 MiB of HBM per device.

```python
import math
from functools import partial
import jax
import jax.numpy as jnp
from jax import lax

M = 1024
R = 128
K = 512
COLS_DEV = 2048
J = 512
NCOLS = 262144
ROWS2 = 65536


def draw_tensor_slab(key, part):
    row_key, col_key, jitter_key = jax.random.split(key, 3)
    position = jnp.arange(NCOLS, dtype=jnp.float32)[None, :] / NCOLS
    rising = jnp.exp(position * math.log(3.0))
    row_scale = jnp.exp(jax.random.uniform(row_key, (M, 1), jnp.float32, 0.0, math.log(10.0)))
    jitter = jnp.exp(jax.random.uniform(jitter_key, (M, NCOLS), jnp.float32, math.log(0.5), math.log(2.0)))
    col_scale = jnp.exp(jax.random.uniform(col_key, (1, NCOLS), jnp.float32, 0.0, math.log(10.0))) * rising
    return (row_scale * col_scale * jitter).astype(jnp.float32)


def block_levels(key, extent, cuts, low, top_value):
    def one(dim, shards_of):
        heights = jax.random.uniform(jax.random.fold_in(jax.random.fold_in(key, 6), dim), (shards_of,), jnp.float32, low / len(cuts), top_value / len(cuts))
        return jnp.repeat(jnp.exp(heights), extent[dim] // shards_of).reshape((-1,) + (1,) * (len(extent) - dim - 1))

    loudness = one(*cuts[0])
    for cut in cuts[1:]:
        loudness = loudness * one(*cut)
    return loudness


def setup_inputs(seed: int = 0) -> dict:
    key_list = jax.random.split(jax.random.key(seed), 6)
    return {
        "tensor_slab": draw_tensor_slab(jax.random.fold_in(key_list[5], 71), 0),
        "left_init": jnp.clip(jnp.exp(jax.random.uniform(key_list[1], (M, R), jnp.float32, math.log(0.15), math.log(1.5))), 0.15, 1.5),
        "right_init": jnp.clip(jnp.exp(math.log(1.0) - 2.3025851 * jax.random.uniform(key_list[2], (R, NCOLS), jnp.float32) ** block_levels(key_list[2], (R, NCOLS), ((1, 128),), -0.2, 0.2)), 0.1, 1.0),
        "second_left_init": jnp.clip(jnp.exp(math.log(1.0) - 2.3025851 * jax.random.uniform(key_list[3], (ROWS2, R), jnp.float32) ** block_levels(key_list[3], (ROWS2, R), ((0, 16),), -0.2, 0.2)), 0.1, 1.0),
        "second_right_init": jnp.clip(jnp.exp(math.log(0.03) - 2.3025851 * jax.random.uniform(key_list[4], (R, K), jnp.float32) ** block_levels(key_list[4], (R, K), ((1, 8),), -0.2, 0.2)), 0.003, 0.03),
    }


def segment_block(tensor_slab, left_fac, right_fac, col_sums, index_block):
    first_col = index_block.astype(jnp.int32) * COLS_DEV
    slab_part = lax.dynamic_slice_in_dim(tensor_slab, first_col, COLS_DEV, 1)
    right_part = lax.dynamic_slice_in_dim(right_fac, first_col, COLS_DEV, 1)
    product = jnp.dot(left_fac, right_part, precision=lax.Precision.HIGHEST)
    quotient = slab_part / product
    numerator = lax.dot_general(left_fac, quotient, (((0,), (0,)), ((), ())), precision=lax.Precision.HIGHEST)
    right_new = right_part * numerator / col_sums[:, None]
    product = jnp.dot(left_fac, right_new, precision=lax.Precision.HIGHEST)
    quotient = slab_part / product
    left_numer = lax.dot_general(quotient, right_new, (((1,), (1,)), ((), ())), precision=lax.Precision.HIGHEST)
    return right_new, left_numer, jnp.sum(right_new, axis=1)


def reference(tensor_slab, left_init, right_init, second_left_init, second_right_init):
    left_fac = left_init
    right_fac = right_init
    for repeat in range(2):
        col_sums = jnp.sum(left_fac, axis=0)
        pieces = lax.map(partial(segment_block, tensor_slab, left_fac, right_fac, col_sums),
                         jnp.arange(NCOLS // COLS_DEV, dtype=jnp.int32))
        right_blocks, left_numers, row_sums = pieces
        right_fac = jnp.transpose(right_blocks, (1, 0, 2)).reshape(R, NCOLS)
        left_fac = left_fac * jnp.sum(left_numers, axis=0) / jnp.sum(row_sums, axis=0)[None, :]
    unfolded = right_fac.reshape(R * J, K)
    product = jnp.dot(second_left_init, second_right_init, precision=lax.Precision.HIGHEST)
    numerator = lax.dot_general(second_left_init, unfolded / product, (((0,), (0,)), ((), ())), precision=lax.Precision.HIGHEST)
    second_right = second_right_init * numerator / jnp.sum(second_left_init, axis=0)[:, None]
    product = jnp.dot(second_left_init, second_right, precision=lax.Precision.HIGHEST)
    left_numer = lax.dot_general(unfolded / product, second_right, (((1,), (1,)), ((), ())), precision=lax.Precision.HIGHEST)
    second_left_out = second_left_init * left_numer / jnp.sum(second_right, axis=1)[None, :]
    return left_fac, second_left_out
```

```python
import functools

import jax
import jax.numpy as jnp
from jax import lax
from jax.experimental import pallas as pl
from jax.experimental.pallas import tpu as pltpu
from jax.sharding import PartitionSpec as P

F32 = jnp.float32
BF16 = jnp.bfloat16
NN = (((1,), (0,)), ((), ()))
NT = (((1,), (1,)), ((), ()))


def mm(a, b, dims=NN):
    return lax.dot_general(a, b, dims, preferred_element_type=F32)


def split(x):
    high = x.astype(BF16)
    low = (x - high.astype(F32)).astype(BF16)
    return high, low


def inverse(x):
    guess = pl.reciprocal(x, approx=True)
    return guess * (2.0 - x * guess)


def three(high, low, axis):
    return jnp.concatenate([high, high, low], axis=axis)


def other_three(high, low, axis):
    return jnp.concatenate([high, low, high], axis=axis)


def kernel(sizes, slab, left, right, sleft, sright, left_out, second_out, *scratch):
    (rows, cols, m, r, w, jl, depth) = sizes
    (slab_v, left_v, right_v, sleft_v, sright_v, left3, left_t, rcat, mult, sums_v,
     sa, ra, la, sc, rc, lc, sb, rb, sright_new, cb, outv, keep,
     slab_sem, in_sem, send_sem, recv_sem) = scratch
    d = rows * cols
    nb = slab_v.shape[0]
    mc = m // d
    rt = min(m, 256)
    nt = m // rt
    kc = sright_v.shape[0] // 1
    my_row, my_col = lax.axis_index("row"), lax.axis_index("col")
    me = my_row * cols + my_col

    def peer(k):
        t = lax.rem(me + k, d)
        return t, (lax.div(t, cols), lax.rem(t, cols))

    def wait(ref, sem):
        pltpu.make_async_copy(ref, ref, sem).wait()

    def remote(src, dst, phase, dev):
        return pltpu.make_async_remote_copy(
            src, dst, send_sem.at[phase], recv_sem.at[phase],
            device_id=dev, device_id_type=pl.DeviceIdType.MESH)

    left_in = pltpu.make_async_copy(left, left_v, in_sem.at[0])
    left_in.start()
    block_copies = []
    for i in range(nb):
        part = pl.ds(i * w, w)
        a = pltpu.make_async_copy(right.at[:, part], right_v.at[i], slab_sem.at[nb + i])
        b = pltpu.make_async_copy(slab.at[:, part], slab_v.at[i], slab_sem.at[i])
        a.start()
        b.start()
    barrier = pltpu.get_barrier_semaphore()

    def greet(k, _):
        pl.semaphore_signal(barrier, inc=1, device_id=peer(k)[1],
                            device_id_type=pl.DeviceIdType.MESH)
        return 0

    lax.fori_loop(1, d, greet, 0)
    own_sleft = pltpu.make_async_copy(
        sleft.at[:, me], sleft_v.at[pl.ds(my_row * (r // rows), r // rows)], in_sem.at[1])
    own_sleft.start()
    own_sright = pltpu.make_async_copy(sright, sright_v.at[my_col], in_sem.at[2])
    own_sright.start()

    def prepare(source):
        value = source[...]
        high, low = split(value)
        left3[...] = three(high, low, 1)
        turned = value.T
        high, low = split(turned)
        left_t[...] = jnp.concatenate([high, low], axis=0)
        return 1.0 / jnp.sum(turned, axis=1, keepdims=True)

    ones = jnp.ones((8, w), BF16)

    def right_half(inv_c, first):
        sums_v[...] = jnp.zeros_like(sums_v)

        def block(i, _):
            if first:
                wait(right_v.at[0], slab_sem.at[nb + i])
                wait(slab_v.at[0], slab_sem.at[i])
            old = right_v[i]
            high, low = split(old)
            r3 = other_three(high, low, 0)
            total = jnp.zeros((r, w), F32)
            for t in range(nt):
                part = slice(t * rt, (t + 1) * rt)
                product = mm(left3[part, :], r3)
                quotient = slab_v[i, part, :] * inverse(product)
                high, low = split(quotient)
                both = mm(left_t[:, part], high)
                total += both[:r] + both[r:] + mm(left_t[:r, part], low)
            new = old * (total * inv_c)
            right_v[i] = new
            high, low = split(new)
            pair = jnp.concatenate([high, low], axis=0)
            rcat[i] = pair
            both = mm(ones, pair, NT)
            sums_v[...] += both[:, :r] + both[:, r:]
            return 0

        lax.fori_loop(0, nb, block, 0)

    def left_half(store):
        def tile(t, _):
            part = pl.ds(t * rt, rt)
            total = jnp.zeros((rt, r), F32)
            lhs = left3[part, :]
            for i in range(nb):
                pair = rcat[i]
                high, low = pair[:r], pair[r:]
                product = mm(lhs, other_three(high, low, 0))
                quotient = slab_v[i, part, :] * inverse(product)
                qh, ql = split(quotient)
                both = mm(qh, pair, NT)
                total += both[:, :r] + both[:, r:] + mm(ql, high, NT)
            store(t, total)
            return 0

        lax.fori_loop(0, nt, tile, 0)

    def scatter(phase, source, dest, size):
        def send(k, _):
            t, dev = peer(k)
            remote(source.at[t, pl.ds(0, size)], dest.at[k - 1, pl.ds(0, size)], phase, dev).start()
            return 0

        lax.fori_loop(1, d, send, 0)

    def gather(phase, source, dest):
        def send(k, _):
            _, dev = peer(k)
            remote(source, dest, phase, dev).start()
            return 0

        lax.fori_loop(1, d, send, 0)

    left_in.wait()
    inv_c = prepare(left_v)
    pl.semaphore_wait(barrier, d - 1)

    def send_sleft(k, _):
        a = lax.rem(my_row + k, rows)
        remote(sleft.at[:, a * cols + my_col],
               sleft_v.at[pl.ds(my_row * (r // rows), r // rows)], 0, (a, my_col)).start()
        return 0

    lax.fori_loop(1, rows, send_sleft, 0)

    def send_sright(k, _):
        b = lax.rem(my_col + k, cols)
        remote(sright, sright_v.at[my_col], 1, (my_row, b)).start()
        return 0

    lax.fori_loop(1, cols, send_sright, 0)

    right_half(inv_c, True)
    own_sleft.wait()
    wait(sleft_v.at[pl.ds(0, r - r // rows)], recv_sem.at[0])
    own_sright.wait()
    wait(sright_v.at[pl.ds(0, cols - 1)], recv_sem.at[1])
    part2 = jnp.zeros((1, r), F32)
    for j in range(jl):
        part2 += jnp.sum(sleft_v[:, j, :], axis=0, keepdims=True)
    line = lax.broadcasted_iota(jnp.int32, (8, r), 0)

    def numer_store(buffer, extra):
        buffer[:, 8:16, :] = jnp.broadcast_to(extra[None], (d, 8, r))

        def store(t, total):
            buffer[pl.ds(t * (rt // mc), rt // mc), 0:mc, :] = total.reshape(rt // mc, mc, r)

        return store

    sums = sums_v[...]
    left_half(numer_store(sa, jnp.where(line == 0, sums, part2)))
    scatter(2, sa, ra, 10)
    own = sa[me]
    old = left_v[pl.ds(me * mc, mc), :]
    wait(ra.at[:, pl.ds(0, 10)], recv_sem.at[2])
    numer = own[:mc] + jnp.sum(ra[:, 0:mc, :], axis=0)
    tail = own[8:10] + jnp.sum(ra[:, 8:10, :], axis=0)
    keep[...] = jnp.broadcast_to(tail[1:2], (8, r))
    new = old * numer / tail[0:1]
    lc[...] = new
    la[pl.ds(me * mc, mc), :] = new
    gather(3, lc, la.at[pl.ds(me * mc, mc)])
    wait(la.at[pl.ds(0, m - mc)], recv_sem.at[3])

    inv_c = prepare(la)
    right_half(inv_c, False)

    per = depth // w
    numer2 = [jnp.zeros((w, r), F32) for _ in range(per)]
    for h in range(per):
        kh = sright_v[pl.ds(h * (cols // per), cols // per)].reshape(w, r)
        high, low = split(kh)
        s3 = other_three(high, low, 1)
        for j in range(jl):
            rows_j = sleft_v[:, j, :]
            high, low = split(rows_j)
            product = mm(three(high, low, 1), s3, NT)
            quotient = right_v[j * per + h] * inverse(product)
            qh, ql = split(quotient.T)
            both = mm(qh, jnp.concatenate([high, low], axis=1))
            numer2[h] += both[:, :r] + both[:, r:] + mm(ql, high)
    own_k = depth // d
    for h in range(per):
        sc[pl.ds(h * (d // per), d // per)] = numer2[h].reshape(d // per, own_k, r)
    scatter(4, sc, rc, own_k)

    left_half(numer_store(sb, sums_v[...]))
    scatter(6, sb, rb, 9)

    wait(rc, recv_sem.at[4])
    numer = sc[me] + jnp.sum(rc[...], axis=0)
    cb[...] = sright_v.reshape(d, own_k, r)[me] * numer / keep[0:1]
    sright_new[me] = cb[...]
    gather(5, cb, sright_new.at[me])

    own = sb[me]
    old = la[pl.ds(me * mc, mc), :]
    wait(sright_new.at[pl.ds(0, d - 1)], recv_sem.at[5])
    fresh = sright_new[...].reshape(depth, r)
    inv_u = 1.0 / jnp.sum(fresh, axis=0, keepdims=True)
    for j in range(jl):
        rows_j = sleft_v[:, j, :]
        high, low = split(rows_j)
        lhs = three(high, low, 1)
        total = jnp.zeros((r, r), F32)
        for h in range(per):
            high, low = split(fresh[h * w:(h + 1) * w])
            product = mm(lhs, other_three(high, low, 1), NT)
            quotient = right_v[j * per + h] * inverse(product)
            qh, ql = split(quotient)
            both = mm(qh, jnp.concatenate([high, low], axis=1))
            total += both[:, :r] + both[:, r:] + mm(ql, high)
        outv[:, j, :] = rows_j * (total * inv_u)

    def send_out(k, _):
        t, dev = peer(k)
        remote(outv.at[t], second_out.at[me], 7, dev).start()
        return 0

    lax.fori_loop(1, d, send_out, 0)
    own_out = pltpu.make_async_copy(outv.at[me], second_out.at[me], in_sem.at[1])
    own_out.start()

    wait(rb.at[:, pl.ds(0, 9)], recv_sem.at[6])
    numer = own[:mc] + jnp.sum(rb[:, 0:mc, :], axis=0)
    tail = own[8:9] + jnp.sum(rb[:, 8:9, :], axis=0)
    mult[...] = old * numer / tail
    gather(8, mult, left_out.at[pl.ds(me * mc, mc)])
    own_left = pltpu.make_async_copy(mult, left_out.at[pl.ds(me * mc, mc)], in_sem.at[2])
    own_left.start()
    own_out.wait()
    own_left.wait()
    wait(second_out.at[pl.ds(0, d - 1)], recv_sem.at[7])
    wait(left_out.at[pl.ds(0, m - mc)], recv_sem.at[8])
    wait(sleft_v.at[pl.ds(0, r - r // rows)], send_sem.at[0])
    wait(sright_v.at[pl.ds(0, cols - 1)], send_sem.at[1])
    wait(ra.at[:, pl.ds(0, 10)], send_sem.at[2])
    wait(la.at[pl.ds(0, m - mc)], send_sem.at[3])
    wait(rc, send_sem.at[4])
    wait(sright_new.at[pl.ds(0, d - 1)], send_sem.at[5])
    wait(rb.at[:, pl.ds(0, 9)], send_sem.at[6])
    wait(second_out.at[pl.ds(0, d - 1)], send_sem.at[7])
    wait(left_out.at[pl.ds(0, m - mc)], send_sem.at[8])


def solution(mesh):
    rows, cols = mesh.shape["row"], mesh.shape["col"]
    d = rows * cols

    def body(slab, left, right, sleft, sright):
        m, width = slab.shape
        r = left.shape[1]
        depth = sright.shape[1] * cols
        jl = width // depth
        w = depth // 2
        nb = width // w
        mc = m // d
        own_k = depth // d
        sleft = sleft.reshape(r // rows, d, jl, r)
        sright = sright.T.reshape(d // cols, own_k, r)
        hbm = pl.BlockSpec(memory_space=pl.ANY)
        left_out, second = pl.pallas_call(
            functools.partial(kernel, (rows, cols, m, r, w, jl, depth)),
            out_shape=(jax.ShapeDtypeStruct((m, r), F32),
                       jax.ShapeDtypeStruct((d, jl, r), F32)),
            in_specs=[hbm] * 5,
            out_specs=(hbm, hbm),
            scratch_shapes=[
                pltpu.VMEM((nb, m, w), F32),
                pltpu.VMEM((m, r), F32),
                pltpu.VMEM((nb, r, w), F32),
                pltpu.VMEM((r, jl, r), F32),
                pltpu.VMEM((cols, d // cols, own_k, r), F32),
                pltpu.VMEM((m, 3 * r), BF16),
                pltpu.VMEM((2 * r, m), BF16),
                pltpu.VMEM((nb, 2 * r, w), BF16),
                pltpu.VMEM((mc, r), F32),
                pltpu.VMEM((8, r), F32),
                pltpu.VMEM((d, 16, r), F32),
                pltpu.VMEM((d - 1, 16, r), F32),
                pltpu.VMEM((m, r), F32),
                pltpu.VMEM((d, own_k, r), F32),
                pltpu.VMEM((d - 1, own_k, r), F32),
                pltpu.VMEM((mc, r), F32),
                pltpu.VMEM((d, 16, r), F32),
                pltpu.VMEM((d - 1, 16, r), F32),
                pltpu.VMEM((d, own_k, r), F32),
                pltpu.VMEM((own_k, r), F32),
                pltpu.VMEM((d, jl, r), F32),
                pltpu.VMEM((8, r), F32),
                pltpu.SemaphoreType.DMA((2 * nb,)),
                pltpu.SemaphoreType.DMA((3,)),
                pltpu.SemaphoreType.DMA((9,)),
                pltpu.SemaphoreType.DMA((9,)),
            ],
            compiler_params=pltpu.CompilerParams(
                collective_id=0, has_side_effects=True, vmem_limit_bytes=60 * 1024 * 1024),
        )(slab, left, right, sleft, sright)
        return left_out, second.reshape(d * jl, r)

    placed = (P(None, ("row", "col")), P(), P(None, ("row", "col")), P("row", None), P(None, "col"))
    return jax.shard_map(
        body, mesh=mesh, in_specs=placed, out_specs=(P(), P(("row", "col"), None)), check_vma=False
    )
```

```python
import contextlib
import functools

import jax
import jax.numpy as jnp
from jax import lax
from jax.experimental import pallas as pl
from jax.experimental.pallas import tpu as pltpu
from jax.sharding import PartitionSpec as P

F32 = jnp.float32
BF16 = jnp.bfloat16
NN = (((1,), (0,)), ((), ()))
NT = (((1,), (1,)), ((), ()))
TILES = 4


def scope(_):
    return contextlib.nullcontext()


def mm(a, b, dims=NN):
    return lax.dot_general(a, b, dims, preferred_element_type=F32)


def split(x):
    high = x.astype(BF16)
    low = (x - high.astype(F32)).astype(BF16)
    return high, low


def inverse(x):
    guess = pl.reciprocal(x, approx=True)
    return guess * (2.0 - x * guess)


def three(high, low, axis):
    return jnp.concatenate([high, high, low], axis=axis)


def other_three(high, low, axis):
    return jnp.concatenate([high, low, high], axis=axis)


def kernel(sizes, slab, left, right, sleft, sright, left_out, second_out, *scratch):
    (rows, cols, m, r, w, jl, depth) = sizes
    (slab_v, left_v, right_v, sleft_v, sright_v, left3, left_t, rcat, nacc, mult, sums_v, csum,
     sa, ra, la, sc, rc, lc, sb, rb, sright_new, cb, outv, keep,
     slab_sem, in_sem, send_sem, recv_sem) = scratch
    d = rows * cols
    nt = TILES
    rt = m // nt
    nb = rcat.shape[0]
    mc = m // d
    dt = d // nt
    own_k = depth // d
    per = depth // w
    rr = r // rows
    my_row, my_col = lax.axis_index("row"), lax.axis_index("col")
    me = my_row * cols + my_col
    my_z = lax.div(me, dt)
    my_in = lax.rem(me, dt)

    def wait(ref, sem):
        pltpu.make_async_copy(ref, ref, sem).wait()

    def remote(src, dst, phase, to, recv=None):
        return pltpu.make_async_remote_copy(
            src, dst, send_sem.at[phase], recv_sem.at[phase if recv is None else recv],
            device_id=to, device_id_type=pl.DeviceIdType.LOGICAL)

    def near_first(q):
        return lax.rem(my_z + lax.div(q * (q + 1), 2), nt)

    def to_plane(z, start):
        def send(k, _):
            t = z * dt + lax.rem(my_in + k, dt)
            start(t, lax.rem(t - me + d, d) - 1)
            return 0

        own = z == my_z

        @pl.when(jnp.logical_not(own))
        def _():
            send(0, 0)

        lax.fori_loop(1, dt, send, 0)

    def to_all(start):
        def plane(q, _):
            to_plane(near_first(q), start)
            return 0

        lax.fori_loop(0, nt, plane, 0)

    with scope("start"):
        left_in = pltpu.make_async_copy(left, left_v, in_sem.at[0])
        left_in.start()
        right_in = pltpu.make_async_copy(right, right_v, in_sem.at[3])
        right_in.start()
        for t in range(nt):
            part = pl.ds(t * rt, rt)
            pltpu.make_async_copy(slab.at[part], slab_v.at[part], slab_sem.at[t]).start()
        barrier = pltpu.get_barrier_semaphore()

        def greet(k, _):
            pl.semaphore_signal(barrier, inc=1, device_id=lax.rem(me + k, d),
                                device_id_type=pl.DeviceIdType.LOGICAL)
            return 0

        lax.fori_loop(1, d, greet, 0)
        own_sleft = pltpu.make_async_copy(
            sleft.at[:, me], sleft_v.at[pl.ds(my_row * rr, rr)], in_sem.at[1])
        own_sleft.start()
        own_sright = pltpu.make_async_copy(sright, sright_v.at[my_col], in_sem.at[2])
        own_sright.start()

    def prepare(source, t):
        value = source[pl.ds(t * rt, rt), :]
        high, low = split(value)
        left3[t] = three(high, low, 1)
        turned = value.T
        high, low = split(turned)
        left_t[t] = jnp.concatenate([high, low], axis=0)
        csum[...] += jnp.broadcast_to(jnp.sum(turned, axis=1, keepdims=True), csum.shape)

    ones = jnp.ones((8, w), BF16)

    def right_tile(t):
        part = pl.ds(t * rt, rt)
        lhs = left3[t]
        turned = left_t[t]
        for i in range(nb):
            pair = rcat[i]
            product = mm(lhs, other_three(pair[:r], pair[r:], 0))
            quotient = slab_v[part, i * w:(i + 1) * w] * inverse(product)
            high, low = split(quotient)
            both = mm(turned, high)
            nacc[i] += both[:r] + both[r:] + mm(turned[:r], low)

    def right_finish():
        inv_c = 1.0 / csum[:, 0:1]
        sums = jnp.zeros((8, r), F32)
        for i in range(nb):
            cut = slice(i * w, (i + 1) * w)
            new = right_v[:, cut] * (nacc[i] * inv_c)
            right_v[:, cut] = new
            high, low = split(new)
            pair = jnp.concatenate([high, low], axis=0)
            rcat[i] = pair
            both = mm(ones, pair, NT)
            sums += both[:, :r] + both[:, r:]
        sums_v[...] = sums

    def left_tile(t, buffer):
        part = pl.ds(t * rt, rt)
        total = jnp.zeros((rt, r), F32)
        lhs = left3[t]
        for i in range(nb):
            pair = rcat[i]
            high, low = pair[:r], pair[r:]
            product = mm(lhs, other_three(high, low, 0))
            quotient = slab_v[part, i * w:(i + 1) * w] * inverse(product)
            qh, ql = split(quotient)
            both = mm(qh, pair, NT)
            total += both[:, :r] + both[:, r:] + mm(ql, high, NT)
        buffer[pl.ds(t * dt, dt), 0:mc, :] = total.reshape(dt, mc, r)

    def reset():
        nacc[...] = jnp.zeros_like(nacc)
        csum[...] = jnp.zeros_like(csum)

    with scope("prep"):
        reset()
        right_in.wait()
        for i in range(nb):
            high, low = split(right_v[:, i * w:(i + 1) * w])
            rcat[i] = jnp.concatenate([high, low], axis=0)
        left_in.wait()

    with scope("right1"):
        def first(t, _):
            prepare(left_v, t)
            wait(slab_v.at[pl.ds(0, rt)], slab_sem.at[t])
            right_tile(t)
            return 0

        lax.fori_loop(0, nt, first, 0)
        right_finish()

    with scope("barrier"):
        pl.semaphore_wait(barrier, d - 1)

    with scope("sendin"):
        def send_sleft(k, _):
            t = lax.rem(my_row + k, rows) * cols + my_col
            remote(sleft.at[:, t], sleft_v.at[pl.ds(my_row * rr, rr)], 0, t).start()
            return 0

        lax.fori_loop(1, rows, send_sleft, 0)

        def send_sright(k, _):
            t = my_row * cols + lax.rem(my_col + k, cols)
            remote(sright, sright_v.at[my_col], 1, t).start()
            return 0

        lax.fori_loop(1, cols, send_sright, 0)

    line = lax.broadcasted_iota(jnp.int32, (8, r), 0)
    with scope("left1"):
        sa[:, 8:16, :] = jnp.broadcast_to(sums_v[...][None], (d, 8, r))

        def tile1(q, _):
            t = near_first(nt - 1 - q)
            left_tile(t, sa)
            to_plane(t, lambda to, slot: remote(
                sa.at[to, pl.ds(0, 9)], ra.at[slot, pl.ds(0, 9)], 2, to).start())
            return 0

        lax.fori_loop(0, nt, tile1, 0)

    with scope("waitin"):
        own_sleft.wait()
        wait(sleft_v.at[pl.ds(0, r - rr)], recv_sem.at[0])
        own_sright.wait()
        wait(sright_v.at[pl.ds(0, cols - 1)], recv_sem.at[1])
        part2 = jnp.zeros((1, r), F32)
        for j in range(jl):
            part2 += jnp.sum(sleft_v[:, j, :], axis=0, keepdims=True)
        reset()

    with scope("rs1wait"):
        own = sa[me]
        old = left_v[pl.ds(me * mc, mc), :]
        wait(ra.at[:, pl.ds(0, 9)], recv_sem.at[2])
    with scope("rs1sum"):
        numer = own[:mc] + jnp.sum(ra[:, 0:mc, :], axis=0)
        tail = own[8:9] + jnp.sum(ra[:, 8:9, :], axis=0)
        new = old * numer / tail
        lc[...] = new
        la[pl.ds(me * mc, mc), :] = new
    with scope("ag1send"):
        to_all(lambda to, slot: remote(lc, la.at[pl.ds(me * mc, mc)], 3, to, 9 + my_z).start())

    with scope("right2"):
        def second(q, _):
            t = near_first(q)

            @pl.when(q == 0)
            def _():
                wait(la.at[pl.ds(0, rt - mc)], recv_sem.at[9 + t])

            @pl.when(q != 0)
            def _():
                wait(la.at[pl.ds(0, rt)], recv_sem.at[9 + t])

            prepare(la, t)
            right_tile(t)
            return 0

        lax.fori_loop(0, nt, second, 0)
        right_finish()

    with scope("numer2"):
        numer2 = [jnp.zeros((w, r), F32) for _ in range(per)]
        for h in range(per):
            kh = sright_v[pl.ds(h * (cols // per), cols // per)].reshape(w, r)
            high, low = split(kh)
            s3 = other_three(high, low, 1)
            for j in range(jl):
                rows_j = sleft_v[:, j, :]
                high, low = split(rows_j)
                product = mm(three(high, low, 1), s3, NT)
                i = j * per + h
                quotient = right_v[:, i * w:(i + 1) * w] * inverse(product)
                qh, ql = split(quotient.T)
                both = mm(qh, jnp.concatenate([high, low], axis=1))
                numer2[h] += both[:, :r] + both[:, r:] + mm(ql, high)
        for h in range(per):
            part = pl.ds(h * (d // per), d // per)
            sc[part, 0:own_k] = numer2[h].reshape(d // per, own_k, r)
        sc[:, own_k:own_k + 1, :] = jnp.broadcast_to(part2[None], (d, 1, r))
    with scope("rs2send"):
        to_all(lambda to, slot: remote(
            sc.at[to, pl.ds(0, own_k + 1)], rc.at[slot, pl.ds(0, own_k + 1)], 4, to).start())

    with scope("left2"):
        sb[:, 8:16, :] = jnp.broadcast_to(sums_v[...][None], (d, 8, r))

        def tile2(t, _):
            left_tile(t, sb)
            return 0

        lax.fori_loop(0, nt, tile2, 0)

    with scope("rs2wait"):
        wait(rc.at[:, pl.ds(0, own_k + 1)], recv_sem.at[4])
    with scope("rs2sum"):
        numer = sc[me] + jnp.sum(rc[...], axis=0)
        cb[...] = (sright_v[lax.div(me, d // cols), lax.rem(me, d // cols)]
                   * numer[:own_k] / numer[own_k:own_k + 1])
        sright_new[me] = cb[...]
    with scope("ag2send"):
        to_all(lambda to, slot: remote(cb, sright_new.at[me], 5, to).start())
    with scope("rs3send"):
        to_all(lambda to, slot: remote(
            sb.at[to, pl.ds(0, 9)], rb.at[slot, pl.ds(0, 9)], 6, to).start())
    with scope("ag2wait"):
        own = sb[me]
        old = la[pl.ds(me * mc, mc), :]
        wait(sright_new.at[pl.ds(0, d - 1)], recv_sem.at[5])
    with scope("left3"):
        fresh = sright_new[...].reshape(depth, r)
        inv_u = 1.0 / jnp.sum(fresh, axis=0, keepdims=True)
        for j in range(jl):
            rows_j = sleft_v[:, j, :]
            high, low = split(rows_j)
            lhs = three(high, low, 1)
            total = jnp.zeros((r, r), F32)
            for h in range(per):
                high, low = split(fresh[h * w:(h + 1) * w])
                product = mm(lhs, other_three(high, low, 1), NT)
                i = j * per + h
                quotient = right_v[:, i * w:(i + 1) * w] * inverse(product)
                qh, ql = split(quotient)
                both = mm(qh, jnp.concatenate([high, low], axis=1))
                total += both[:, :r] + both[:, r:] + mm(ql, high)
            outv[:, j, :] = rows_j * (total * inv_u)
    with scope("a2asend"):
        to_all(lambda to, slot: remote(outv.at[to], second_out.at[me], 7, to).start())
        own_out = pltpu.make_async_copy(outv.at[me], second_out.at[me], in_sem.at[1])
        own_out.start()
    with scope("rs3wait"):
        wait(rb.at[:, pl.ds(0, 9)], recv_sem.at[6])
    with scope("rs3sum"):
        numer = own[:mc] + jnp.sum(rb[:, 0:mc, :], axis=0)
        tail = own[8:9] + jnp.sum(rb[:, 8:9, :], axis=0)
        mult[...] = old * numer / tail
    with scope("ag3send"):
        to_all(lambda to, slot: remote(mult, left_out.at[pl.ds(me * mc, mc)], 8, to).start())
        own_left = pltpu.make_async_copy(mult, left_out.at[pl.ds(me * mc, mc)], in_sem.at[2])
        own_left.start()
    with scope("a2await"):
        own_out.wait()
        wait(second_out.at[pl.ds(0, d - 1)], recv_sem.at[7])
    with scope("ag3wait"):
        own_left.wait()
        wait(left_out.at[pl.ds(0, m - mc)], recv_sem.at[8])
    with scope("sendwait"):
        wait(sleft_v.at[pl.ds(0, r - rr)], send_sem.at[0])
        wait(sright_v.at[pl.ds(0, cols - 1)], send_sem.at[1])
        wait(ra.at[:, pl.ds(0, 9)], send_sem.at[2])
        wait(la.at[pl.ds(0, m - mc)], send_sem.at[3])
        wait(rc.at[:, pl.ds(0, own_k + 1)], send_sem.at[4])
        wait(sright_new.at[pl.ds(0, d - 1)], send_sem.at[5])
        wait(rb.at[:, pl.ds(0, 9)], send_sem.at[6])
        wait(second_out.at[pl.ds(0, d - 1)], send_sem.at[7])
        wait(left_out.at[pl.ds(0, m - mc)], send_sem.at[8])


def solution(mesh):
    rows, cols = mesh.shape["row"], mesh.shape["col"]
    d = rows * cols

    def body(slab, left, right, sleft, sright):
        m, width = slab.shape
        r = left.shape[1]
        depth = sright.shape[1] * cols
        jl = width // depth
        w = depth // 2
        nb = width // w
        mc = m // d
        rt = m // TILES
        own_k = depth // d
        sleft = sleft.reshape(r // rows, d, jl, r)
        sright = sright.T.reshape(d // cols, own_k, r)
        hbm = pl.BlockSpec(memory_space=pl.ANY)
        left_out, second = pl.pallas_call(
            functools.partial(kernel, (rows, cols, m, r, w, jl, depth)),
            out_shape=(jax.ShapeDtypeStruct((m, r), F32),
                       jax.ShapeDtypeStruct((d, jl, r), F32)),
            in_specs=[hbm] * 5,
            out_specs=(hbm, hbm),
            scratch_shapes=[
                pltpu.VMEM((m, width), F32),
                pltpu.VMEM((m, r), F32),
                pltpu.VMEM((r, width), F32),
                pltpu.VMEM((r, jl, r), F32),
                pltpu.VMEM((cols, d // cols, own_k, r), F32),
                pltpu.VMEM((TILES, rt, 3 * r), BF16),
                pltpu.VMEM((TILES, 2 * r, rt), BF16),
                pltpu.VMEM((nb, 2 * r, w), BF16),
                pltpu.VMEM((nb, r, w), F32),
                pltpu.VMEM((mc, r), F32),
                pltpu.VMEM((8, r), F32),
                pltpu.VMEM((r, 128), F32),
                pltpu.VMEM((d, 16, r), F32),
                pltpu.VMEM((d - 1, 16, r), F32),
                pltpu.VMEM((m, r), F32),
                pltpu.VMEM((d, 8, r), F32),
                pltpu.VMEM((d - 1, 8, r), F32),
                pltpu.VMEM((mc, r), F32),
                pltpu.VMEM((d, 16, r), F32),
                pltpu.VMEM((d - 1, 16, r), F32),
                pltpu.VMEM((d, own_k, r), F32),
                pltpu.VMEM((own_k, r), F32),
                pltpu.VMEM((d, jl, r), F32),
                pltpu.VMEM((8, r), F32),
                pltpu.SemaphoreType.DMA((TILES,)),
                pltpu.SemaphoreType.DMA((4,)),
                pltpu.SemaphoreType.DMA((9,)),
                pltpu.SemaphoreType.DMA((9 + TILES,)),
            ],
            compiler_params=pltpu.CompilerParams(
                collective_id=0, has_side_effects=True, vmem_limit_bytes=60 * 1024 * 1024),
        )(slab, left, right, sleft, sright)
        return left_out, second.reshape(d * jl, r)

    placed = (P(None, ("row", "col")), P(), P(None, ("row", "col")), P("row", None), P(None, "col"))
    return jax.shard_map(
        body, mesh=mesh, in_specs=placed, out_specs=(P(), P(("row", "col"), None)), check_vma=False
    )
```

```python
import contextlib
import functools

import jax
import jax.numpy as jnp
from jax import lax
from jax.experimental import pallas as pl
from jax.experimental.pallas import tpu as pltpu
from jax.sharding import PartitionSpec as P

F32 = jnp.float32
BF16 = jnp.bfloat16
NN = (((1,), (0,)), ((), ()))
NT = (((1,), (1,)), ((), ()))
TILES = 4
AHEAD = 1
SENDS = 8


def scope(_):
    return contextlib.nullcontext()


def mm(a, b, dims=NN):
    return lax.dot_general(a, b, dims, preferred_element_type=F32)


def split(x):
    high = x.astype(BF16)
    low = (x - high.astype(F32)).astype(BF16)
    return high, low


def inverse(x):
    guess = pl.reciprocal(x, approx=True)
    return guess * (2.0 - x * guess)


def three(high, low, axis):
    return jnp.concatenate([high, high, low], axis=axis)


def other_three(high, low, axis):
    return jnp.concatenate([high, low, high], axis=axis)


def kernel(sizes, slab, left, right, sleft, sright, left_out, second_out, *scratch):
    (rows, cols, m, r, w, jl, depth) = sizes
    (slab_v, left_v, right_v, right_t, sleft_v, sright_v, c2_v, left3, left_t, rcat3, rcat_t,
     nacc, csum, la, lc, mult, last, sc, rc, sright_new, cb, outv, keep,
     sl3, slpair, slt3, srt3, slf, ub, ur, sa, pr, sm, ra,
     slab_sem, in_sem, send_sem, recv_sem) = scratch
    d = rows * cols
    nt = TILES
    rt = m // nt
    nb = rcat3.shape[0]
    mc = m // d
    dt = d // nt
    xh = dt // (2 * cols)
    own_k = depth // d
    per = depth // w
    rr = r // rows
    half = d // 2
    my_row, my_col = lax.axis_index("row"), lax.axis_index("col")
    me = my_row * cols + my_col
    my_z = lax.div(me, dt)
    core = lax.rem(my_row, 2)
    my_x = lax.rem(lax.div(my_row, 2), xh)
    partner = me + cols * (1 - 2 * core)
    PAIR, GATHER, FORWARD, LAST, LASTF = 9, 9 + 2 * nt, 9 + 3 * nt, 9 + 4 * nt, 9 + 5 * nt

    def wait(ref, sem):
        pltpu.make_async_copy(ref, ref, sem).wait()

    def remote(src, dst, phase, to, recv=None):
        return pltpu.make_async_remote_copy(
            src, dst, send_sem.at[phase], recv_sem.at[phase if recv is None else recv],
            device_id=to, device_id_type=pl.DeviceIdType.LOGICAL)

    def near_first(q):
        return lax.rem(my_z + lax.div(q * (q + 1), 2), nt)

    def loop(n, body, start=0, unroll=1):
        def step(k, _):
            body(k)
            return 0

        lax.fori_loop(start, n, step, 0, unroll=unroll)

    def to_all(start):
        def one(k):
            t = me + k
            start(jnp.where(t >= d, t - d, t), k - 1)

        loop(d, one, 1, SENDS)

    def to_plane(z, start):
        oz = z - my_z
        oz = jnp.where(oz < 0, oz + nt, oz)
        for ox in range(xh):
            x = my_x + ox
            x = jnp.where(x >= xh, x - xh, x)
            base = z * dt + (x * 2 + core) * cols
            first = oz * (xh * cols) + ox * cols - 1

            def one(k, base=base, first=first):
                c = my_col + k
                start(base + jnp.where(c >= cols, c - cols, c), first + k)

            if ox == 0:
                @pl.when(oz != 0)
                def _():
                    one(0)
                loop(cols, one, 1, cols - 1)
            else:
                loop(cols, one, 0, cols)

    with scope("start"):
        left_in = pltpu.make_async_copy(left, left_v, in_sem.at[0])
        left_in.start()
        right_in = pltpu.make_async_copy(right, right_v, in_sem.at[3])
        right_in.start()
        for t in range(nt):
            part = pl.ds(t * rt, rt)
            pltpu.make_async_copy(slab.at[part], slab_v.at[part], slab_sem.at[t]).start()
        barrier = pltpu.get_barrier_semaphore()

        def greet(k):
            t = me + k
            pl.semaphore_signal(barrier, inc=1, device_id=jnp.where(t >= d, t - d, t),
                                device_id_type=pl.DeviceIdType.LOGICAL)

        loop(d, greet, 1, SENDS)
        own_sleft = pltpu.make_async_copy(
            sleft.at[:, me], sleft_v.at[pl.ds(my_row * rr, rr)], in_sem.at[1])
        own_sleft.start()
        own_sright = pltpu.make_async_copy(sright, sright_v.at[my_col], in_sem.at[2])
        own_sright.start()
        c2_in = pltpu.make_async_copy(sleft.at[my_col], c2_v, in_sem.at[4])
        c2_in.start()

    def prepare(source, t):
        value = source[pl.ds(t * rt, rt), :]
        high, low = split(value)
        left3[t] = three(high, low, 1)
        turned = value.T
        high, low = split(turned)
        left_t[t] = jnp.concatenate([high, low], axis=0)
        csum[...] += jnp.broadcast_to(jnp.sum(turned, axis=1, keepdims=True), csum.shape)

    def right_tile(t):
        part = pl.ds(t * rt, rt)
        lhs = left3[t]
        turned = left_t[t]
        ahead = [mm(lhs, rcat3[i]) for i in range(AHEAD)]
        for i in range(nb):
            if i + AHEAD < nb:
                ahead.append(mm(lhs, rcat3[i + AHEAD]))
            quotient = slab_v[part, i * w:(i + 1) * w] * inverse(ahead[i])
            high, low = split(quotient)
            both = mm(turned, high)
            nacc[i] += both[:r] + both[r:] + mm(turned[:r], low)

    def right_finish():
        inv_c = 1.0 / csum[:, 0:1]
        sums = jnp.zeros((1, r), F32)
        for i in range(nb):
            cut = slice(i * w, (i + 1) * w)
            new = right_v[:, cut] * (nacc[i] * inv_c)
            right_v[:, cut] = new
            high, low = split(new)
            rcat3[i] = other_three(high, low, 0)
            turned = new.T
            right_t[i] = turned
            high, low = split(turned)
            rcat_t[i] = jnp.concatenate([high, low], axis=1)
            sums += jnp.sum(turned, axis=0, keepdims=True)
        return sums

    def left_tile(t, buffer):
        part = pl.ds(t * rt, rt)
        total = jnp.zeros((rt, r), F32)
        lhs = left3[t]
        ahead = [mm(lhs, rcat3[i]) for i in range(AHEAD)]
        for i in range(nb):
            if i + AHEAD < nb:
                ahead.append(mm(lhs, rcat3[i + AHEAD]))
            quotient = slab_v[part, i * w:(i + 1) * w] * inverse(ahead[i])
            qh, ql = split(quotient)
            both = mm(qh, rcat_t[i])
            total += both[:, :r] + both[:, r:] + mm(ql, rcat_t[i, :, :r])
        buffer[pl.ds(t * dt, dt)] = total.reshape(dt, mc, r)

    def reset():
        nacc[...] = jnp.zeros_like(nacc)
        csum[...] = jnp.zeros_like(csum)

    def group(z, x, c):
        return z * dt + (x * 2 + c) * cols

    def left_sums(turn, phase):
        mine, theirs, message, arrived = sa.at[turn], pr.at[turn], sm.at[turn], ra.at[turn]
        remote(ub.at[turn], ur.at[turn], PAIR + turn, partner, 9 + 6 * nt + turn).start()

        def combine(q):
            t = near_first(nt - 1 - q)
            wait(theirs.at[pl.ds(0, xh * cols)], recv_sem.at[PAIR + turn * nt + q])
            for x in range(xh):
                part = pl.ds(group(t, x, core), cols)
                message[part, 0:mc, :] = mine[part] + theirs[part]
            to_plane(t, lambda to, slot: remote(
                message.at[to, pl.ds(0, 10)], arrived.at[slot, pl.ds(0, 10)], phase, to).start())

        def tile(q):
            t = near_first(nt - 1 - q)
            left_tile(t, mine)
            for x in range(xh):
                part = pl.ds(group(t, x, 1 - core), cols)
                remote(mine.at[part], theirs.at[part], PAIR + turn, partner, PAIR + turn * nt + q).start()

            @pl.when(q == 0)
            def _():
                wait(ur.at[turn], recv_sem.at[9 + 6 * nt + turn])
                message[:, 8:16, :] = jnp.broadcast_to((ub[turn] + ur[turn])[None], (d, 8, r))

            @pl.when(q > 0)
            def _():
                combine(q - 1)

        loop(nt, tile)
        combine(nt - 1)

    def owned(turn, phase, old):
        wait(ra.at[turn, :, pl.ds(0, 10)], recv_sem.at[phase])
        own = sm[turn, me]
        numer = own[:mc] + jnp.sum(ra[turn, :, 0:mc, :], axis=0)
        tail = own[8:10] + jnp.sum(ra[turn, :, 8:10, :], axis=0)
        return old * numer / tail[0:1], tail[1:2]

    with scope("prep"):
        reset()
        right_in.wait()
        for i in range(nb):
            high, low = split(right_v[:, i * w:(i + 1) * w])
            rcat3[i] = other_three(high, low, 0)
        left_in.wait()

    line = lax.broadcasted_iota(jnp.int32, (8, r), 0)
    with scope("right1"):
        def first(t):
            prepare(left_v, t)
            wait(slab_v.at[pl.ds(0, rt)], slab_sem.at[t])
            right_tile(t)

        loop(nt, first)
        sums = right_finish()
        c2_in.wait()
        part2 = jnp.sum(jnp.sum(c2_v[...], axis=0), axis=0, keepdims=True)
        ub[0] = jnp.where(line == 0, sums, part2)

    with scope("barrier"):
        pl.semaphore_wait(barrier, d - 1)

    with scope("sendin"):
        def send_sleft(k):
            t = lax.rem(my_row + k, rows) * cols + my_col
            remote(sleft.at[:, t], sleft_v.at[pl.ds(my_row * rr, rr)], 0, t).start()

        def send_sright(k):
            t = my_row * cols + lax.rem(my_col + k, cols)
            remote(sright, sright_v.at[my_col], 1, t).start()

    with scope("left1"):
        left_sums(0, 2)

    with scope("sendin"):
        loop(rows, send_sleft, 1)
        loop(cols, send_sright, 1)
        reset()

    with scope("rs1wait"):
        new, total2 = owned(0, 2, left_v[pl.ds(me * mc, mc), :])
        keep[...] = jnp.broadcast_to(total2, (8, r))
        lc[...] = new
        la[pl.ds(me * mc, mc), :] = new
    with scope("ag1send"):
        def ag1(q):
            to_plane(near_first(q), lambda to, slot: remote(
                lc, la.at[pl.ds(me * mc, mc)], 3, to, GATHER + my_z).start())

        loop(nt, ag1)

    def blocks(q):
        t = near_first(q)
        return t, [pl.ds(group(t, x, core) * mc, cols * mc) for x in range(xh)]

    with scope("slprep"):
        own_sleft.wait()
        wait(sleft_v.at[pl.ds(0, r - rr)], recv_sem.at[0])
        own_sright.wait()
        wait(sright_v.at[pl.ds(0, cols - 1)], recv_sem.at[1])
        for g in range(jl // 2):
            two = jnp.concatenate([sleft_v[:, 2 * g, :], sleft_v[:, 2 * g + 1, :]], axis=0)
            slf[g] = two
            high, low = split(two)
            sl3[g] = three(high, low, 1)
            slpair[g] = jnp.concatenate([high, low], axis=1)
            high, low = split(two.T)
            slt3[g] = other_three(high, low, 0)
        for h in range(per):
            high, low = split(sright_v[pl.ds(h * (cols // per), cols // per)].reshape(w, r))
            srt3[h] = three(high, low, 1)

    with scope("right2"):
        def forward(q):
            t, parts = blocks(q)

            @pl.when(q == 0)
            def _():
                wait(la.at[pl.ds(0, (xh * cols - 1) * mc)], recv_sem.at[GATHER + t])

            @pl.when(q != 0)
            def _():
                wait(la.at[pl.ds(0, xh * cols * mc)], recv_sem.at[GATHER + t])

            for part in parts:
                remote(la.at[part], la.at[part], GATHER, partner, FORWARD + q).start()

        forward(0)

        def second(q):
            t = near_first(q)
            wait(la.at[pl.ds(0, xh * cols * mc)], recv_sem.at[FORWARD + q])

            @pl.when(q < nt - 1)
            def _():
                forward(q + 1)

            prepare(la, t)
            right_tile(t)

        loop(nt, second)
        sums = right_finish()
        ub[1] = jnp.broadcast_to(sums, (8, r))

    with scope("numer2"):
        for h in range(per):
            total = jnp.zeros((w, r), F32)
            for g in range(jl // 2):
                product = mm(srt3[h], slt3[g])
                value = jnp.concatenate(
                    [right_t[2 * g * per + h], right_t[(2 * g + 1) * per + h]], axis=1)
                qh, ql = split(value * inverse(product))
                both = mm(qh, slpair[g])
                total += both[:, :r] + both[:, r:] + mm(ql, slpair[g, :, :r])
            sc[pl.ds(h * (d // per), d // per)] = total.reshape(d // per, own_k, r)
    with scope("rs2send"):
        to_all(lambda to, slot: remote(sc.at[to], rc.at[slot], 4, to).start())

    with scope("left2"):
        left_sums(1, 6)

    with scope("rs2wait"):
        wait(rc, recv_sem.at[4])
    with scope("rs2sum"):
        numer = sc[me] + jnp.sum(rc[...], axis=0)
        cb[...] = (sright_v[lax.div(me, d // cols), lax.rem(me, d // cols)]
                   * numer / keep[0:1])
        sright_new[me] = cb[...]
    with scope("ag2send"):
        to_all(lambda to, slot: remote(cb, sright_new.at[me], 5, to).start())
    with scope("rs3wait"):
        new, _ = owned(1, 6, la[pl.ds(me * mc, mc), :])
        mult[...] = new
        last[pl.ds(me * mc, mc), :] = new
    with scope("ag3send"):
        def ag3(q):
            to_plane(near_first(q), lambda to, slot: remote(
                mult, last.at[pl.ds(me * mc, mc)], 8, to, LAST + my_z).start())

        loop(nt, ag3)
    with scope("ag2wait"):
        wait(sright_new.at[pl.ds(0, d - 1)], recv_sem.at[5])
    with scope("left3"):
        fresh = sright_new[...].reshape(depth, r)
        inv_u = 1.0 / jnp.sum(fresh, axis=0, keepdims=True)
        threes, pairs = [], []
        for h in range(per):
            part = fresh[h * w:(h + 1) * w]
            high, low = split(part)
            pairs.append(jnp.concatenate([high, low], axis=1))
            high, low = split(part.T)
            threes.append(other_three(high, low, 0))
        for g in range(jl // 2):
            total = jnp.zeros((2 * r, r), F32)
            for h in range(per):
                product = mm(sl3[g], threes[h])
                i, k = 2 * g * per + h, (2 * g + 1) * per + h
                value = jnp.concatenate(
                    [right_v[:, i * w:(i + 1) * w], right_v[:, k * w:(k + 1) * w]], axis=0)
                qh, ql = split(value * inverse(product))
                both = mm(qh, pairs[h])
                total += both[:, :r] + both[:, r:] + mm(ql, pairs[h][:, :r])
            result = slf[g] * (total * inv_u)
            outv[:, 2 * g, :] = result[:r]
            outv[:, 2 * g + 1, :] = result[r:]
    with scope("a2asend"):
        to_all(lambda to, slot: remote(outv.at[to], second_out.at[me], 7, to).start())
        own_out = pltpu.make_async_copy(outv.at[me], second_out.at[me], in_sem.at[1])
        own_out.start()
    with scope("ag3wait"):
        def finish(q):
            t, parts = blocks(q)

            @pl.when(q == 0)
            def _():
                wait(last.at[pl.ds(0, (xh * cols - 1) * mc)], recv_sem.at[LAST + t])

            @pl.when(q != 0)
            def _():
                wait(last.at[pl.ds(0, xh * cols * mc)], recv_sem.at[LAST + t])

            for part in parts:
                remote(last.at[part], left_out.at[part], LAST, partner, LASTF).start()
                pltpu.make_async_copy(last.at[part], left_out.at[part], in_sem.at[2]).start()

        loop(nt, finish)
    with scope("a2await"):
        own_out.wait()
        wait(second_out.at[pl.ds(0, d - 1)], recv_sem.at[7])
    with scope("ag3end"):
        wait(left_out.at[pl.ds(0, m // 2)], in_sem.at[2])
        wait(left_out.at[pl.ds(0, m // 2)], recv_sem.at[LASTF])
    with scope("sendwait"):
        wait(sleft_v.at[pl.ds(0, r - rr)], send_sem.at[0])
        wait(sright_v.at[pl.ds(0, cols - 1)], send_sem.at[1])
        wait(sc.at[pl.ds(0, d - 1)], send_sem.at[4])
        wait(sright_new.at[pl.ds(0, d - 1)], send_sem.at[5])
        wait(second_out.at[pl.ds(0, d - 1)], send_sem.at[7])
        for turn, phase in ((0, 2), (1, 6)):
            wait(ra.at[turn, :, pl.ds(0, 10)], send_sem.at[phase])
            wait(ur.at[turn], send_sem.at[PAIR + turn])
            wait(pr.at[turn, pl.ds(0, half)], send_sem.at[PAIR + turn])
        wait(la.at[pl.ds(0, (half - 1) * mc)], send_sem.at[3])
        wait(la.at[pl.ds(0, half * mc)], send_sem.at[GATHER])
        wait(last.at[pl.ds(0, (half - 1) * mc)], send_sem.at[8])
        wait(last.at[pl.ds(0, half * mc)], send_sem.at[LAST])


def solution(mesh):
    rows, cols = mesh.shape["row"], mesh.shape["col"]
    d = rows * cols

    def body(slab, left, right, sleft, sright):
        m, width = slab.shape
        r = left.shape[1]
        depth = sright.shape[1] * cols
        jl = width // depth
        w = depth // 2
        nb = width // w
        mc = m // d
        rt = m // TILES
        own_k = depth // d
        sleft = sleft.reshape(r // rows, d, jl, r)
        sright = sright.T.reshape(d // cols, own_k, r)
        hbm = pl.BlockSpec(memory_space=pl.ANY)
        left_out, second = pl.pallas_call(
            functools.partial(kernel, (rows, cols, m, r, w, jl, depth)),
            out_shape=(jax.ShapeDtypeStruct((m, r), F32),
                       jax.ShapeDtypeStruct((d, jl, r), F32)),
            in_specs=[hbm] * 5,
            out_specs=(hbm, hbm),
            scratch_shapes=[
                pltpu.VMEM((m, width), F32),
                pltpu.VMEM((m, r), F32),
                pltpu.VMEM((r, width), F32),
                pltpu.VMEM((nb, w, r), F32),
                pltpu.VMEM((r, jl, r), F32),
                pltpu.VMEM((cols, d // cols, own_k, r), F32),
                pltpu.VMEM((d, jl, r), F32),
                pltpu.VMEM((TILES, rt, 3 * r), BF16),
                pltpu.VMEM((TILES, 2 * r, rt), BF16),
                pltpu.VMEM((nb, 3 * r, w), BF16),
                pltpu.VMEM((nb, w, 2 * r), BF16),
                pltpu.VMEM((nb, r, w), F32),
                pltpu.VMEM((r, 128), F32),
                pltpu.VMEM((m, r), F32),
                pltpu.VMEM((mc, r), F32),
                pltpu.VMEM((mc, r), F32),
                pltpu.VMEM((m, r), F32),
                pltpu.VMEM((d, own_k, r), F32),
                pltpu.VMEM((d - 1, own_k, r), F32),
                pltpu.VMEM((d, own_k, r), F32),
                pltpu.VMEM((own_k, r), F32),
                pltpu.VMEM((d, jl, r), F32),
                pltpu.VMEM((8, r), F32),
                pltpu.VMEM((jl // 2, 2 * r, 3 * r), BF16),
                pltpu.VMEM((jl // 2, 2 * r, 2 * r), BF16),
                pltpu.VMEM((jl // 2, 3 * r, 2 * r), BF16),
                pltpu.VMEM((2, w, 3 * r), BF16),
                pltpu.VMEM((jl // 2, 2 * r, r), F32),
                pltpu.VMEM((2, 8, r), F32),
                pltpu.VMEM((2, 8, r), F32),
                pltpu.VMEM((2, d, mc, r), F32),
                pltpu.VMEM((2, d, mc, r), F32),
                pltpu.VMEM((2, d, 16, r), F32),
                pltpu.VMEM((2, d // 2 - 1, 16, r), F32),
                pltpu.SemaphoreType.DMA((TILES,)),
                pltpu.SemaphoreType.DMA((5,)),
                pltpu.SemaphoreType.DMA((9 + 6 * TILES,)),
                pltpu.SemaphoreType.DMA((9 + 6 * TILES + 2,)),
            ],
            compiler_params=pltpu.CompilerParams(
                collective_id=0, has_side_effects=True, vmem_limit_bytes=60 * 1024 * 1024),
        )(slab, left, right, sleft, sright)
        return left_out, second.reshape(d * jl, r)

    placed = (P(None, ("row", "col")), P(), P(None, ("row", "col")), P("row", None), P(None, "col"))
    return jax.shard_map(
        body, mesh=mesh, in_specs=placed, out_specs=(P(), P(("row", "col"), None)), check_vma=False
    )
```

```python
import contextlib
import functools

import jax
import jax.numpy as jnp
from jax import lax
from jax.experimental import pallas as pl
from jax.experimental.pallas import tpu as pltpu
from jax.sharding import PartitionSpec as P

F32 = jnp.float32
BF16 = jnp.bfloat16
NN = (((1,), (0,)), ((), ()))
NT = (((1,), (1,)), ((), ()))
TILES = 4
AHEAD = 1
SENDS = 8


def scope(_):
    return contextlib.nullcontext()


def mm(a, b, dims=NN):
    return lax.dot_general(a, b, dims, preferred_element_type=F32)


def split(x):
    high = x.astype(BF16)
    low = (x - high.astype(F32)).astype(BF16)
    return high, low


def inverse(x):
    guess = pl.reciprocal(x, approx=True)
    return guess * (2.0 - x * guess)


def three(high, low, axis):
    return jnp.concatenate([high, high, low], axis=axis)


def other_three(high, low, axis):
    return jnp.concatenate([high, low, high], axis=axis)


def kernel(sizes, slab, left, right, sleft, sright, left_out, second_out, *scratch):
    (rows, cols, m, r, w, jl, depth) = sizes
    (slab_v, left_v, right_v, right_t, sleft_v, sright_v, c2_v, noise, left2, left_t, rd, rdt,
     nacc, csum, la, lc, mult, last, sc, rc, sright_new, cb, outv, keep,
     sl3, slpair, slt3, srt3, slf, ub, ur, sa, pr, sm, ra,
     slab_sem, in_sem, send_sem, recv_sem) = scratch
    d = rows * cols
    nt = TILES
    rt = m // nt
    nb = rd.shape[0]
    mc = m // d
    dt = d // nt
    xh = dt // (2 * cols)
    own_k = depth // d
    per = depth // w
    rr = r // rows
    half = d // 2
    my_row, my_col = lax.axis_index("row"), lax.axis_index("col")
    me = my_row * cols + my_col
    my_z = lax.div(me, dt)
    core = lax.rem(my_row, 2)
    my_x = lax.rem(lax.div(my_row, 2), xh)
    partner = me + cols * (1 - 2 * core)
    PAIR, GATHER, FORWARD, LAST, LASTF = 9, 9 + 2 * nt, 9 + 3 * nt, 9 + 4 * nt, 9 + 5 * nt

    def wait(ref, sem):
        pltpu.make_async_copy(ref, ref, sem).wait()

    def remote(src, dst, phase, to, recv=None):
        return pltpu.make_async_remote_copy(
            src, dst, send_sem.at[phase], recv_sem.at[phase if recv is None else recv],
            device_id=to, device_id_type=pl.DeviceIdType.LOGICAL)

    def near_first(q):
        return lax.rem(my_z + lax.div(q * (q + 1), 2), nt)

    def loop(n, body, start=0, unroll=1):
        def step(k, _):
            body(k)
            return 0

        lax.fori_loop(start, n, step, 0, unroll=unroll)

    def to_all(start):
        def one(k):
            t = me + k
            start(jnp.where(t >= d, t - d, t), k - 1)

        loop(d, one, 1, SENDS)

    def to_plane(z, start):
        oz = z - my_z
        oz = jnp.where(oz < 0, oz + nt, oz)
        for ox in range(xh):
            x = my_x + ox
            x = jnp.where(x >= xh, x - xh, x)
            base = z * dt + (x * 2 + core) * cols
            first = oz * (xh * cols) + ox * cols - 1

            def one(k, base=base, first=first):
                c = my_col + k
                start(base + jnp.where(c >= cols, c - cols, c), first + k)

            if ox == 0:
                @pl.when(oz != 0)
                def _():
                    one(0)
                loop(cols, one, 1, cols - 1)
            else:
                loop(cols, one, 0, cols)

    with scope("start"):
        left_in = pltpu.make_async_copy(left, left_v, in_sem.at[0])
        left_in.start()
        right_in = pltpu.make_async_copy(right, right_v, in_sem.at[3])
        right_in.start()
        for t in range(nt):
            part = pl.ds(t * rt, rt)
            pltpu.make_async_copy(slab.at[part], slab_v.at[part], slab_sem.at[t]).start()
        barrier = pltpu.get_barrier_semaphore()

        def greet(k):
            t = me + k
            pl.semaphore_signal(barrier, inc=1, device_id=jnp.where(t >= d, t - d, t),
                                device_id_type=pl.DeviceIdType.LOGICAL)

        loop(d, greet, 1, SENDS)
        own_sleft = pltpu.make_async_copy(
            sleft.at[:, me], sleft_v.at[pl.ds(my_row * rr, rr)], in_sem.at[1])
        own_sleft.start()
        own_sright = pltpu.make_async_copy(sright, sright_v.at[my_col], in_sem.at[2])
        own_sright.start()
        c2_in = pltpu.make_async_copy(sleft.at[my_col], c2_v, in_sem.at[4])
        c2_in.start()

    def prepare(source, t):
        value = source[pl.ds(t * rt, rt), :]
        high, low = split(value)
        left2[t] = jnp.concatenate([high, low], axis=1)
        turned = value.T
        high, low = split(turned)
        left_t[t] = jnp.concatenate([high, low], axis=0)
        csum[...] += jnp.broadcast_to(jnp.sum(turned, axis=1, keepdims=True), csum.shape)

    def product(lhs, i):
        return mm(lhs, jnp.concatenate([rd[i], rd[i]], axis=0))

    def quotients(t, fresh):
        part = pl.ds(t * rt, rt)
        lhs = left2[t]
        ahead = [product(lhs, i) for i in range(AHEAD)]
        for i in range(nb):
            if i + AHEAD < nb:
                ahead.append(product(lhs, i + AHEAD))
            cut = slice(i * w, (i + 1) * w)
            top = slab_v[part, cut]
            if fresh:
                top = top * noise[...]
                slab_v[part, cut] = top
            yield i, (top * inverse(ahead[i])).astype(BF16)

    def right_tile(t, fresh):
        turned = left_t[t]
        for i, quotient in quotients(t, fresh):
            both = mm(turned, quotient)
            nacc[i] += both[:r] + both[r:]

    def right_finish():
        inv_c = 1.0 / csum[:, 0:1]
        sums = jnp.zeros((1, r), F32)
        for i in range(nb):
            cut = slice(i * w, (i + 1) * w)
            new = right_v[:, cut] * (nacc[i] * inv_c)
            right_v[:, cut] = new
            rd[i] = (new * noise[:r, :]).astype(BF16)
            turned = new.T
            right_t[i] = turned
            rdt[i] = (turned * noise[:, :r]).astype(BF16)
            sums += jnp.sum(turned, axis=0, keepdims=True)
        return sums

    def left_tile(t, buffer):
        total = jnp.zeros((rt, r), F32)
        for i, quotient in quotients(t, False):
            total += mm(quotient, rdt[i])
        buffer[pl.ds(t * dt, dt)] = total.reshape(dt, mc, r)

    def reset():
        nacc[...] = jnp.zeros_like(nacc)
        csum[...] = jnp.zeros_like(csum)

    def group(z, x, c):
        return z * dt + (x * 2 + c) * cols

    def left_sums(turn, phase):
        mine, theirs, message, arrived = sa.at[turn], pr.at[turn], sm.at[turn], ra.at[turn]
        remote(ub.at[turn], ur.at[turn], PAIR + turn, partner, 9 + 6 * nt + turn).start()

        def combine(q):
            t = near_first(nt - 1 - q)
            wait(theirs.at[pl.ds(0, xh * cols)], recv_sem.at[PAIR + turn * nt + q])
            for x in range(xh):
                part = pl.ds(group(t, x, core), cols)
                message[part, 0:mc, :] = mine[part] + theirs[part]
            to_plane(t, lambda to, slot: remote(
                message.at[to, pl.ds(0, 10)], arrived.at[slot, pl.ds(0, 10)], phase, to).start())

        def tile(q):
            t = near_first(nt - 1 - q)
            left_tile(t, mine)
            for x in range(xh):
                part = pl.ds(group(t, x, 1 - core), cols)
                remote(mine.at[part], theirs.at[part], PAIR + turn, partner, PAIR + turn * nt + q).start()

            @pl.when(q == 0)
            def _():
                wait(ur.at[turn], recv_sem.at[9 + 6 * nt + turn])
                message[:, 8:16, :] = jnp.broadcast_to((ub[turn] + ur[turn])[None], (d, 8, r))

            @pl.when(q > 0)
            def _():
                combine(q - 1)

        loop(nt, tile)
        combine(nt - 1)

    def owned(turn, phase, old):
        wait(ra.at[turn, :, pl.ds(0, 10)], recv_sem.at[phase])
        own = sm[turn, me]
        numer = own[:mc] + jnp.sum(ra[turn, :, 0:mc, :], axis=0)
        tail = own[8:10] + jnp.sum(ra[turn, :, 8:10, :], axis=0)
        return old * numer / tail[0:1], tail[1:2]

    with scope("prep"):
        reset()
        down = lax.broadcasted_iota(jnp.int32, (rt, w), 0).astype(F32)
        across = lax.broadcasted_iota(jnp.int32, (rt, w), 1).astype(F32)
        one = down * 0.7548776662 + across * 0.5698402910
        two = down * 0.6710436067 + across * 0.8191725134
        noise[...] = 1.0 + ((one - jnp.floor(one)) + (two - jnp.floor(two)) - 1.0) * (1.0 / 128)
        right_in.wait()
        for i in range(nb):
            rd[i] = (right_v[:, i * w:(i + 1) * w] * noise[:r, :]).astype(BF16)
        left_in.wait()

    line = lax.broadcasted_iota(jnp.int32, (8, r), 0)
    with scope("right1"):
        def first(t):
            prepare(left_v, t)
            wait(slab_v.at[pl.ds(0, rt)], slab_sem.at[t])
            right_tile(t, True)

        loop(nt, first)
        sums = right_finish()
        c2_in.wait()
        part2 = jnp.sum(jnp.sum(c2_v[...], axis=0), axis=0, keepdims=True)
        ub[0] = jnp.where(line == 0, sums, part2)

    with scope("barrier"):
        pl.semaphore_wait(barrier, d - 1)

    with scope("sendin"):
        def send_sleft(k):
            t = lax.rem(my_row + k, rows) * cols + my_col
            remote(sleft.at[:, t], sleft_v.at[pl.ds(my_row * rr, rr)], 0, t).start()

        def send_sright(k):
            t = my_row * cols + lax.rem(my_col + k, cols)
            remote(sright, sright_v.at[my_col], 1, t).start()

    with scope("left1"):
        left_sums(0, 2)

    with scope("sendin"):
        loop(rows, send_sleft, 1)
        loop(cols, send_sright, 1)
        reset()

    with scope("rs1wait"):
        new, total2 = owned(0, 2, left_v[pl.ds(me * mc, mc), :])
        keep[...] = jnp.broadcast_to(total2, (8, r))
        lc[...] = new
        la[pl.ds(me * mc, mc), :] = new
    with scope("ag1send"):
        def ag1(q):
            to_plane(near_first(q), lambda to, slot: remote(
                lc, la.at[pl.ds(me * mc, mc)], 3, to, GATHER + my_z).start())

        loop(nt, ag1)

    def blocks(q):
        t = near_first(q)
        return t, [pl.ds(group(t, x, core) * mc, cols * mc) for x in range(xh)]

    with scope("slprep"):
        own_sleft.wait()
        wait(sleft_v.at[pl.ds(0, r - rr)], recv_sem.at[0])
        own_sright.wait()
        wait(sright_v.at[pl.ds(0, cols - 1)], recv_sem.at[1])
        for g in range(jl // 2):
            two = jnp.concatenate([sleft_v[:, 2 * g, :], sleft_v[:, 2 * g + 1, :]], axis=0)
            slf[g] = two
            high, low = split(two)
            sl3[g] = three(high, low, 1)
            slpair[g] = jnp.concatenate([high, low], axis=1)
            high, low = split(two.T)
            slt3[g] = other_three(high, low, 0)
        for h in range(per):
            high, low = split(sright_v[pl.ds(h * (cols // per), cols // per)].reshape(w, r))
            srt3[h] = three(high, low, 1)

    with scope("right2"):
        def forward(q):
            t, parts = blocks(q)

            @pl.when(q == 0)
            def _():
                wait(la.at[pl.ds(0, (xh * cols - 1) * mc)], recv_sem.at[GATHER + t])

            @pl.when(q != 0)
            def _():
                wait(la.at[pl.ds(0, xh * cols * mc)], recv_sem.at[GATHER + t])

            for part in parts:
                remote(la.at[part], la.at[part], GATHER, partner, FORWARD + q).start()

        forward(0)

        def second(q):
            t = near_first(q)
            wait(la.at[pl.ds(0, xh * cols * mc)], recv_sem.at[FORWARD + q])

            @pl.when(q < nt - 1)
            def _():
                forward(q + 1)

            prepare(la, t)
            right_tile(t, False)

        loop(nt, second)
        sums = right_finish()
        ub[1] = jnp.broadcast_to(sums, (8, r))

    with scope("numer2"):
        for h in range(per):
            total = jnp.zeros((w, r), F32)
            for g in range(jl // 2):
                joint = mm(srt3[h], slt3[g])
                value = jnp.concatenate(
                    [right_t[2 * g * per + h], right_t[(2 * g + 1) * per + h]], axis=1)
                qh, ql = split(value * inverse(joint))
                both = mm(qh, slpair[g])
                total += both[:, :r] + both[:, r:] + mm(ql, slpair[g, :, :r])
            sc[pl.ds(h * (d // per), d // per)] = total.reshape(d // per, own_k, r)
    with scope("rs2send"):
        to_all(lambda to, slot: remote(sc.at[to], rc.at[slot], 4, to).start())

    with scope("left2"):
        left_sums(1, 6)

    with scope("rs2wait"):
        wait(rc, recv_sem.at[4])
    with scope("rs2sum"):
        numer = sc[me] + jnp.sum(rc[...], axis=0)
        cb[...] = (sright_v[lax.div(me, d // cols), lax.rem(me, d // cols)]
                   * numer / keep[0:1])
        sright_new[me] = cb[...]
    with scope("ag2send"):
        to_all(lambda to, slot: remote(cb, sright_new.at[me], 5, to).start())
    with scope("rs3wait"):
        new, _ = owned(1, 6, la[pl.ds(me * mc, mc), :])
        mult[...] = new
        last[pl.ds(me * mc, mc), :] = new
    with scope("ag3send"):
        def ag3(q):
            to_plane(near_first(q), lambda to, slot: remote(
                mult, last.at[pl.ds(me * mc, mc)], 8, to, LAST + my_z).start())

        loop(nt, ag3)
    with scope("ag2wait"):
        wait(sright_new.at[pl.ds(0, d - 1)], recv_sem.at[5])
    with scope("left3"):
        fresh = sright_new[...].reshape(depth, r)
        inv_u = 1.0 / jnp.sum(fresh, axis=0, keepdims=True)
        threes, pairs = [], []
        for h in range(per):
            part = fresh[h * w:(h + 1) * w]
            high, low = split(part)
            pairs.append(jnp.concatenate([high, low], axis=1))
            high, low = split(part.T)
            threes.append(other_three(high, low, 0))
        for g in range(jl // 2):
            total = jnp.zeros((2 * r, r), F32)
            for h in range(per):
                joint = mm(sl3[g], threes[h])
                i, k = 2 * g * per + h, (2 * g + 1) * per + h
                value = jnp.concatenate(
                    [right_v[:, i * w:(i + 1) * w], right_v[:, k * w:(k + 1) * w]], axis=0)
                qh, ql = split(value * inverse(joint))
                both = mm(qh, pairs[h])
                total += both[:, :r] + both[:, r:] + mm(ql, pairs[h][:, :r])
            result = slf[g] * (total * inv_u)
            outv[:, 2 * g, :] = result[:r]
            outv[:, 2 * g + 1, :] = result[r:]
    with scope("a2asend"):
        to_all(lambda to, slot: remote(outv.at[to], second_out.at[me], 7, to).start())
        own_out = pltpu.make_async_copy(outv.at[me], second_out.at[me], in_sem.at[1])
        own_out.start()
    with scope("ag3wait"):
        def finish(q):
            t, parts = blocks(q)

            @pl.when(q == 0)
            def _():
                wait(last.at[pl.ds(0, (xh * cols - 1) * mc)], recv_sem.at[LAST + t])

            @pl.when(q != 0)
            def _():
                wait(last.at[pl.ds(0, xh * cols * mc)], recv_sem.at[LAST + t])

            for part in parts:
                remote(last.at[part], left_out.at[part], LAST, partner, LASTF).start()
                pltpu.make_async_copy(last.at[part], left_out.at[part], in_sem.at[2]).start()

        loop(nt, finish)
    with scope("a2await"):
        own_out.wait()
        wait(second_out.at[pl.ds(0, d - 1)], recv_sem.at[7])
    with scope("ag3end"):
        wait(left_out.at[pl.ds(0, m // 2)], in_sem.at[2])
        wait(left_out.at[pl.ds(0, m // 2)], recv_sem.at[LASTF])
    with scope("sendwait"):
        wait(sleft_v.at[pl.ds(0, r - rr)], send_sem.at[0])
        wait(sright_v.at[pl.ds(0, cols - 1)], send_sem.at[1])
        wait(sc.at[pl.ds(0, d - 1)], send_sem.at[4])
        wait(sright_new.at[pl.ds(0, d - 1)], send_sem.at[5])
        wait(second_out.at[pl.ds(0, d - 1)], send_sem.at[7])
        for turn, phase in ((0, 2), (1, 6)):
            wait(ra.at[turn, :, pl.ds(0, 10)], send_sem.at[phase])
            wait(ur.at[turn], send_sem.at[PAIR + turn])
            wait(pr.at[turn, pl.ds(0, half)], send_sem.at[PAIR + turn])
        wait(la.at[pl.ds(0, (half - 1) * mc)], send_sem.at[3])
        wait(la.at[pl.ds(0, half * mc)], send_sem.at[GATHER])
        wait(last.at[pl.ds(0, (half - 1) * mc)], send_sem.at[8])
        wait(last.at[pl.ds(0, half * mc)], send_sem.at[LAST])


def solution(mesh):
    rows, cols = mesh.shape["row"], mesh.shape["col"]
    d = rows * cols

    def body(slab, left, right, sleft, sright):
        m, width = slab.shape
        r = left.shape[1]
        depth = sright.shape[1] * cols
        jl = width // depth
        w = depth // 2
        nb = width // w
        mc = m // d
        rt = m // TILES
        own_k = depth // d
        sleft = sleft.reshape(r // rows, d, jl, r)
        sright = sright.T.reshape(d // cols, own_k, r)
        hbm = pl.BlockSpec(memory_space=pl.ANY)
        left_out, second = pl.pallas_call(
            functools.partial(kernel, (rows, cols, m, r, w, jl, depth)),
            out_shape=(jax.ShapeDtypeStruct((m, r), F32),
                       jax.ShapeDtypeStruct((d, jl, r), F32)),
            in_specs=[hbm] * 5,
            out_specs=(hbm, hbm),
            scratch_shapes=[
                pltpu.VMEM((m, width), F32),
                pltpu.VMEM((m, r), F32),
                pltpu.VMEM((r, width), F32),
                pltpu.VMEM((nb, w, r), F32),
                pltpu.VMEM((r, jl, r), F32),
                pltpu.VMEM((cols, d // cols, own_k, r), F32),
                pltpu.VMEM((d, jl, r), F32),
                pltpu.VMEM((rt, w), F32),
                pltpu.VMEM((TILES, rt, 2 * r), BF16),
                pltpu.VMEM((TILES, 2 * r, rt), BF16),
                pltpu.VMEM((nb, r, w), BF16),
                pltpu.VMEM((nb, w, r), BF16),
                pltpu.VMEM((nb, r, w), F32),
                pltpu.VMEM((r, 128), F32),
                pltpu.VMEM((m, r), F32),
                pltpu.VMEM((mc, r), F32),
                pltpu.VMEM((mc, r), F32),
                pltpu.VMEM((m, r), F32),
                pltpu.VMEM((d, own_k, r), F32),
                pltpu.VMEM((d - 1, own_k, r), F32),
                pltpu.VMEM((d, own_k, r), F32),
                pltpu.VMEM((own_k, r), F32),
                pltpu.VMEM((d, jl, r), F32),
                pltpu.VMEM((8, r), F32),
                pltpu.VMEM((jl // 2, 2 * r, 3 * r), BF16),
                pltpu.VMEM((jl // 2, 2 * r, 2 * r), BF16),
                pltpu.VMEM((jl // 2, 3 * r, 2 * r), BF16),
                pltpu.VMEM((2, w, 3 * r), BF16),
                pltpu.VMEM((jl // 2, 2 * r, r), F32),
                pltpu.VMEM((2, 8, r), F32),
                pltpu.VMEM((2, 8, r), F32),
                pltpu.VMEM((2, d, mc, r), F32),
                pltpu.VMEM((2, d, mc, r), F32),
                pltpu.VMEM((2, d, 16, r), F32),
                pltpu.VMEM((2, d // 2 - 1, 16, r), F32),
                pltpu.SemaphoreType.DMA((TILES,)),
                pltpu.SemaphoreType.DMA((5,)),
                pltpu.SemaphoreType.DMA((9 + 6 * TILES,)),
                pltpu.SemaphoreType.DMA((9 + 6 * TILES + 2,)),
            ],
            compiler_params=pltpu.CompilerParams(
                collective_id=0, has_side_effects=True, vmem_limit_bytes=60 * 1024 * 1024),
        )(slab, left, right, sleft, sright)
        return left_out, second.reshape(d * jl, r)

    placed = (P(None, ("row", "col")), P(), P(None, ("row", "col")), P("row", None), P(None, "col"))
    return jax.shard_map(
        body, mesh=mesh, in_specs=placed, out_specs=(P(), P(("row", "col"), None)), check_vma=False
    )
```

```python
import contextlib
import functools

import jax
import jax.numpy as jnp
from jax import lax
from jax.experimental import pallas as pl
from jax.experimental.pallas import tpu as pltpu
from jax.sharding import PartitionSpec as P

F32 = jnp.float32
BF16 = jnp.bfloat16
NN = (((1,), (0,)), ((), ()))
NT = (((1,), (1,)), ((), ()))
TILES = 4
AHEAD = 1
CHUNK = 4
SCALE = 1.5


def scope(_):
    return contextlib.nullcontext()


def mm(a, b, dims=NN):
    return lax.dot_general(a, b, dims, preferred_element_type=F32)


def split(x):
    high = x.astype(BF16)
    low = (x - high.astype(F32)).astype(BF16)
    return high, low


def inverse(x):
    guess = pl.reciprocal(x, approx=True)
    return guess * (2.0 - x * guess)


def three(high, low, axis):
    return jnp.concatenate([high, high, low], axis=axis)


def other_three(high, low, axis):
    return jnp.concatenate([high, low, high], axis=axis)


def kernel(sizes, slab, left, right, sleft, sright, left_out, second_out, *scratch):
    (rows, cols, m, r, w, jl, depth) = sizes
    (slab_v, left_v, right_v, right_t, sleft_v, sright_v, c2_v, noise, left2, left_t, rd, rpair,
     nacc, csum, sums_v, la, lc, mult, last, sc, rc, sright_new, cb, outv, keep,
     sl3, slpair, slt3, srt3, slf, ub, ur, sa, pr, sm, ra,
     slab_sem, in_sem, send_sem, recv_sem) = scratch
    d = rows * cols
    nt = TILES
    rt = m // nt
    nb = rd.shape[0]
    mc = m // d
    dt = d // nt
    xh = dt // (2 * cols)
    own_k = depth // d
    per = depth // w
    rr = r // rows
    half = d // 2
    my_row, my_col = lax.axis_index("row"), lax.axis_index("col")
    me = my_row * cols + my_col
    my_z = lax.div(me, dt)
    my_in = lax.rem(me, dt)
    core = lax.rem(my_row, 2)
    my_x = lax.rem(lax.div(my_row, 2), xh)
    partner = me + cols * (1 - 2 * core)
    PAIR, GATHER, FORWARD, LAST, LASTF = 9, 9 + 2 * nt, 9 + 3 * nt, 9 + 4 * nt, 9 + 5 * nt

    def wait(ref, sem):
        pltpu.make_async_copy(ref, ref, sem).wait()

    def remote(src, dst, phase, to, recv=None):
        return pltpu.make_async_remote_copy(
            src, dst, send_sem.at[phase], recv_sem.at[phase if recv is None else recv],
            device_id=to, device_id_type=pl.DeviceIdType.LOGICAL)

    def near_first(q):
        return lax.rem(my_z + lax.div(q * (q + 1), 2), nt)

    def loop(n, body, start=0, unroll=1):
        def step(k, _):
            body(k)
            return 0

        lax.fori_loop(start, n, step, 0, unroll=unroll)

    def offset(z):
        oz = z - my_z
        return jnp.where(oz < 0, oz + nt, oz)

    def to_whole_plane(z, start, first):
        def one(k):
            i = my_in + k
            start(z * dt + jnp.where(i >= dt, i - dt, i), first + k)

        loop(dt, one, 1, dt - 1)

        @pl.when(z != my_z)
        def _():
            one(0)

    def to_all(start):
        def plane(q):
            z = near_first(nt - 1 - q)
            to_whole_plane(z, start, offset(z) * dt - 1)

        loop(nt, plane)

    def to_plane(z, start, first=0):
        for ox in range(xh):
            x = my_x + ox
            x = jnp.where(x >= xh, x - xh, x)
            base = z * dt + (x * 2 + core) * cols

            def one(k, base=base, ox=ox):
                c = my_col + k
                start(base + jnp.where(c >= cols, c - cols, c), first + ox * cols + k)

            if ox == 0:
                @pl.when(z != my_z)
                def _():
                    one(0)
                loop(cols, one, 1, cols - 1)
            else:
                loop(cols, one, 0, cols)

    with scope("start"):
        left_in = pltpu.make_async_copy(left, left_v, in_sem.at[0])
        left_in.start()
        right_in = pltpu.make_async_copy(right, right_v, in_sem.at[3])
        right_in.start()
        for i in range(nb):
            part = pl.ds(i * w, w)
            pltpu.make_async_copy(slab.at[:, part], slab_v.at[:, part], slab_sem.at[i]).start()
        barrier = pltpu.get_barrier_semaphore()

        def greet(k):
            t = me + k
            pl.semaphore_signal(barrier, inc=1, device_id=jnp.where(t >= d, t - d, t),
                                device_id_type=pl.DeviceIdType.LOGICAL)

        own_sleft = pltpu.make_async_copy(
            sleft.at[:, me], sleft_v.at[pl.ds(my_row * rr, rr)], in_sem.at[1])
        own_sleft.start()
        own_sright = pltpu.make_async_copy(sright, sright_v.at[my_col], in_sem.at[2])
        own_sright.start()
        c2_in = pltpu.make_async_copy(sleft.at[my_col], c2_v, in_sem.at[4])
        c2_in.start()

    def prepare(source, t):
        value = source[pl.ds(t * rt, rt), :]
        high, low = split(value)
        left2[t] = jnp.concatenate([high, low], axis=1)
        turned = value.T
        high, low = split(turned)
        left_t[t] = jnp.concatenate([high, low], axis=0)
        csum[...] += SCALE * jnp.broadcast_to(jnp.sum(turned, axis=1, keepdims=True), csum.shape)

    def dither(i, t):
        at = pl.multiple_of(8 * lax.rem(11 * i + 9 * t + 5 * me, rt // 8), 8)
        return noise[pl.ds(at, rt), :]

    def products(count, one):
        ahead = [one(i) for i in range(AHEAD)]
        for i in range(count):
            if i + AHEAD < count:
                ahead.append(one(i + AHEAD))
            yield i, ahead[i]

    def right_times(i):
        return jnp.concatenate([rd[i], rd[i]], axis=0)

    def new_right(i, total, inv_c):
        cut = pl.ds(i * w, w)
        new = right_v[:, cut] * (total * inv_c)
        right_v[:, cut] = new
        turned = new.T
        right_t[i] = turned
        return new, turned

    def rounded_right(i, new, turned):
        rd[i] = (new * dither(i, 1)[:r]).astype(BF16)
        high, low = split(turned)
        rpair[i] = jnp.concatenate([high, low], axis=1)
        sums_v[0:1] += SCALE * jnp.sum(turned, axis=0, keepdims=True)

    def right_blocks(first, count):
        for g in range(count):
            i = first + g
            wait(slab_v.at[:, pl.ds(0, w)], slab_sem.at[i])
        parts = []
        for n, joint in products(count * nt, lambda n: mm(left2[n % nt], right_times(first + n // nt))):
            i, t = first + n // nt, n % nt
            rows_t, cut = slice(t * rt, (t + 1) * rt), pl.ds(i * w, w)
            top = slab_v[rows_t, cut] * (SCALE * dither(i, t))
            slab_v[rows_t, cut] = top
            parts.append((top * inverse(joint)).astype(BF16))
            if t == nt - 1:
                both = mm(jnp.concatenate([left_t[k] for k in range(nt)], axis=1),
                          jnp.concatenate(parts, axis=0))
                parts = []
                nacc[i] = both[:r] + both[r:]

    def quotients(t):
        part = pl.ds(t * rt, rt)
        lhs = left2[t]
        for i, joint in products(nb, lambda i: mm(lhs, right_times(i))):
            yield i, (slab_v[part, i * w:(i + 1) * w] * inverse(joint)).astype(BF16)

    def right_tile(t):
        turned = left_t[t]
        for i, quotient in quotients(t):
            both = mm(turned, quotient)
            nacc[i] += both[:r] + both[r:]

    def left_tile(t, buffer):
        total = jnp.zeros((rt, r), F32)
        parts = []
        for i, quotient in quotients(t):
            parts.append(quotient)
            if len(parts) == CHUNK:
                both = mm(jnp.concatenate(parts, axis=1),
                          jnp.concatenate([rpair[k] for k in range(i + 1 - CHUNK, i + 1)], axis=0))
                total += both[:, :r] + both[:, r:]
                parts = []
        buffer[pl.ds(t * dt, dt)] = total.reshape(dt, mc, r)

    def reset():
        nacc[...] = jnp.zeros_like(nacc)
        csum[...] = jnp.zeros_like(csum)
        sums_v[...] = jnp.zeros_like(sums_v)

    def group(z, x, c):
        return z * dt + (x * 2 + c) * cols

    def left_sums(turn, phase):
        mine, theirs, message, arrived = sa.at[turn], pr.at[turn], sm.at[turn], ra.at[turn]
        remote(ub.at[turn], ur.at[turn], PAIR + turn, partner, 9 + 6 * nt + turn).start()

        rows_sent = 10 - turn

        def combine(q):
            t = near_first(nt - 1 - q)
            wait(theirs.at[pl.ds(0, xh * cols)], recv_sem.at[PAIR + turn * nt + q])
            for x in range(xh):
                part = pl.ds(group(t, x, core), cols)
                message[part, 0:mc, :] = mine[part] + theirs[part]
                message[part, 8:16, :] = jnp.broadcast_to((ub[turn] + ur[turn])[None], (cols, 8, r))
            to_plane(t, lambda to, slot: remote(
                message.at[to, pl.ds(0, rows_sent)], arrived.at[slot, pl.ds(0, rows_sent)],
                phase, to).start(), offset(t) * (xh * cols) - 1)

        def tile(q):
            t = near_first(nt - 1 - q)
            left_tile(t, mine)
            for x in range(xh):
                part = pl.ds(group(t, x, 1 - core), cols)
                remote(mine.at[part], theirs.at[part], PAIR + turn, partner,
                       PAIR + turn * nt + q).start()

            @pl.when(q == 1)
            def _():
                wait(ur.at[turn], recv_sem.at[9 + 6 * nt + turn])

            @pl.when(q > 0)
            def _():
                combine(q - 1)

        loop(nt, tile)
        combine(nt - 1)

    def owned(turn, phase, old):
        wait(ra.at[turn, :, pl.ds(0, 10 - turn)], recv_sem.at[phase])
        own = sm[turn, me]
        numer = own[:mc] + jnp.sum(ra[turn, :, 0:mc, :], axis=0)
        tail = own[8:10 - turn] + jnp.sum(ra[turn, :, 8:10 - turn, :], axis=0)
        return old * numer / tail[0:1], tail

    with scope("prep"):
        reset()
        down = lax.broadcasted_iota(jnp.int32, noise.shape, 0).astype(F32)
        across = lax.broadcasted_iota(jnp.int32, noise.shape, 1).astype(F32)
        one = down * 0.7548776662 + across * 0.5698402910
        two = down * 0.6710436067 + across * 0.8191725134
        noise[...] = 1.0 + ((one - jnp.floor(one)) + (two - jnp.floor(two)) - 1.0) * (1.0 / 128)
        left_in.wait()

        def greet_and_prepare(t):
            for k in range(1, dt):
                greet(t * dt + k)

            @pl.when(t > 0)
            def _():
                greet(t * dt)

            prepare(left_v, t)

        loop(nt, greet_and_prepare)
        right_in.wait()
        for i in range(nb):
            rd[i] = (right_v[:, i * w:(i + 1) * w] * dither(i, 1)[:r]).astype(BF16)

    line = lax.broadcasted_iota(jnp.int32, (8, r), 0)
    with scope("right1"):
        inv_c = 1.0 / csum[:, 0:1]

        def finish_blocks(first):
            for i in (first, first + 1):
                rounded_right(i, *new_right(i, nacc[i], inv_c))

        right_blocks(0, 2)

        def two_blocks(g):
            right_blocks(2 * g, 2)
            finish_blocks(2 * g - 2)

        loop(nb // 2, two_blocks, 1)
        finish_blocks(nb - 2)
        c2_in.wait()
        part2 = jnp.sum(jnp.sum(c2_v[...], axis=0), axis=0, keepdims=True)
        ub[0] = jnp.where(line == 0, sums_v[0:1], part2)

    with scope("barrier"):
        pl.semaphore_wait(barrier, d - 1)

    with scope("sendin"):
        def send_sleft(k):
            t = lax.rem(my_row + k, rows) * cols + my_col
            remote(sleft.at[:, t], sleft_v.at[pl.ds(my_row * rr, rr)], 0, t).start()

        def send_sright(k):
            t = my_row * cols + lax.rem(my_col + k, cols)
            remote(sright, sright_v.at[my_col], 1, t).start()

    with scope("left1"):
        left_sums(0, 2)

    with scope("sendin"):
        loop(rows, send_sleft, 1)
        loop(cols, send_sright, 1)
        reset()

    with scope("rs1wait"):
        new, tail = owned(0, 2, left_v[pl.ds(me * mc, mc), :])
        keep[...] = jnp.broadcast_to(tail[1:2], (8, r))
        lc[...] = new
        la[pl.ds(me * mc, mc), :] = new
    with scope("ag1send"):
        def share(to, slot):
            remote(lc, la.at[pl.ds(me * mc, mc)], 3, to, GATHER + my_z).start()

        loop(nt, lambda q: to_plane(near_first(q), share))

    def blocks(q):
        t = near_first(q)
        return t, [pl.ds(group(t, x, core) * mc, cols * mc) for x in range(xh)]

    with scope("slprep"):
        own_sleft.wait()
        wait(sleft_v.at[pl.ds(0, r - rr)], recv_sem.at[0])
        own_sright.wait()
        wait(sright_v.at[pl.ds(0, cols - 1)], recv_sem.at[1])
        for g in range(jl // 2):
            two = jnp.concatenate([sleft_v[:, 2 * g, :], sleft_v[:, 2 * g + 1, :]], axis=0)
            slf[g] = two
            high, low = split(two)
            sl3[g] = three(high, low, 1)
            slpair[g] = jnp.concatenate([high, low], axis=1)
            high, low = split(two.T)
            slt3[g] = other_three(high, low, 0)
        for h in range(per):
            high, low = split(sright_v[pl.ds(h * (cols // per), cols // per)].reshape(w, r))
            srt3[h] = three(high, low, 1)

    with scope("right2"):
        def forward(q):
            t, parts = blocks(q)

            @pl.when(q == 0)
            def _():
                wait(la.at[pl.ds(0, (xh * cols - 1) * mc)], recv_sem.at[GATHER + t])

            @pl.when(q != 0)
            def _():
                wait(la.at[pl.ds(0, xh * cols * mc)], recv_sem.at[GATHER + t])

            for part in parts:
                remote(la.at[part], la.at[part], GATHER, partner, FORWARD + q).start()

        forward(0)

        def second(q):
            t = near_first(q)
            wait(la.at[pl.ds(0, xh * cols * mc)], recv_sem.at[FORWARD + q])

            @pl.when(q < nt - 1)
            def _():
                forward(q + 1)

            prepare(la, t)
            right_tile(t)

        loop(nt, second)
        inv_c = 1.0 / csum[:, 0:1]
        for i in range(nb):
            new_right(i, nacc[i], inv_c)

    with scope("numer2"):
        for h in range(per):
            total = jnp.zeros((w, r), F32)
            for g in range(jl // 2):
                joint = mm(srt3[h], slt3[g])
                value = jnp.concatenate(
                    [right_t[2 * g * per + h], right_t[(2 * g + 1) * per + h]], axis=1)
                qh, ql = split(value * inverse(joint))
                both = mm(qh, slpair[g])
                total += both[:, :r] + both[:, r:] + mm(ql, slpair[g, :, :r])
            sc[pl.ds(h * (d // per), d // per)] = total.reshape(d // per, own_k, r)
    with scope("rs2send"):
        to_all(lambda to, slot: remote(sc.at[to], rc.at[slot], 4, to).start())

    with scope("left2"):
        for i in range(nb):
            rounded_right(i, right_v[:, i * w:(i + 1) * w], right_t[i])
        ub[1] = jnp.broadcast_to(sums_v[0:1], (8, r))
        left_sums(1, 6)

    with scope("rs2wait"):
        wait(rc, recv_sem.at[4])
    with scope("rs2sum"):
        numer = sc[me] + jnp.sum(rc[...], axis=0)
        cb[...] = (sright_v[lax.div(me, d // cols), lax.rem(me, d // cols)]
                   * numer / keep[0:1])
        sright_new[me] = cb[...]
    with scope("ag2send"):
        to_all(lambda to, slot: remote(cb, sright_new.at[me], 5, to).start())
    with scope("rs3wait"):
        new, _ = owned(1, 6, la[pl.ds(me * mc, mc), :])
        mult[...] = new
        last[pl.ds(me * mc, mc), :] = new
    with scope("ag3send"):
        def ag3(q):
            to_plane(near_first(q), lambda to, slot: remote(
                mult, last.at[pl.ds(me * mc, mc)], 8, to, LAST + my_z).start())

        loop(nt, ag3)
    with scope("ag2wait"):
        wait(sright_new.at[pl.ds(0, d - 1)], recv_sem.at[5])
    with scope("left3"):
        fresh = sright_new[...].reshape(depth, r)
        inv_u = 1.0 / jnp.sum(fresh, axis=0, keepdims=True)
        threes, pairs = [], []
        for h in range(per):
            part = fresh[h * w:(h + 1) * w]
            high, low = split(part)
            pairs.append(jnp.concatenate([high, low], axis=1))
            high, low = split(part.T)
            threes.append(other_three(high, low, 0))
        for g in range(jl // 2):
            total = jnp.zeros((2 * r, r), F32)
            for h in range(per):
                joint = mm(sl3[g], threes[h])
                i, k = 2 * g * per + h, (2 * g + 1) * per + h
                value = jnp.concatenate(
                    [right_v[:, i * w:(i + 1) * w], right_v[:, k * w:(k + 1) * w]], axis=0)
                qh, ql = split(value * inverse(joint))
                both = mm(qh, pairs[h])
                total += both[:, :r] + both[:, r:] + mm(ql, pairs[h][:, :r])
            result = slf[g] * (total * inv_u)
            outv[:, 2 * g, :] = result[:r]
            outv[:, 2 * g + 1, :] = result[r:]
    with scope("a2asend"):
        to_all(lambda to, slot: remote(outv.at[to], second_out.at[me], 7, to).start())
        own_out = pltpu.make_async_copy(outv.at[me], second_out.at[me], in_sem.at[1])
        own_out.start()
    with scope("ag3wait"):
        def finish(q):
            t, parts = blocks(q)

            @pl.when(q == 0)
            def _():
                wait(last.at[pl.ds(0, (xh * cols - 1) * mc)], recv_sem.at[LAST + t])

            @pl.when(q != 0)
            def _():
                wait(last.at[pl.ds(0, xh * cols * mc)], recv_sem.at[LAST + t])

            for part in parts:
                remote(last.at[part], left_out.at[part], LAST, partner, LASTF).start()
                pltpu.make_async_copy(last.at[part], left_out.at[part], in_sem.at[2]).start()

        loop(nt, finish)
    with scope("a2await"):
        own_out.wait()
        wait(second_out.at[pl.ds(0, d - 1)], recv_sem.at[7])
    with scope("ag3end"):
        wait(left_out.at[pl.ds(0, m // 2)], in_sem.at[2])
        wait(left_out.at[pl.ds(0, m // 2)], recv_sem.at[LASTF])
    with scope("sendwait"):
        wait(sleft_v.at[pl.ds(0, r - rr)], send_sem.at[0])
        wait(sright_v.at[pl.ds(0, cols - 1)], send_sem.at[1])
        wait(sc.at[pl.ds(0, d - 1)], send_sem.at[4])
        wait(sright_new.at[pl.ds(0, d - 1)], send_sem.at[5])
        wait(second_out.at[pl.ds(0, d - 1)], send_sem.at[7])
        for turn, phase in ((0, 2), (1, 6)):
            wait(ra.at[turn, :, pl.ds(0, 10 - turn)], send_sem.at[phase])
            wait(ur.at[turn], send_sem.at[PAIR + turn])
            wait(pr.at[turn, pl.ds(0, half)], send_sem.at[PAIR + turn])
        wait(la.at[pl.ds(0, (half - 1) * mc)], send_sem.at[3])
        wait(la.at[pl.ds(0, half * mc)], send_sem.at[GATHER])
        wait(last.at[pl.ds(0, (half - 1) * mc)], send_sem.at[8])
        wait(last.at[pl.ds(0, half * mc)], send_sem.at[LAST])


def deliver(left, second, left_out, second_out, left_v, second_v, sem):
    ins = (pltpu.make_async_copy(left, left_v, sem.at[0]),
           pltpu.make_async_copy(second, second_v, sem.at[1]))
    outs = (pltpu.make_async_copy(left_v, left_out, sem.at[2]),
            pltpu.make_async_copy(second_v, second_out, sem.at[3]))
    for copy in ins:
        copy.start()
    for copy, out in zip(ins, outs):
        copy.wait()
        out.start()
    for out in outs:
        out.wait()


def solution(mesh):
    rows, cols = mesh.shape["row"], mesh.shape["col"]
    d = rows * cols

    def body(slab, left, right, sleft, sright):
        m, width = slab.shape
        r = left.shape[1]
        depth = sright.shape[1] * cols
        jl = width // depth
        w = depth // 2
        nb = width // w
        mc = m // d
        rt = m // TILES
        own_k = depth // d
        sleft = sleft.reshape(r // rows, d, jl, r)
        sright = sright.T.reshape(d // cols, own_k, r)
        hbm = pl.BlockSpec(memory_space=pl.ANY)
        left_out, second = pl.pallas_call(
            functools.partial(kernel, (rows, cols, m, r, w, jl, depth)),
            out_shape=(jax.ShapeDtypeStruct((m, r), F32),
                       jax.ShapeDtypeStruct((d, jl, r), F32)),
            in_specs=[hbm] * 5,
            out_specs=(hbm, hbm),
            scratch_shapes=[
                pltpu.VMEM((m, width), F32),
                pltpu.VMEM((m, r), F32),
                pltpu.VMEM((r, width), F32),
                pltpu.VMEM((nb, w, r), F32),
                pltpu.VMEM((r, jl, r), F32),
                pltpu.VMEM((cols, d // cols, own_k, r), F32),
                pltpu.VMEM((d, jl, r), F32),
                pltpu.VMEM((2 * rt, w), F32),
                pltpu.VMEM((TILES, rt, 2 * r), BF16),
                pltpu.VMEM((TILES, 2 * r, rt), BF16),
                pltpu.VMEM((nb, r, w), BF16),
                pltpu.VMEM((nb, w, 2 * r), BF16),
                pltpu.VMEM((nb, r, w), F32),
                pltpu.VMEM((r, 128), F32),
                pltpu.VMEM((8, r), F32),
                pltpu.VMEM((m, r), F32),
                pltpu.VMEM((mc, r), F32),
                pltpu.VMEM((mc, r), F32),
                pltpu.VMEM((m, r), F32),
                pltpu.VMEM((d, own_k, r), F32),
                pltpu.VMEM((d - 1, own_k, r), F32),
                pltpu.VMEM((d, own_k, r), F32),
                pltpu.VMEM((own_k, r), F32),
                pltpu.VMEM((d, jl, r), F32),
                pltpu.VMEM((8, r), F32),
                pltpu.VMEM((jl // 2, 2 * r, 3 * r), BF16),
                pltpu.VMEM((jl // 2, 2 * r, 2 * r), BF16),
                pltpu.VMEM((jl // 2, 3 * r, 2 * r), BF16),
                pltpu.VMEM((2, w, 3 * r), BF16),
                pltpu.VMEM((jl // 2, 2 * r, r), F32),
                pltpu.VMEM((2, 8, r), F32),
                pltpu.VMEM((2, 8, r), F32),
                pltpu.VMEM((2, d, mc, r), F32),
                pltpu.VMEM((2, d, mc, r), F32),
                pltpu.VMEM((2, d, 16, r), F32),
                pltpu.VMEM((2, d // 2 - 1, 16, r), F32),
                pltpu.SemaphoreType.DMA((nb,)),
                pltpu.SemaphoreType.DMA((5,)),
                pltpu.SemaphoreType.DMA((9 + 6 * TILES,)),
                pltpu.SemaphoreType.DMA((9 + 6 * TILES + 2,)),
            ],
            compiler_params=pltpu.CompilerParams(
                collective_id=0, has_side_effects=True, vmem_limit_bytes=60 * 1024 * 1024),
        )(slab, left, right, sleft, sright)
        second = second.reshape(d * jl, r)
        return pl.pallas_call(
            deliver,
            out_shape=(jax.ShapeDtypeStruct((m, r), F32),
                       jax.ShapeDtypeStruct((d * jl, r), F32)),
            in_specs=[hbm] * 2,
            out_specs=(hbm, hbm),
            scratch_shapes=[pltpu.VMEM((m, r), F32), pltpu.VMEM((d * jl, r), F32),
                            pltpu.SemaphoreType.DMA((4,))],
            compiler_params=pltpu.CompilerParams(vmem_limit_bytes=60 * 1024 * 1024),
        )(left_out, second)

    placed = (P(None, ("row", "col")), P(), P(None, ("row", "col")), P("row", None), P(None, "col"))
    return jax.shard_map(
        body, mesh=mesh, in_specs=placed, out_specs=(P(), P(("row", "col"), None)), check_vma=False
    )
```

```python
import contextlib
import functools

import jax
import jax.numpy as jnp
from jax import lax
from jax.experimental import pallas as pl
from jax.experimental.pallas import tpu as pltpu
from jax.sharding import PartitionSpec as P

F32 = jnp.float32
BF16 = jnp.bfloat16
NN = (((1,), (0,)), ((), ()))
NT = (((1,), (1,)), ((), ()))
TILES = 4
AHEAD = 1
CHUNK = 4
SCALE = 1.5


def scope(_):
    return contextlib.nullcontext()


def mm(a, b, dims=NN):
    return lax.dot_general(a, b, dims, preferred_element_type=F32)


def split(x):
    high = x.astype(BF16)
    low = (x - high.astype(F32)).astype(BF16)
    return high, low


def inverse(x):
    guess = pl.reciprocal(x, approx=True)
    return guess * (2.0 - x * guess)


def three(high, low, axis):
    return jnp.concatenate([high, high, low], axis=axis)


def other_three(high, low, axis):
    return jnp.concatenate([high, low, high], axis=axis)


def kernel(sizes, slab, left, right, sleft, sright, left_out, second_out, *scratch):
    (rows, cols, m, r, w, jl, depth) = sizes
    (slab_v, left_v, right_v, right_t, sleft_v, sright_v, c2_v, noise, left2, left_t, rd, rpair,
     nacc, csum, sums_v, la, lc, mult, last, sp, sq, sc, rc, sright_new, cb, outv, keep,
     sl3, slpair, slt3, inv2, slf, ub, ur, sa, pr, sm, ra,
     slab_sem, in_sem, send_sem, recv_sem) = scratch
    d = rows * cols
    nt = TILES
    rt = m // nt
    nb = rd.shape[0]
    mc = m // d
    dt = d // nt
    xh = dt // (2 * cols)
    own_k = depth // d
    per = depth // w
    rr = r // rows
    half = d // 2
    my_row, my_col = lax.axis_index("row"), lax.axis_index("col")
    me = my_row * cols + my_col
    my_z = lax.div(me, dt)
    my_in = lax.rem(me, dt)
    core = lax.rem(my_row, 2)
    my_x = lax.rem(lax.div(my_row, 2), xh)
    partner = me + cols * (1 - 2 * core)
    PAIR, GATHER, FORWARD, LAST, LASTF = 9, 9 + 2 * nt, 9 + 3 * nt, 9 + 4 * nt, 9 + 5 * nt

    def wait(ref, sem):
        pltpu.make_async_copy(ref, ref, sem).wait()

    def remote(src, dst, phase, to, recv=None):
        return pltpu.make_async_remote_copy(
            src, dst, send_sem.at[phase], recv_sem.at[phase if recv is None else recv],
            device_id=to, device_id_type=pl.DeviceIdType.LOGICAL)

    def near_first(q):
        return lax.rem(my_z + lax.div(q * (q + 1), 2), nt)

    def loop(n, body, start=0, unroll=1):
        def step(k, _):
            body(k)
            return 0

        lax.fori_loop(start, n, step, 0, unroll=unroll)

    def offset(z):
        oz = z - my_z
        return jnp.where(oz < 0, oz + nt, oz)

    def to_whole_plane(z, start, first):
        def one(k):
            i = my_in + k
            start(z * dt + jnp.where(i >= dt, i - dt, i), first + k)

        loop(dt, one, 1, dt - 1)

        @pl.when(z != my_z)
        def _():
            one(0)

    def to_all(start):
        def plane(q):
            z = near_first(nt - 1 - q)
            to_whole_plane(z, start, offset(z) * dt - 1)

        loop(nt, plane)

    def to_plane(z, start, first=0):
        for ox in range(xh):
            x = my_x + ox
            x = jnp.where(x >= xh, x - xh, x)
            base = z * dt + (x * 2 + core) * cols

            def one(k, base=base, ox=ox, x=x):
                c = my_col + k
                c = jnp.where(c >= cols, c - cols, c)
                start(base + c, first + ox * cols + k, (z * xh + x) * cols + c)

            if ox == 0:
                @pl.when(z != my_z)
                def _():
                    one(0)
                loop(cols, one, 1, cols - 1)
            else:
                loop(cols, one, 0, cols)

    with scope("start"):
        left_in = pltpu.make_async_copy(left, left_v, in_sem.at[0])
        left_in.start()
        right_in = pltpu.make_async_copy(right, right_v, in_sem.at[3])
        right_in.start()
        barrier = pltpu.get_barrier_semaphore()

        def greet(k):
            t = me + k
            pl.semaphore_signal(barrier, inc=1, device_id=jnp.where(t >= d, t - d, t),
                                device_id_type=pl.DeviceIdType.LOGICAL)

        for g in range(nt):
            for k in range(max(1, g * dt), (g + 1) * dt):
                greet(k)
            for i in range(g * nb // nt, (g + 1) * nb // nt):
                part = pl.ds(i * w, w)
                pltpu.make_async_copy(slab.at[:, part], slab_v.at[:, part], slab_sem.at[i]).start()
        own_sleft = pltpu.make_async_copy(
            sleft.at[:, me], sleft_v.at[pl.ds(my_row * rr, rr)], in_sem.at[1])
        own_sleft.start()
        own_sright = pltpu.make_async_copy(sright, sright_v.at[my_col], in_sem.at[2])
        own_sright.start()
        c2_in = pltpu.make_async_copy(sleft.at[my_col], c2_v, in_sem.at[4])
        c2_in.start()

    def prepare(source, t):
        value = source[pl.ds(t * rt, rt), :]
        high, low = split(value * (1.0 / SCALE))
        left2[t] = jnp.concatenate([high, low], axis=1)
        turned = value.T
        high, low = split(turned)
        left_t[t] = jnp.concatenate([high, low], axis=0)
        csum[...] += SCALE * jnp.broadcast_to(jnp.sum(turned, axis=1, keepdims=True), csum.shape)

    def dither(i, t):
        at = pl.multiple_of(8 * lax.rem(11 * i + 9 * t + 5 * me, rt // 8), 8)
        return noise[pl.ds(at, rt), :]

    def products(count, one):
        ahead = [one(i) for i in range(AHEAD)]
        for i in range(count):
            if i + AHEAD < count:
                ahead.append(one(i + AHEAD))
            yield i, ahead[i]

    def right_times(i):
        return jnp.concatenate([rd[i], rd[i]], axis=0)

    def new_right(i, total, inv_c):
        cut = pl.ds(i * w, w)
        new = right_v[:, cut] * (total * inv_c)
        right_v[:, cut] = new
        turned = new.T
        right_t[i] = turned
        return new, turned

    def rounded_right(i, new, turned):
        rd[i] = (new * dither(i, 1)[:r]).astype(BF16)
        high, low = split(turned)
        rpair[i] = jnp.concatenate([high, low], axis=1)
        sums_v[0:1] += SCALE * jnp.sum(turned, axis=0, keepdims=True)

    def right_blocks(first, count):
        for g in range(count):
            i = first + g
            wait(slab_v.at[:, pl.ds(0, w)], slab_sem.at[i])
        parts = []
        for n, joint in products(count * nt, lambda n: mm(left2[n % nt], right_times(first + n // nt))):
            i, t = first + n // nt, n % nt
            rows_t, cut = slice(t * rt, (t + 1) * rt), pl.ds(i * w, w)
            top = slab_v[rows_t, cut] * dither(i, t)
            slab_v[rows_t, cut] = top
            parts.append((top * inverse(joint)).astype(BF16))
            if t == nt - 1:
                both = mm(jnp.concatenate([left_t[k] for k in range(nt)], axis=1),
                          jnp.concatenate(parts, axis=0))
                parts = []
                nacc[i] = both[:r] + both[r:]

    def quotients(t):
        part = pl.ds(t * rt, rt)
        lhs = left2[t]
        for i, joint in products(nb, lambda i: mm(lhs, right_times(i))):
            yield i, (slab_v[part, i * w:(i + 1) * w] * inverse(joint)).astype(BF16)

    def right_tile(t, inv_c=None):
        turned = left_t[t]
        for i, quotient in quotients(t):
            both = mm(turned, quotient)
            total = nacc[i] + both[:r] + both[r:]
            if inv_c is None:
                nacc[i] = total
            else:
                new_right(i, total, inv_c)

    def left_tile(t, buffer):
        total = jnp.zeros((rt, r), F32)
        parts = []
        for i, quotient in quotients(t):
            parts.append(quotient)
            if len(parts) == CHUNK:
                both = mm(jnp.concatenate(parts, axis=1),
                          jnp.concatenate([rpair[k] for k in range(i + 1 - CHUNK, i + 1)], axis=0))
                total += both[:, :r] + both[:, r:]
                parts = []
        buffer[pl.ds(t * dt, dt)] = total.reshape(dt, mc, r)

    def left_part(t, c, buffer):
        size = cols * mc
        starts = [(x * 2 + c) * size for x in range(xh)]
        lhs = jnp.concatenate([left2[t, pl.ds(at, size), :] for at in starts], axis=0)
        total = jnp.zeros((xh * size, r), F32)
        parts = []
        for i, joint in products(nb, lambda i: mm(lhs, right_times(i))):
            cut = slice(i * w, (i + 1) * w)
            top = jnp.concatenate([slab_v[pl.ds(t * rt + at, size), cut] for at in starts], axis=0)
            parts.append((top * inverse(joint)).astype(BF16))
            if len(parts) == CHUNK:
                both = mm(jnp.concatenate(parts, axis=1),
                          jnp.concatenate([rpair[k] for k in range(i + 1 - CHUNK, i + 1)], axis=0))
                total += both[:, :r] + both[:, r:]
                parts = []
        for x in range(xh):
            buffer[pl.ds(group(t, x, c), cols)] = total[x * size:(x + 1) * size].reshape(cols, mc, r)

    def reset():
        nacc[...] = jnp.zeros_like(nacc)
        csum[...] = jnp.zeros_like(csum)
        sums_v[...] = jnp.zeros_like(sums_v)

    def group(z, x, c):
        return z * dt + (x * 2 + c) * cols

    def left_sums(turn, phase):
        mine, theirs, message, arrived = sa.at[turn], pr.at[turn], sm.at[turn], ra.at[turn]
        remote(ub.at[turn], ur.at[turn], PAIR + turn, partner, 9 + 6 * nt + turn).start()

        rows_sent = 10 - turn

        def combine(q):
            t = near_first(nt - 1 - q)
            wait(theirs.at[pl.ds(0, xh * cols)], recv_sem.at[PAIR + turn * nt + q])
            for x in range(xh):
                part = pl.ds(group(t, x, core), cols)
                message[part, 0:mc, :] = mine[part] + theirs[part]
                message[part, 8:16, :] = jnp.broadcast_to((ub[turn] + ur[turn])[None], (cols, 8, r))
            to_plane(t, lambda to, slot, _: remote(
                message.at[to, pl.ds(0, rows_sent)], arrived.at[slot, pl.ds(0, rows_sent)],
                phase, to).start(), offset(t) * (xh * cols) - 1)

        def exchange(q):
            for x in range(xh):
                part = pl.ds(group(near_first(nt - 1 - q), x, 1 - core), cols)
                remote(mine.at[part], theirs.at[part], PAIR + turn, partner,
                       PAIR + turn * nt + q).start()

        def tile(q):
            left_tile(near_first(nt - 1 - q), mine)
            exchange(q)

            @pl.when(q == 1)
            def _():
                wait(ur.at[turn], recv_sem.at[9 + 6 * nt + turn])

            @pl.when(q > 0)
            def _():
                combine(q - 1)

        loop(nt - 1, tile)
        left_part(my_z, 1 - core, mine)
        exchange(nt - 1)
        combine(nt - 2)
        left_part(my_z, core, mine)
        combine(nt - 1)

    def owned(turn, phase, old):
        wait(ra.at[turn, :, pl.ds(0, 10 - turn)], recv_sem.at[phase])
        own = sm[turn, me]
        numer = own[:mc] + jnp.sum(ra[turn, :, 0:mc, :], axis=0)
        tail = own[8:10 - turn] + jnp.sum(ra[turn, :, 8:10 - turn, :], axis=0)
        return old * numer / tail[0:1], tail

    with scope("prep"):
        reset()
        down = lax.broadcasted_iota(jnp.int32, noise.shape, 0).astype(F32)
        across = lax.broadcasted_iota(jnp.int32, noise.shape, 1).astype(F32)
        one = down * 0.7548776662 + across * 0.5698402910
        two = down * 0.6710436067 + across * 0.8191725134
        noise[...] = 1.0 + ((one - jnp.floor(one)) + (two - jnp.floor(two)) - 1.0) * (1.0 / 128)
        left_in.wait()

        loop(nt, lambda t: prepare(left_v, t))
        right_in.wait()
        for i in range(nb):
            rd[i] = (right_v[:, i * w:(i + 1) * w] * dither(i, 1)[:r]).astype(BF16)

    line = lax.broadcasted_iota(jnp.int32, (8, r), 0)
    with scope("right1"):
        inv_c = 1.0 / csum[:, 0:1]

        def finish_blocks(first):
            for i in (first, first + 1):
                rounded_right(i, *new_right(i, nacc[i], inv_c))

        right_blocks(0, 2)

        def two_blocks(g):
            right_blocks(2 * g, 2)
            finish_blocks(2 * g - 2)

        loop(nb // 2, two_blocks, 1)
        finish_blocks(nb - 2)
        c2_in.wait()
        part2 = jnp.sum(jnp.sum(c2_v[...], axis=0), axis=0, keepdims=True)
        ub[0] = jnp.where(line == 0, sums_v[0:1], part2)

    with scope("barrier"):
        pl.semaphore_wait(barrier, d - 1)

    with scope("sendin"):
        def send_sleft(k):
            t = lax.rem(my_row + k, rows) * cols + my_col
            remote(sleft.at[:, t], sleft_v.at[pl.ds(my_row * rr, rr)], 0, t).start()

        def send_sright(k):
            t = my_row * cols + lax.rem(my_col + k, cols)
            remote(sright, sright_v.at[my_col], 1, t).start()

    with scope("left1"):
        left_sums(0, 2)

    with scope("sendin"):
        loop(rows, send_sleft, 1)
        loop(cols, send_sright, 1)
        reset()

    with scope("rs1wait"):
        new, tail = owned(0, 2, left_v[pl.ds(me * mc, mc), :])
        keep[...] = jnp.broadcast_to(tail[1:2], (8, r))
        lc[...] = new
        la[pl.ds(me * mc, mc), :] = new
    with scope("ag1send"):
        def share(to, slot, _):
            remote(lc, la.at[pl.ds(me * mc, mc)], 3, to, GATHER + my_z).start()

        loop(nt, lambda q: to_plane(near_first(q), share))

    def blocks(q):
        t = near_first(q)
        return t, [pl.ds(group(t, x, core) * mc, cols * mc) for x in range(xh)]

    with scope("slprep"):
        own_sleft.wait()
        wait(sleft_v.at[pl.ds(0, r - rr)], recv_sem.at[0])
        own_sright.wait()
        wait(sright_v.at[pl.ds(0, cols - 1)], recv_sem.at[1])
        for g in range(jl // 2):
            two = jnp.concatenate([sleft_v[:, 2 * g, :], sleft_v[:, 2 * g + 1, :]], axis=0)
            slf[g] = two
            high, low = split(two)
            sl3[g] = three(high, low, 1)
            slpair[g] = jnp.concatenate([high, low], axis=1)
            high, low = split(two.T)
            slt3[g] = other_three(high, low, 0)
        for h in range(per):
            high, low = split(sright_v[pl.ds(h * (cols // per), cols // per)].reshape(w, r))
            lhs = three(high, low, 1)
            for g in range(jl // 2):
                inv2[h, g] = inverse(mm(lhs, slt3[g]))

    with scope("right2"):
        def forward(q):
            t, parts = blocks(q)

            @pl.when(q == 0)
            def _():
                wait(la.at[pl.ds(0, (xh * cols - 1) * mc)], recv_sem.at[GATHER + t])

            @pl.when(q != 0)
            def _():
                wait(la.at[pl.ds(0, xh * cols * mc)], recv_sem.at[GATHER + t])

            for part in parts:
                remote(la.at[part], la.at[part], GATHER, partner, FORWARD + q).start()

        forward(0)

        def second(q):
            t = near_first(q)
            wait(la.at[pl.ds(0, xh * cols * mc)], recv_sem.at[FORWARD + q])
            prepare(la, t)
            right_tile(t)

            @pl.when(q == 0)
            def _():
                for k in range(1, nt):
                    forward(k)

        loop(nt - 1, second)
        t = near_first(nt - 1)
        wait(la.at[pl.ds(0, xh * cols * mc)], recv_sem.at[FORWARD + nt - 1])
        prepare(la, t)
        right_tile(t, 1.0 / csum[:, 0:1])

    chip = (my_z * xh + my_x) * cols + my_col
    mine_k = core * half + chip
    with scope("numer2"):
        def half_numer(h):
            total = jnp.zeros((w, r), F32)
            for g in range(jl // 2):
                value = jnp.concatenate(
                    [right_t[2 * g * per + h], right_t[(2 * g + 1) * per + h]], axis=1)
                qh, ql = split(value * inv2[h, g])
                both = mm(qh, slpair[g])
                total += both[:, :r] + both[:, r:] + mm(ql, slpair[g, :, :r])
            return total.reshape(half, own_k, r)

        sp[...] = half_numer(1 - core)
        remote(sp, sq, 4, partner, 9 + 6 * nt + 2).start()
        own2 = half_numer(core)
        wait(sq, recv_sem.at[9 + 6 * nt + 2])
        sc[...] = own2 + sq[...]
    with scope("rs2send"):
        def rs2(q):
            z = near_first(nt - 1 - q)
            to_plane(z, lambda to, slot, at: remote(sc.at[at], rc.at[slot], 4, to).start(),
                     offset(z) * (xh * cols) - 1)

        loop(nt, rs2)

    with scope("left2"):
        for i in range(nb):
            rounded_right(i, right_v[:, i * w:(i + 1) * w], right_t[i])
        ub[1] = jnp.broadcast_to(sums_v[0:1], (8, r))
        left_sums(1, 6)

    with scope("rs2wait"):
        wait(rc, recv_sem.at[4])
    with scope("rs2sum"):
        numer = sc[chip] + jnp.sum(rc[...], axis=0)
        cb[...] = (sright_v[lax.div(mine_k, d // cols), lax.rem(mine_k, d // cols)]
                   * numer / keep[0:1])
        sright_new[mine_k] = cb[...]
    with scope("ag2send"):
        to_all(lambda to, slot: remote(cb, sright_new.at[mine_k], 5, to).start())
    with scope("rs3wait"):
        new, _ = owned(1, 6, la[pl.ds(me * mc, mc), :])
        mult[...] = new
        last[pl.ds(me * mc, mc), :] = new
    with scope("ag3send"):
        def ag3(q):
            to_plane(near_first(q), lambda to, slot, _: remote(
                mult, last.at[pl.ds(me * mc, mc)], 8, to, LAST + my_z).start())

        loop(nt, ag3)
    with scope("ag2wait"):
        wait(sright_new.at[pl.ds(0, d - 1)], recv_sem.at[5])
    with scope("left3"):
        fresh = sright_new[...].reshape(depth, r)
        inv_u = 1.0 / jnp.sum(fresh, axis=0, keepdims=True)
        threes, pairs = [], []
        for h in range(per):
            part = fresh[h * w:(h + 1) * w]
            high, low = split(part)
            pairs.append(jnp.concatenate([high, low], axis=1))
            high, low = split(part.T)
            threes.append(other_three(high, low, 0))
        for g in range(jl // 2):
            total = jnp.zeros((2 * r, r), F32)
            for h in range(per):
                joint = mm(sl3[g], threes[h])
                i, k = 2 * g * per + h, (2 * g + 1) * per + h
                value = jnp.concatenate(
                    [right_v[:, i * w:(i + 1) * w], right_v[:, k * w:(k + 1) * w]], axis=0)
                qh, ql = split(value * inverse(joint))
                both = mm(qh, pairs[h])
                total += both[:, :r] + both[:, r:] + mm(ql, pairs[h][:, :r])
            result = slf[g] * (total * inv_u)
            outv[:, 2 * g, :] = result[:r]
            outv[:, 2 * g + 1, :] = result[r:]
    with scope("a2asend"):
        to_all(lambda to, slot: remote(outv.at[to], second_out.at[me], 7, to).start())
        own_out = pltpu.make_async_copy(outv.at[me], second_out.at[me], in_sem.at[1])
        own_out.start()
    with scope("ag3wait"):
        def finish(q):
            t, parts = blocks(q)

            @pl.when(q == 0)
            def _():
                wait(last.at[pl.ds(0, (xh * cols - 1) * mc)], recv_sem.at[LAST + t])

            @pl.when(q != 0)
            def _():
                wait(last.at[pl.ds(0, xh * cols * mc)], recv_sem.at[LAST + t])

            for part in parts:
                remote(last.at[part], left_out.at[part], LAST, partner, LASTF).start()
                pltpu.make_async_copy(last.at[part], left_out.at[part], in_sem.at[2]).start()

        loop(nt, finish)
    with scope("a2await"):
        own_out.wait()
        wait(second_out.at[pl.ds(0, d - 1)], recv_sem.at[7])
    with scope("ag3end"):
        wait(left_out.at[pl.ds(0, m // 2)], in_sem.at[2])
        wait(left_out.at[pl.ds(0, m // 2)], recv_sem.at[LASTF])
    with scope("sendwait"):
        wait(sleft_v.at[pl.ds(0, r - rr)], send_sem.at[0])
        wait(sright_v.at[pl.ds(0, cols - 1)], send_sem.at[1])
        wait(rc, send_sem.at[4])
        wait(sq, send_sem.at[4])
        wait(sright_new.at[pl.ds(0, d - 1)], send_sem.at[5])
        wait(second_out.at[pl.ds(0, d - 1)], send_sem.at[7])
        for turn, phase in ((0, 2), (1, 6)):
            wait(ra.at[turn, :, pl.ds(0, 10 - turn)], send_sem.at[phase])
            wait(ur.at[turn], send_sem.at[PAIR + turn])
            wait(pr.at[turn, pl.ds(0, half)], send_sem.at[PAIR + turn])
        wait(la.at[pl.ds(0, (half - 1) * mc)], send_sem.at[3])
        wait(la.at[pl.ds(0, half * mc)], send_sem.at[GATHER])
        wait(last.at[pl.ds(0, (half - 1) * mc)], send_sem.at[8])
        wait(last.at[pl.ds(0, half * mc)], send_sem.at[LAST])


def deliver(left, second, left_out, second_out, left_v, second_v, sem):
    ins = (pltpu.make_async_copy(left, left_v, sem.at[0]),
           pltpu.make_async_copy(second, second_v, sem.at[1]))
    outs = (pltpu.make_async_copy(left_v, left_out, sem.at[2]),
            pltpu.make_async_copy(second_v, second_out, sem.at[3]))
    for copy in ins:
        copy.start()
    for copy, out in zip(ins, outs):
        copy.wait()
        out.start()
    for out in outs:
        out.wait()


def solution(mesh):
    rows, cols = mesh.shape["row"], mesh.shape["col"]
    d = rows * cols

    def body(slab, left, right, sleft, sright):
        m, width = slab.shape
        r = left.shape[1]
        depth = sright.shape[1] * cols
        jl = width // depth
        w = depth // 2
        nb = width // w
        mc = m // d
        rt = m // TILES
        own_k = depth // d
        sleft = sleft.reshape(r // rows, d, jl, r)
        sright = sright.T.reshape(d // cols, own_k, r)
        hbm = pl.BlockSpec(memory_space=pl.ANY)
        left_out, second = pl.pallas_call(
            functools.partial(kernel, (rows, cols, m, r, w, jl, depth)),
            out_shape=(jax.ShapeDtypeStruct((m, r), F32),
                       jax.ShapeDtypeStruct((d, jl, r), F32)),
            in_specs=[hbm] * 5,
            out_specs=(hbm, hbm),
            scratch_shapes=[
                pltpu.VMEM((m, width), F32),
                pltpu.VMEM((m, r), F32),
                pltpu.VMEM((r, width), F32),
                pltpu.VMEM((nb, w, r), F32),
                pltpu.VMEM((r, jl, r), F32),
                pltpu.VMEM((cols, d // cols, own_k, r), F32),
                pltpu.VMEM((d, jl, r), F32),
                pltpu.VMEM((2 * rt, w), F32),
                pltpu.VMEM((TILES, rt, 2 * r), BF16),
                pltpu.VMEM((TILES, 2 * r, rt), BF16),
                pltpu.VMEM((nb, r, w), BF16),
                pltpu.VMEM((nb, w, 2 * r), BF16),
                pltpu.VMEM((nb, r, w), F32),
                pltpu.VMEM((r, 128), F32),
                pltpu.VMEM((8, r), F32),
                pltpu.VMEM((m, r), F32),
                pltpu.VMEM((mc, r), F32),
                pltpu.VMEM((mc, r), F32),
                pltpu.VMEM((m, r), F32),
                pltpu.VMEM((d // 2, own_k, r), F32),
                pltpu.VMEM((d // 2, own_k, r), F32),
                pltpu.VMEM((d // 2, own_k, r), F32),
                pltpu.VMEM((d // 2 - 1, own_k, r), F32),
                pltpu.VMEM((d, own_k, r), F32),
                pltpu.VMEM((own_k, r), F32),
                pltpu.VMEM((d, jl, r), F32),
                pltpu.VMEM((8, r), F32),
                pltpu.VMEM((jl // 2, 2 * r, 3 * r), BF16),
                pltpu.VMEM((jl // 2, 2 * r, 2 * r), BF16),
                pltpu.VMEM((jl // 2, 3 * r, 2 * r), BF16),
                pltpu.VMEM((2, jl // 2, w, 2 * r), F32),
                pltpu.VMEM((jl // 2, 2 * r, r), F32),
                pltpu.VMEM((2, 8, r), F32),
                pltpu.VMEM((2, 8, r), F32),
                pltpu.VMEM((2, d, mc, r), F32),
                pltpu.VMEM((2, d, mc, r), F32),
                pltpu.VMEM((2, d, 16, r), F32),
                pltpu.VMEM((2, d // 2 - 1, 16, r), F32),
                pltpu.SemaphoreType.DMA((nb,)),
                pltpu.SemaphoreType.DMA((5,)),
                pltpu.SemaphoreType.DMA((9 + 6 * TILES,)),
                pltpu.SemaphoreType.DMA((9 + 6 * TILES + 3,)),
            ],
            compiler_params=pltpu.CompilerParams(
                collective_id=0, has_side_effects=True, vmem_limit_bytes=60 * 1024 * 1024),
        )(slab, left, right, sleft, sright)
        second = second.reshape(d * jl, r)
        return pl.pallas_call(
            deliver,
            out_shape=(jax.ShapeDtypeStruct((m, r), F32),
                       jax.ShapeDtypeStruct((d * jl, r), F32)),
            in_specs=[hbm] * 2,
            out_specs=(hbm, hbm),
            scratch_shapes=[pltpu.VMEM((m, r), F32), pltpu.VMEM((d * jl, r), F32),
                            pltpu.SemaphoreType.DMA((4,))],
            compiler_params=pltpu.CompilerParams(vmem_limit_bytes=60 * 1024 * 1024),
        )(left_out, second)

    placed = (P(None, ("row", "col")), P(), P(None, ("row", "col")), P("row", None), P(None, "col"))
    return jax.shard_map(
        body, mesh=mesh, in_specs=placed, out_specs=(P(), P(("row", "col"), None)), check_vma=False
    )
```

```python
import contextlib
import functools

import jax
import jax.numpy as jnp
from jax import lax
from jax.experimental import pallas as pl
from jax.experimental.pallas import tpu as pltpu
from jax.sharding import PartitionSpec as P

F32 = jnp.float32
BF16 = jnp.bfloat16
NN = (((1,), (0,)), ((), ()))
NT = (((1,), (1,)), ((), ()))
TILES = 4
AHEAD = 1
CHUNK = 4
SCALE = 1.5
PIECES = 4


def scope(_):
    return contextlib.nullcontext()


def mm(a, b, dims=NN):
    return lax.dot_general(a, b, dims, preferred_element_type=F32)


def split(x):
    high = x.astype(BF16)
    low = (x - high.astype(F32)).astype(BF16)
    return high, low


def inverse(x):
    guess = pl.reciprocal(x, approx=True)
    return guess * (2.0 - x * guess)


def three(high, low, axis):
    return jnp.concatenate([high, high, low], axis=axis)


def other_three(high, low, axis):
    return jnp.concatenate([high, low, high], axis=axis)


def kernel(sizes, slab, left, right, sleft, sright, left_out, second_out, *scratch):
    (rows, cols, m, r, w, jl, depth) = sizes
    (slab_v, left_v, right_v, right_t, sleft_v, sright_v, c2_v, noise, left2, left_t, rd, rpair,
     nacc, csum, sums_v, la, lc, mult, last, sp, sq, sc, rc, sright_new, cb, outv, keep,
     sl3, slpair, slt3, inv2, slf, ub, ur, sa, pr, sm, ra,
     slab_sem, in_sem, send_sem, recv_sem) = scratch
    d = rows * cols
    nt = TILES
    rt = m // nt
    nb = rd.shape[0]
    mc = m // d
    dt = d // nt
    xh = dt // (2 * cols)
    own_k = depth // d
    per = depth // w
    rr = r // rows
    half = d // 2
    my_row, my_col = lax.axis_index("row"), lax.axis_index("col")
    me = my_row * cols + my_col
    my_z = lax.div(me, dt)
    my_in = lax.rem(me, dt)
    core = lax.rem(my_row, 2)
    my_x = lax.rem(lax.div(my_row, 2), xh)
    partner = me + cols * (1 - 2 * core)
    PAIR, GATHER, FORWARD, LAST, LASTF = 9, 9 + 2 * nt, 9 + 3 * nt, 9 + 4 * nt, 9 + 5 * nt

    def wait(ref, sem):
        pltpu.make_async_copy(ref, ref, sem).wait()

    def remote(src, dst, phase, to, recv=None):
        return pltpu.make_async_remote_copy(
            src, dst, send_sem.at[phase], recv_sem.at[phase if recv is None else recv],
            device_id=to, device_id_type=pl.DeviceIdType.LOGICAL)

    def near_first(q):
        return lax.rem(my_z + lax.div(q * (q + 1), 2), nt)

    def loop(n, body, start=0, unroll=1):
        def step(k, _):
            body(k)
            return 0

        lax.fori_loop(start, n, step, 0, unroll=unroll)

    def offset(z):
        oz = z - my_z
        return jnp.where(oz < 0, oz + nt, oz)

    def to_whole_plane(z, start, first):
        def one(k):
            i = my_in + k
            start(z * dt + jnp.where(i >= dt, i - dt, i), first + k)

        loop(dt, one, 1, dt - 1)

        @pl.when(z != my_z)
        def _():
            one(0)

    def to_all(start):
        def plane(q):
            z = near_first(nt - 1 - q)
            to_whole_plane(z, start, offset(z) * dt - 1)

        loop(nt, plane)

    def to_plane(z, start, first=0):
        for ox in range(xh):
            x = my_x + ox
            x = jnp.where(x >= xh, x - xh, x)
            base = z * dt + (x * 2 + core) * cols

            def one(k, base=base, ox=ox, x=x):
                c = my_col + k
                c = jnp.where(c >= cols, c - cols, c)
                start(base + c, first + ox * cols + k, (z * xh + x) * cols + c)

            if ox == 0:
                @pl.when(z != my_z)
                def _():
                    one(0)
                loop(cols, one, 1, cols - 1)
            else:
                loop(cols, one, 0, cols)

    with scope("start"):
        left_in = pltpu.make_async_copy(left, left_v, in_sem.at[0])
        left_in.start()
        right_in = pltpu.make_async_copy(right, right_v, in_sem.at[3])
        right_in.start()
        barrier = pltpu.get_barrier_semaphore()

        def greet(k):
            t = me + k
            pl.semaphore_signal(barrier, inc=1, device_id=jnp.where(t >= d, t - d, t),
                                device_id_type=pl.DeviceIdType.LOGICAL)

        for g in range(nt):
            for k in range(max(1, g * dt), (g + 1) * dt):
                greet(k)
            for i in range(g * nb // nt, (g + 1) * nb // nt):
                part = pl.ds(i * w, w)
                pltpu.make_async_copy(slab.at[:, part], slab_v.at[:, part], slab_sem.at[i]).start()
        own_sleft = pltpu.make_async_copy(
            sleft.at[:, me], sleft_v.at[pl.ds(my_row * rr, rr)], in_sem.at[1])
        own_sleft.start()
        own_sright = pltpu.make_async_copy(sright, sright_v.at[my_col], in_sem.at[2])
        own_sright.start()
        c2_in = pltpu.make_async_copy(sleft.at[my_col], c2_v, in_sem.at[4])
        c2_in.start()

    def prepare(source, t):
        value = source[pl.ds(t * rt, rt), :]
        high, low = split(value * (1.0 / SCALE))
        left2[t] = jnp.concatenate([high, low], axis=1)
        turned = value.T
        high, low = split(turned)
        left_t[t] = jnp.concatenate([high, low], axis=0)
        csum[...] += SCALE * jnp.broadcast_to(jnp.sum(turned, axis=1, keepdims=True), csum.shape)

    def dither(i, t):
        at = pl.multiple_of(8 * lax.rem(11 * i + 9 * t + 5 * me, rt // 8), 8)
        return noise[pl.ds(at, rt), :]

    def products(count, one):
        ahead = [one(i) for i in range(AHEAD)]
        for i in range(count):
            if i + AHEAD < count:
                ahead.append(one(i + AHEAD))
            yield i, ahead[i]

    def right_times(i):
        return jnp.concatenate([rd[i], rd[i]], axis=0)

    def new_right(i, total, inv_c):
        cut = pl.ds(i * w, w)
        new = right_v[:, cut] * (total * inv_c)
        right_v[:, cut] = new
        turned = new.T
        right_t[i] = turned
        return new, turned

    def rounded_right(i, new, turned):
        rd[i] = (new * dither(i, 1)[:r]).astype(BF16)
        high, low = split(turned)
        rpair[i] = jnp.concatenate([high, low], axis=1)
        sums_v[0:1] += SCALE * jnp.sum(turned, axis=0, keepdims=True)

    def right_blocks(first, count):
        for g in range(count):
            i = first + g
            wait(slab_v.at[:, pl.ds(0, w)], slab_sem.at[i])
        parts = []
        for n, joint in products(count * nt, lambda n: mm(left2[n % nt], right_times(first + n // nt))):
            i, t = first + n // nt, n % nt
            rows_t, cut = slice(t * rt, (t + 1) * rt), pl.ds(i * w, w)
            top = slab_v[rows_t, cut] * dither(i, t)
            slab_v[rows_t, cut] = top
            parts.append((top * inverse(joint)).astype(BF16))
            if t == nt - 1:
                both = mm(jnp.concatenate([left_t[k] for k in range(nt)], axis=1),
                          jnp.concatenate(parts, axis=0))
                parts = []
                nacc[i] = both[:r] + both[r:]

    def quotients(t):
        part = pl.ds(t * rt, rt)
        lhs = left2[t]
        for i, joint in products(nb, lambda i: mm(lhs, right_times(i))):
            yield i, (slab_v[part, i * w:(i + 1) * w] * inverse(joint)).astype(BF16)

    def right_tile(t, inv_c=None):
        turned = left_t[t]
        for i, quotient in quotients(t):
            both = mm(turned, quotient)
            total = nacc[i] + both[:r] + both[r:]
            if inv_c is None:
                nacc[i] = total
            else:
                new_right(i, total, inv_c)

    def left_tile(t, buffer):
        total = jnp.zeros((rt, r), F32)
        parts = []
        for i, quotient in quotients(t):
            parts.append(quotient)
            if len(parts) == CHUNK:
                both = mm(jnp.concatenate(parts, axis=1),
                          jnp.concatenate([rpair[k] for k in range(i + 1 - CHUNK, i + 1)], axis=0))
                total += both[:, :r] + both[:, r:]
                parts = []
        buffer[pl.ds(t * dt, dt)] = total.reshape(dt, mc, r)

    def left_part(t, c, buffer):
        size = cols * mc
        starts = [(x * 2 + c) * size for x in range(xh)]
        lhs = jnp.concatenate([left2[t, pl.ds(at, size), :] for at in starts], axis=0)
        total = jnp.zeros((xh * size, r), F32)
        parts = []
        for i, joint in products(nb, lambda i: mm(lhs, right_times(i))):
            cut = slice(i * w, (i + 1) * w)
            top = jnp.concatenate([slab_v[pl.ds(t * rt + at, size), cut] for at in starts], axis=0)
            parts.append((top * inverse(joint)).astype(BF16))
            if len(parts) == CHUNK:
                both = mm(jnp.concatenate(parts, axis=1),
                          jnp.concatenate([rpair[k] for k in range(i + 1 - CHUNK, i + 1)], axis=0))
                total += both[:, :r] + both[:, r:]
                parts = []
        for x in range(xh):
            buffer[pl.ds(group(t, x, c), cols)] = total[x * size:(x + 1) * size].reshape(cols, mc, r)

    def reset():
        nacc[...] = jnp.zeros_like(nacc)
        csum[...] = jnp.zeros_like(csum)
        sums_v[...] = jnp.zeros_like(sums_v)

    def group(z, x, c):
        return z * dt + (x * 2 + c) * cols

    def left_sums(turn, phase):
        mine, theirs, message, arrived = sa.at[turn], pr.at[turn], sm.at[turn], ra.at[turn]
        remote(ub.at[turn], ur.at[turn], PAIR + turn, partner, 9 + 6 * nt + turn).start()

        rows_sent = 10 - turn

        def combine(q):
            t = near_first(nt - 1 - q)
            wait(theirs.at[pl.ds(0, xh * cols)], recv_sem.at[PAIR + turn * nt + q])
            for x in range(xh):
                part = pl.ds(group(t, x, core), cols)
                message[part, 0:mc, :] = mine[part] + theirs[part]
                message[part, 8:16, :] = jnp.broadcast_to((ub[turn] + ur[turn])[None], (cols, 8, r))
            to_plane(t, lambda to, slot, _: remote(
                message.at[to, pl.ds(0, rows_sent)], arrived.at[slot, pl.ds(0, rows_sent)],
                phase, to).start(), offset(t) * (xh * cols) - 1)

        def exchange(q):
            for x in range(xh):
                part = pl.ds(group(near_first(nt - 1 - q), x, 1 - core), cols)
                remote(mine.at[part], theirs.at[part], PAIR + turn, partner,
                       PAIR + turn * nt + q).start()

        def tile(q):
            left_tile(near_first(nt - 1 - q), mine)
            exchange(q)

            @pl.when(q == 1)
            def _():
                wait(ur.at[turn], recv_sem.at[9 + 6 * nt + turn])

            @pl.when(q > 0)
            def _():
                combine(q - 1)

        loop(nt - 1, tile)
        left_part(my_z, 1 - core, mine)
        exchange(nt - 1)
        combine(nt - 2)
        left_part(my_z, core, mine)
        combine(nt - 1)

    def owned(turn, phase, old):
        wait(ra.at[turn, :, pl.ds(0, 10 - turn)], recv_sem.at[phase])
        own = sm[turn, me]
        numer = own[:mc] + jnp.sum(ra[turn, :, 0:mc, :], axis=0)
        tail = own[8:10 - turn] + jnp.sum(ra[turn, :, 8:10 - turn, :], axis=0)
        return old * numer / tail[0:1], tail

    with scope("prep"):
        reset()
        down = lax.broadcasted_iota(jnp.int32, noise.shape, 0).astype(F32)
        across = lax.broadcasted_iota(jnp.int32, noise.shape, 1).astype(F32)
        one = down * 0.7548776662 + across * 0.5698402910
        two = down * 0.6710436067 + across * 0.8191725134
        noise[...] = 1.0 + ((one - jnp.floor(one)) + (two - jnp.floor(two)) - 1.0) * (1.0 / 128)
        left_in.wait()

        loop(nt, lambda t: prepare(left_v, t))
        right_in.wait()
        for i in range(nb):
            rd[i] = (right_v[:, i * w:(i + 1) * w] * dither(i, 1)[:r]).astype(BF16)

    line = lax.broadcasted_iota(jnp.int32, (8, r), 0)
    with scope("right1"):
        inv_c = 1.0 / csum[:, 0:1]

        def finish_blocks(first):
            for i in (first, first + 1):
                rounded_right(i, *new_right(i, nacc[i], inv_c))

        right_blocks(0, 2)

        def two_blocks(g):
            right_blocks(2 * g, 2)
            finish_blocks(2 * g - 2)

        loop(nb // 2, two_blocks, 1)
        finish_blocks(nb - 2)
        c2_in.wait()
        part2 = jnp.sum(jnp.sum(c2_v[...], axis=0), axis=0, keepdims=True)
        ub[0] = jnp.where(line == 0, sums_v[0:1], part2)

    with scope("barrier"):
        pl.semaphore_wait(barrier, d - 1)

    with scope("sendin"):
        def send_sleft(k):
            t = lax.rem(my_row + k, rows) * cols + my_col
            remote(sleft.at[:, t], sleft_v.at[pl.ds(my_row * rr, rr)], 0, t).start()

        def send_sright(k):
            t = my_row * cols + lax.rem(my_col + k, cols)
            remote(sright, sright_v.at[my_col], 1, t).start()

    with scope("left1"):
        left_sums(0, 2)

    with scope("sendin"):
        loop(rows, send_sleft, 1)
        loop(cols, send_sright, 1)
        reset()

    with scope("rs1wait"):
        new, tail = owned(0, 2, left_v[pl.ds(me * mc, mc), :])
        keep[...] = jnp.broadcast_to(tail[1:2], (8, r))
        lc[...] = new
        la[pl.ds(me * mc, mc), :] = new
    with scope("ag1send"):
        def share(to, slot, _):
            remote(lc, la.at[pl.ds(me * mc, mc)], 3, to, GATHER + my_z).start()

        loop(nt, lambda q: to_plane(near_first(q), share))

    def blocks(q):
        t = near_first(q)
        return t, [pl.ds(group(t, x, core) * mc, cols * mc) for x in range(xh)]

    with scope("slprep"):
        own_sleft.wait()
        wait(sleft_v.at[pl.ds(0, r - rr)], recv_sem.at[0])
        own_sright.wait()
        wait(sright_v.at[pl.ds(0, cols - 1)], recv_sem.at[1])
        for g in range(jl // 2):
            two = jnp.concatenate([sleft_v[:, 2 * g, :], sleft_v[:, 2 * g + 1, :]], axis=0)
            slf[g] = two
            high, low = split(two)
            sl3[g] = three(high, low, 1)
            slpair[g] = jnp.concatenate([high, low], axis=1)
            high, low = split(two.T)
            slt3[g] = other_three(high, low, 0)
        for h in range(per):
            high, low = split(sright_v[pl.ds(h * (cols // per), cols // per)].reshape(w, r))
            lhs = three(high, low, 1)
            for g in range(jl // 2):
                inv2[h, g] = inverse(mm(lhs, slt3[g]))

    with scope("right2"):
        def forward(q):
            t, parts = blocks(q)

            @pl.when(q == 0)
            def _():
                wait(la.at[pl.ds(0, (xh * cols - 1) * mc)], recv_sem.at[GATHER + t])

            @pl.when(q != 0)
            def _():
                wait(la.at[pl.ds(0, xh * cols * mc)], recv_sem.at[GATHER + t])

            for part in parts:
                remote(la.at[part], la.at[part], GATHER, partner, FORWARD + q).start()

        forward(0)

        def second(q):
            t = near_first(q)
            wait(la.at[pl.ds(0, xh * cols * mc)], recv_sem.at[FORWARD + q])
            prepare(la, t)
            right_tile(t)

            @pl.when(q == 0)
            def _():
                for k in range(1, nt):
                    forward(k)

        loop(nt - 1, second)
        t = near_first(nt - 1)
        wait(la.at[pl.ds(0, xh * cols * mc)], recv_sem.at[FORWARD + nt - 1])
        prepare(la, t)
        right_tile(t, 1.0 / csum[:, 0:1])

    chip = (my_z * xh + my_x) * cols + my_col
    mine_k = core * half + chip
    with scope("numer2"):
        def half_numer(h):
            total = jnp.zeros((w, r), F32)
            for g in range(jl // 2):
                value = jnp.concatenate(
                    [right_t[2 * g * per + h], right_t[(2 * g + 1) * per + h]], axis=1)
                qh, ql = split(value * inv2[h, g])
                both = mm(qh, slpair[g])
                total += both[:, :r] + both[:, r:] + mm(ql, slpair[g, :, :r])
            return total.reshape(half, own_k, r)

        sp[...] = half_numer(1 - core)
        remote(sp, sq, 4, partner, 9 + 6 * nt + 2).start()
        own2 = half_numer(core)
        wait(sq, recv_sem.at[9 + 6 * nt + 2])
        sc[...] = own2 + sq[...]
    with scope("rs2send"):
        def rs2(q):
            z = near_first(nt - 1 - q)
            to_plane(z, lambda to, slot, at: remote(sc.at[at], rc.at[slot], 4, to).start(),
                     offset(z) * (xh * cols) - 1)

        loop(nt, rs2)

    with scope("left2"):
        for i in range(nb):
            rounded_right(i, right_v[:, i * w:(i + 1) * w], right_t[i])
        ub[1] = jnp.broadcast_to(sums_v[0:1], (8, r))
        left_sums(1, 6)

    with scope("rs2wait"):
        wait(rc, recv_sem.at[4])
    with scope("rs2sum"):
        numer = sc[chip] + jnp.sum(rc[...], axis=0)
        cb[...] = (sright_v[lax.div(mine_k, d // cols), lax.rem(mine_k, d // cols)]
                   * numer / keep[0:1])
        sright_new[mine_k] = cb[...]
    with scope("ag2send"):
        def ag2(q):
            to_plane(near_first(nt - 1 - q), lambda to, slot, _: remote(
                cb, sright_new.at[mine_k], 5, to).start())

        loop(nt, ag2)
    with scope("rs3wait"):
        new, _ = owned(1, 6, la[pl.ds(me * mc, mc), :])
        mult[...] = new
        last[pl.ds(me * mc, mc), :] = new
    with scope("ag3send"):
        def ag3(q):
            to_plane(near_first(q), lambda to, slot, _: remote(
                mult, last.at[pl.ds(me * mc, mc)], 8, to, LAST + my_z).start())

        loop(nt, ag3)
    with scope("ag2wait"):
        wait(sright_new.at[pl.ds(0, half - 1)], recv_sem.at[5])
        part = pl.ds(core * half, half)
        remote(sright_new.at[part], sright_new.at[part], 10, partner, 9 + 6 * nt + 3).start()
    with scope("left3"):
        sums = jnp.zeros((1, r), F32)
        totals = [jnp.zeros((2 * r, r), F32) for _ in range(jl // 2)]
        for h in (core, 1 - core):
            if h is not core:
                wait(sright_new.at[pl.ds(0, half)], recv_sem.at[9 + 6 * nt + 3])
            part = sright_new[pl.ds(h * half, half)].reshape(w, r)
            sums += jnp.sum(part, axis=0, keepdims=True)
            high, low = split(part)
            pair = jnp.concatenate([high, low], axis=1)
            high, low = split(part.T)
            triple = other_three(high, low, 0)
            for g in range(jl // 2):
                joint = mm(sl3[g], triple)
                value = jnp.concatenate(
                    [right_v[:, pl.ds(pl.multiple_of((k * per + h) * w, w), w)]
                     for k in (2 * g, 2 * g + 1)], axis=0)
                qh, ql = split(value * inverse(joint))
                both = mm(qh, pair)
                totals[g] += both[:, :r] + both[:, r:] + mm(ql, pair[:, :r])
        inv_u = 1.0 / sums
        for g in range(jl // 2):
            result = slf[g] * (totals[g] * inv_u)
            outv[:, 2 * g, :] = result[:r]
            outv[:, 2 * g + 1, :] = result[r:]
    with scope("a2asend"):
        to_all(lambda to, slot: remote(outv.at[to], second_out.at[me], 7, to).start())
        own_out = pltpu.make_async_copy(outv.at[me], second_out.at[me], in_sem.at[1])
        own_out.start()
    with scope("ag3wait"):
        def finish(q):
            t, parts = blocks(q)

            @pl.when(q == 0)
            def _():
                wait(last.at[pl.ds(0, (xh * cols - 1) * mc)], recv_sem.at[LAST + t])

            @pl.when(q != 0)
            def _():
                wait(last.at[pl.ds(0, xh * cols * mc)], recv_sem.at[LAST + t])

            for part in parts:
                remote(last.at[part], left_out.at[part], LAST, partner, LASTF).start()
                pltpu.make_async_copy(last.at[part], left_out.at[part], in_sem.at[2]).start()

        loop(nt, finish)
    with scope("a2await"):
        own_out.wait()
        wait(second_out.at[pl.ds(0, d - 1)], recv_sem.at[7])
    with scope("ag3end"):
        wait(left_out.at[pl.ds(0, m // 2)], in_sem.at[2])
        wait(left_out.at[pl.ds(0, m // 2)], recv_sem.at[LASTF])
    with scope("sendwait"):
        wait(sleft_v.at[pl.ds(0, r - rr)], send_sem.at[0])
        wait(sright_v.at[pl.ds(0, cols - 1)], send_sem.at[1])
        wait(rc, send_sem.at[4])
        wait(sq, send_sem.at[4])
        wait(sright_new.at[pl.ds(0, half - 1)], send_sem.at[5])
        wait(sright_new.at[pl.ds(0, half)], send_sem.at[10])
        wait(second_out.at[pl.ds(0, d - 1)], send_sem.at[7])
        for turn, phase in ((0, 2), (1, 6)):
            wait(ra.at[turn, :, pl.ds(0, 10 - turn)], send_sem.at[phase])
            wait(ur.at[turn], send_sem.at[PAIR + turn])
            wait(pr.at[turn, pl.ds(0, half)], send_sem.at[PAIR + turn])
        wait(la.at[pl.ds(0, (half - 1) * mc)], send_sem.at[3])
        wait(la.at[pl.ds(0, half * mc)], send_sem.at[GATHER])
        wait(last.at[pl.ds(0, (half - 1) * mc)], send_sem.at[8])
        wait(last.at[pl.ds(0, half * mc)], send_sem.at[LAST])


def deliver(left, second, left_out, second_out, left_v, second_v, sem):
    n = left.shape[0] // PIECES
    moves = [(left.at[pl.ds(i * n, n)], left_v.at[pl.ds(i * n, n)], left_out.at[pl.ds(i * n, n)])
             for i in range(PIECES)] + [(second, second_v, second_out)]
    ins = [pltpu.make_async_copy(a, b, sem.at[0, i]) for i, (a, b, _) in enumerate(moves)]
    outs = [pltpu.make_async_copy(b, c, sem.at[1, i]) for i, (_, b, c) in enumerate(moves)]
    for copy in ins:
        copy.start()
    for copy, out in zip(ins, outs):
        copy.wait()
        out.start()
    for out in outs:
        out.wait()


def solution(mesh):
    rows, cols = mesh.shape["row"], mesh.shape["col"]
    d = rows * cols

    def body(slab, left, right, sleft, sright):
        m, width = slab.shape
        r = left.shape[1]
        depth = sright.shape[1] * cols
        jl = width // depth
        w = depth // 2
        nb = width // w
        mc = m // d
        rt = m // TILES
        own_k = depth // d
        sleft = sleft.reshape(r // rows, d, jl, r)
        sright = sright.T.reshape(d // cols, own_k, r)
        hbm = pl.BlockSpec(memory_space=pl.ANY)
        left_out, second = pl.pallas_call(
            functools.partial(kernel, (rows, cols, m, r, w, jl, depth)),
            out_shape=(jax.ShapeDtypeStruct((m, r), F32),
                       jax.ShapeDtypeStruct((d, jl, r), F32)),
            in_specs=[hbm] * 5,
            out_specs=(hbm, hbm),
            scratch_shapes=[
                pltpu.VMEM((m, width), F32),
                pltpu.VMEM((m, r), F32),
                pltpu.VMEM((r, width), F32),
                pltpu.VMEM((nb, w, r), F32),
                pltpu.VMEM((r, jl, r), F32),
                pltpu.VMEM((cols, d // cols, own_k, r), F32),
                pltpu.VMEM((d, jl, r), F32),
                pltpu.VMEM((2 * rt, w), F32),
                pltpu.VMEM((TILES, rt, 2 * r), BF16),
                pltpu.VMEM((TILES, 2 * r, rt), BF16),
                pltpu.VMEM((nb, r, w), BF16),
                pltpu.VMEM((nb, w, 2 * r), BF16),
                pltpu.VMEM((nb, r, w), F32),
                pltpu.VMEM((r, 128), F32),
                pltpu.VMEM((8, r), F32),
                pltpu.VMEM((m, r), F32),
                pltpu.VMEM((mc, r), F32),
                pltpu.VMEM((mc, r), F32),
                pltpu.VMEM((m, r), F32),
                pltpu.VMEM((d // 2, own_k, r), F32),
                pltpu.VMEM((d // 2, own_k, r), F32),
                pltpu.VMEM((d // 2, own_k, r), F32),
                pltpu.VMEM((d // 2 - 1, own_k, r), F32),
                pltpu.VMEM((d, own_k, r), F32),
                pltpu.VMEM((own_k, r), F32),
                pltpu.VMEM((d, jl, r), F32),
                pltpu.VMEM((8, r), F32),
                pltpu.VMEM((jl // 2, 2 * r, 3 * r), BF16),
                pltpu.VMEM((jl // 2, 2 * r, 2 * r), BF16),
                pltpu.VMEM((jl // 2, 3 * r, 2 * r), BF16),
                pltpu.VMEM((2, jl // 2, w, 2 * r), F32),
                pltpu.VMEM((jl // 2, 2 * r, r), F32),
                pltpu.VMEM((2, 8, r), F32),
                pltpu.VMEM((2, 8, r), F32),
                pltpu.VMEM((2, d, mc, r), F32),
                pltpu.VMEM((2, d, mc, r), F32),
                pltpu.VMEM((2, d, 16, r), F32),
                pltpu.VMEM((2, d // 2 - 1, 16, r), F32),
                pltpu.SemaphoreType.DMA((nb,)),
                pltpu.SemaphoreType.DMA((5,)),
                pltpu.SemaphoreType.DMA((9 + 6 * TILES,)),
                pltpu.SemaphoreType.DMA((9 + 6 * TILES + 4,)),
            ],
            compiler_params=pltpu.CompilerParams(
                collective_id=0, has_side_effects=True, vmem_limit_bytes=60 * 1024 * 1024),
        )(slab, left, right, sleft, sright)
        second = second.reshape(d * jl, r)
        return pl.pallas_call(
            deliver,
            out_shape=(jax.ShapeDtypeStruct((m, r), F32),
                       jax.ShapeDtypeStruct((d * jl, r), F32)),
            in_specs=[hbm] * 2,
            out_specs=(hbm, hbm),
            scratch_shapes=[pltpu.VMEM((m, r), F32), pltpu.VMEM((d * jl, r), F32),
                            pltpu.SemaphoreType.DMA((2, PIECES + 1))],
            compiler_params=pltpu.CompilerParams(vmem_limit_bytes=60 * 1024 * 1024),
        )(left_out, second)

    placed = (P(None, ("row", "col")), P(), P(None, ("row", "col")), P("row", None), P(None, "col"))
    return jax.shard_map(
        body, mesh=mesh, in_specs=placed, out_specs=(P(), P(("row", "col"), None)), check_vma=False
    )
```

```python
import contextlib
import functools

import jax
import jax.numpy as jnp
from jax import lax
from jax.experimental import pallas as pl
from jax.experimental.pallas import tpu as pltpu
from jax.sharding import PartitionSpec as P

F32 = jnp.float32
BF16 = jnp.bfloat16
NN = (((1,), (0,)), ((), ()))
NT = (((1,), (1,)), ((), ()))
TILES = 4
AHEAD = 1
CHUNK = 4
SCALE = 1.5
LIMIT = 40 * 1024 * 1024


def scope(_):
    return contextlib.nullcontext()


def mm(a, b, dims=NN):
    return lax.dot_general(a, b, dims, preferred_element_type=F32)


def split(x):
    high = x.astype(BF16)
    low = (x - high.astype(F32)).astype(BF16)
    return high, low


def inverse(x):
    guess = pl.reciprocal(x, approx=True)
    return guess * (2.0 - x * guess)


def three(high, low, axis):
    return jnp.concatenate([high, high, low], axis=axis)


def other_three(high, low, axis):
    return jnp.concatenate([high, low, high], axis=axis)


def kernel(sizes, slab, left, right, sleft, sright, left_out, second_out, *scratch):
    (rows, cols, m, r, w, jl, depth) = sizes
    (slab_v, left_v, right_v, right_t, sleft_v, sright_v, c2_v, noise, left2, left_t, rd, rpair,
     nacc, csum, sums_v, la, lc, mult, last, sp, sq, sc, rc, sright_new, cb, outv, keep,
     sl3, slpair, slt3, inv2, slf, ub, ur, sa, pr, sm, ra,
     slab_sem, in_sem, send_sem, recv_sem) = scratch
    d = rows * cols
    nt = TILES
    rt = m // nt
    nb = rd.shape[0]
    mc = m // d
    dt = d // nt
    xh = dt // (2 * cols)
    own_k = depth // d
    per = depth // w
    rr = r // rows
    half = d // 2
    my_row, my_col = lax.axis_index("row"), lax.axis_index("col")
    me = my_row * cols + my_col
    my_z = lax.div(me, dt)
    my_in = lax.rem(me, dt)
    core = lax.rem(my_row, 2)
    my_x = lax.rem(lax.div(my_row, 2), xh)
    partner = me + cols * (1 - 2 * core)
    PAIR, GATHER, FORWARD, LAST, LASTF = 9, 9 + 2 * nt, 9 + 3 * nt, 9 + 4 * nt, 9 + 5 * nt

    def wait(ref, sem):
        pltpu.make_async_copy(ref, ref, sem).wait()

    def remote(src, dst, phase, to, recv=None):
        return pltpu.make_async_remote_copy(
            src, dst, send_sem.at[phase], recv_sem.at[phase if recv is None else recv],
            device_id=to, device_id_type=pl.DeviceIdType.LOGICAL)

    def near_first(q):
        return lax.rem(my_z + lax.div(q * (q + 1), 2), nt)

    def loop(n, body, start=0, unroll=1):
        def step(k, _):
            body(k)
            return 0

        lax.fori_loop(start, n, step, 0, unroll=unroll)

    def offset(z):
        oz = z - my_z
        return jnp.where(oz < 0, oz + nt, oz)

    def to_whole_plane(z, start, first):
        def one(k):
            i = my_in + k
            start(z * dt + jnp.where(i >= dt, i - dt, i), first + k)

        loop(dt, one, 1, dt - 1)

        @pl.when(z != my_z)
        def _():
            one(0)

    def to_all(start):
        def plane(q):
            z = near_first(nt - 1 - q)
            to_whole_plane(z, start, offset(z) * dt - 1)

        loop(nt, plane)

    def to_plane(z, start, first=0):
        for ox in range(xh):
            x = my_x + ox
            x = jnp.where(x >= xh, x - xh, x)
            base = z * dt + (x * 2 + core) * cols

            def one(k, base=base, ox=ox, x=x):
                c = my_col + k
                c = jnp.where(c >= cols, c - cols, c)
                start(base + c, first + ox * cols + k, (z * xh + x) * cols + c)

            if ox == 0:
                @pl.when(z != my_z)
                def _():
                    one(0)
                loop(cols, one, 1, cols - 1)
            else:
                loop(cols, one, 0, cols)

    with scope("start"):
        left_in = pltpu.make_async_copy(left, left_v, in_sem.at[0])
        left_in.start()
        right_in = pltpu.make_async_copy(right, right_v, in_sem.at[3])
        right_in.start()
        barrier = pltpu.get_barrier_semaphore()

        def greet(k):
            t = me + k
            pl.semaphore_signal(barrier, inc=1, device_id=jnp.where(t >= d, t - d, t),
                                device_id_type=pl.DeviceIdType.LOGICAL)

        for g in range(nt):
            for k in range(max(1, g * dt), (g + 1) * dt):
                greet(k)
            for i in range(g * nb // nt, (g + 1) * nb // nt):
                part = pl.ds(i * w, w)
                pltpu.make_async_copy(slab.at[:, part], slab_v.at[:, part], slab_sem.at[i]).start()
        own_sleft = pltpu.make_async_copy(
            sleft.at[:, me], sleft_v.at[pl.ds(my_row * rr, rr)], in_sem.at[1])
        own_sleft.start()
        own_sright = pltpu.make_async_copy(sright, sright_v.at[my_col], in_sem.at[2])
        own_sright.start()
        c2_in = pltpu.make_async_copy(sleft.at[my_col], c2_v, in_sem.at[4])
        c2_in.start()

    def prepare(source, t):
        value = source[pl.ds(t * rt, rt), :]
        high, low = split(value * (1.0 / SCALE))
        left2[t] = jnp.concatenate([high, low], axis=1)
        turned = value.T
        high, low = split(turned)
        left_t[t] = jnp.concatenate([high, low], axis=0)
        csum[...] += SCALE * jnp.broadcast_to(jnp.sum(turned, axis=1, keepdims=True), csum.shape)

    def dither(i, t):
        at = pl.multiple_of(8 * lax.rem(11 * i + 9 * t + 5 * me, rt // 8), 8)
        return noise[pl.ds(at, rt), :]

    def products(count, one):
        ahead = [one(i) for i in range(AHEAD)]
        for i in range(count):
            if i + AHEAD < count:
                ahead.append(one(i + AHEAD))
            yield i, ahead[i]

    def right_times(i):
        return jnp.concatenate([rd[i], rd[i]], axis=0)

    def new_right(i, total, inv_c):
        cut = pl.ds(i * w, w)
        new = right_v[:, cut] * (total * inv_c)
        right_v[:, cut] = new
        turned = new.T
        right_t[i] = turned
        return new, turned

    def rounded_right(i, new, turned):
        rd[i] = (new * dither(i, 1)[:r]).astype(BF16)
        high, low = split(turned)
        rpair[i] = jnp.concatenate([high, low], axis=1)
        sums_v[0:1] += SCALE * jnp.sum(turned, axis=0, keepdims=True)

    def right_blocks(first, count):
        for g in range(count):
            i = first + g
            wait(slab_v.at[:, pl.ds(0, w)], slab_sem.at[i])
        parts = []
        for n, joint in products(count * nt, lambda n: mm(left2[n % nt], right_times(first + n // nt))):
            i, t = first + n // nt, n % nt
            rows_t, cut = slice(t * rt, (t + 1) * rt), pl.ds(i * w, w)
            top = slab_v[rows_t, cut] * dither(i, t)
            slab_v[rows_t, cut] = top
            parts.append((top * inverse(joint)).astype(BF16))
            if t == nt - 1:
                both = mm(jnp.concatenate([left_t[k] for k in range(nt)], axis=1),
                          jnp.concatenate(parts, axis=0))
                parts = []
                nacc[i] = both[:r] + both[r:]

    def quotients(t):
        part = pl.ds(t * rt, rt)
        lhs = left2[t]
        for i, joint in products(nb, lambda i: mm(lhs, right_times(i))):
            yield i, (slab_v[part, i * w:(i + 1) * w] * inverse(joint)).astype(BF16)

    def right_tile(t, inv_c=None):
        turned = left_t[t]
        for i, quotient in quotients(t):
            both = mm(turned, quotient)
            total = nacc[i] + both[:r] + both[r:]
            if inv_c is None:
                nacc[i] = total
            else:
                new_right(i, total, inv_c)

    def left_tile(t, buffer):
        total = jnp.zeros((rt, r), F32)
        parts = []
        for i, quotient in quotients(t):
            parts.append(quotient)
            if len(parts) == CHUNK:
                both = mm(jnp.concatenate(parts, axis=1),
                          jnp.concatenate([rpair[k] for k in range(i + 1 - CHUNK, i + 1)], axis=0))
                total += both[:, :r] + both[:, r:]
                parts = []
        buffer[pl.ds(t * dt, dt)] = total.reshape(dt, mc, r)

    def left_part(t, c, buffer):
        size = cols * mc
        starts = [(x * 2 + c) * size for x in range(xh)]
        lhs = jnp.concatenate([left2[t, pl.ds(at, size), :] for at in starts], axis=0)
        total = jnp.zeros((xh * size, r), F32)
        parts = []
        for i, joint in products(nb, lambda i: mm(lhs, right_times(i))):
            cut = slice(i * w, (i + 1) * w)
            top = jnp.concatenate([slab_v[pl.ds(t * rt + at, size), cut] for at in starts], axis=0)
            parts.append((top * inverse(joint)).astype(BF16))
            if len(parts) == CHUNK:
                both = mm(jnp.concatenate(parts, axis=1),
                          jnp.concatenate([rpair[k] for k in range(i + 1 - CHUNK, i + 1)], axis=0))
                total += both[:, :r] + both[:, r:]
                parts = []
        for x in range(xh):
            buffer[pl.ds(group(t, x, c), cols)] = total[x * size:(x + 1) * size].reshape(cols, mc, r)

    def reset():
        nacc[...] = jnp.zeros_like(nacc)
        csum[...] = jnp.zeros_like(csum)
        sums_v[...] = jnp.zeros_like(sums_v)

    def group(z, x, c):
        return z * dt + (x * 2 + c) * cols

    def left_sums(turn, phase):
        mine, theirs, message, arrived = sa.at[turn], pr.at[turn], sm.at[turn], ra.at[turn]
        remote(ub.at[turn], ur.at[turn], PAIR + turn, partner, 9 + 6 * nt + turn).start()

        rows_sent = 10 - turn

        def combine(q):
            t = near_first(nt - 1 - q)
            wait(theirs.at[pl.ds(0, xh * cols)], recv_sem.at[PAIR + turn * nt + q])
            for x in range(xh):
                part = pl.ds(group(t, x, core), cols)
                message[part, 0:mc, :] = mine[part] + theirs[part]
                message[part, 8:16, :] = jnp.broadcast_to((ub[turn] + ur[turn])[None], (cols, 8, r))
            to_plane(t, lambda to, slot, _: remote(
                message.at[to, pl.ds(0, rows_sent)], arrived.at[slot, pl.ds(0, rows_sent)],
                phase, to).start(), offset(t) * (xh * cols) - 1)

        def exchange(q):
            for x in range(xh):
                part = pl.ds(group(near_first(nt - 1 - q), x, 1 - core), cols)
                remote(mine.at[part], theirs.at[part], PAIR + turn, partner,
                       PAIR + turn * nt + q).start()

        def tile(q):
            left_tile(near_first(nt - 1 - q), mine)
            exchange(q)

            @pl.when(q == 1)
            def _():
                wait(ur.at[turn], recv_sem.at[9 + 6 * nt + turn])

            @pl.when(q > 0)
            def _():
                combine(q - 1)

        loop(nt - 1, tile)
        left_part(my_z, 1 - core, mine)
        exchange(nt - 1)
        combine(nt - 2)
        left_part(my_z, core, mine)
        combine(nt - 1)

    def owned(turn, phase, old):
        wait(ra.at[turn, :, pl.ds(0, 10 - turn)], recv_sem.at[phase])
        own = sm[turn, me]
        numer = own[:mc] + jnp.sum(ra[turn, :, 0:mc, :], axis=0)
        tail = own[8:10 - turn] + jnp.sum(ra[turn, :, 8:10 - turn, :], axis=0)
        return old * numer / tail[0:1], tail

    with scope("prep"):
        reset()
        down = lax.broadcasted_iota(jnp.int32, noise.shape, 0).astype(F32)
        across = lax.broadcasted_iota(jnp.int32, noise.shape, 1).astype(F32)
        one = down * 0.7548776662 + across * 0.5698402910
        two = down * 0.6710436067 + across * 0.8191725134
        noise[...] = 1.0 + ((one - jnp.floor(one)) + (two - jnp.floor(two)) - 1.0) * (1.0 / 128)
        left_in.wait()

        loop(nt, lambda t: prepare(left_v, t))
        right_in.wait()
        for i in range(nb):
            rd[i] = (right_v[:, i * w:(i + 1) * w] * dither(i, 1)[:r]).astype(BF16)

    line = lax.broadcasted_iota(jnp.int32, (8, r), 0)
    with scope("right1"):
        inv_c = 1.0 / csum[:, 0:1]

        def finish_blocks(first):
            for i in (first, first + 1):
                rounded_right(i, *new_right(i, nacc[i], inv_c))

        right_blocks(0, 2)

        def two_blocks(g):
            right_blocks(2 * g, 2)
            finish_blocks(2 * g - 2)

        loop(nb // 2, two_blocks, 1)
        finish_blocks(nb - 2)
        c2_in.wait()
        part2 = jnp.sum(jnp.sum(c2_v[...], axis=0), axis=0, keepdims=True)
        ub[0] = jnp.where(line == 0, sums_v[0:1], part2)

    with scope("barrier"):
        pl.semaphore_wait(barrier, d - 1)

    with scope("sendin"):
        def send_sleft(k):
            t = lax.rem(my_row + k, rows) * cols + my_col
            remote(sleft.at[:, t], sleft_v.at[pl.ds(my_row * rr, rr)], 0, t).start()

        def send_sright(k):
            t = my_row * cols + lax.rem(my_col + k, cols)
            remote(sright, sright_v.at[my_col], 1, t).start()

    with scope("left1"):
        left_sums(0, 2)

    with scope("sendin"):
        loop(rows, send_sleft, 1)
        loop(cols, send_sright, 1)
        reset()

    with scope("rs1wait"):
        new, tail = owned(0, 2, left_v[pl.ds(me * mc, mc), :])
        keep[...] = jnp.broadcast_to(tail[1:2], (8, r))
        lc[...] = new
        la[pl.ds(me * mc, mc), :] = new
    with scope("ag1send"):
        def share(to, slot, _):
            remote(lc, la.at[pl.ds(me * mc, mc)], 3, to, GATHER + my_z).start()

        loop(nt, lambda q: to_plane(near_first(q), share))

    def blocks(q):
        t = near_first(q)
        return t, [pl.ds(group(t, x, core) * mc, cols * mc) for x in range(xh)]

    with scope("slprep"):
        own_sleft.wait()
        wait(sleft_v.at[pl.ds(0, r - rr)], recv_sem.at[0])
        own_sright.wait()
        wait(sright_v.at[pl.ds(0, cols - 1)], recv_sem.at[1])
        for g in range(jl // 2):
            two = jnp.concatenate([sleft_v[:, 2 * g, :], sleft_v[:, 2 * g + 1, :]], axis=0)
            slf[g] = two
            high, low = split(two)
            sl3[g] = three(high, low, 1)
            slpair[g] = jnp.concatenate([high, low], axis=1)
            high, low = split(two.T)
            slt3[g] = other_three(high, low, 0)
        for h in range(per):
            high, low = split(sright_v[pl.ds(h * (cols // per), cols // per)].reshape(w, r))
            lhs = three(high, low, 1)
            for g in range(jl // 2):
                inv2[h, g] = inverse(mm(lhs, slt3[g]))

    with scope("right2"):
        def forward(q):
            t, parts = blocks(q)

            @pl.when(q == 0)
            def _():
                wait(la.at[pl.ds(0, (xh * cols - 1) * mc)], recv_sem.at[GATHER + t])

            @pl.when(q != 0)
            def _():
                wait(la.at[pl.ds(0, xh * cols * mc)], recv_sem.at[GATHER + t])

            for part in parts:
                remote(la.at[part], la.at[part], GATHER, partner, FORWARD + q).start()

        forward(0)

        def second(q):
            t = near_first(q)
            wait(la.at[pl.ds(0, xh * cols * mc)], recv_sem.at[FORWARD + q])
            prepare(la, t)
            right_tile(t)

            @pl.when(q == 0)
            def _():
                for k in range(1, nt):
                    forward(k)

        loop(nt - 1, second)
        t = near_first(nt - 1)
        wait(la.at[pl.ds(0, xh * cols * mc)], recv_sem.at[FORWARD + nt - 1])
        prepare(la, t)
        right_tile(t, 1.0 / csum[:, 0:1])

    chip = (my_z * xh + my_x) * cols + my_col
    mine_k = core * half + chip
    with scope("numer2"):
        def half_numer(h):
            total = jnp.zeros((w, r), F32)
            for g in range(jl // 2):
                value = jnp.concatenate(
                    [right_t[2 * g * per + h], right_t[(2 * g + 1) * per + h]], axis=1)
                qh, ql = split(value * inv2[h, g])
                both = mm(qh, slpair[g])
                total += both[:, :r] + both[:, r:] + mm(ql, slpair[g, :, :r])
            return total.reshape(half, own_k, r)

        sp[...] = half_numer(1 - core)
        remote(sp, sq, 4, partner, 9 + 6 * nt + 2).start()
        own2 = half_numer(core)
        wait(sq, recv_sem.at[9 + 6 * nt + 2])
        sc[...] = own2 + sq[...]
    with scope("rs2send"):
        def rs2(q):
            z = near_first(nt - 1 - q)
            to_plane(z, lambda to, slot, at: remote(sc.at[at], rc.at[slot], 4, to).start(),
                     offset(z) * (xh * cols) - 1)

        loop(nt, rs2)

    with scope("left2"):
        for i in range(nb):
            rounded_right(i, right_v[:, i * w:(i + 1) * w], right_t[i])
        ub[1] = jnp.broadcast_to(sums_v[0:1], (8, r))
        left_sums(1, 6)

    with scope("rs2wait"):
        wait(rc, recv_sem.at[4])
    with scope("rs2sum"):
        numer = sc[chip] + jnp.sum(rc[...], axis=0)
        cb[...] = (sright_v[lax.div(mine_k, d // cols), lax.rem(mine_k, d // cols)]
                   * numer / keep[0:1])
        sright_new[mine_k] = cb[...]
    with scope("ag2send"):
        def ag2(q):
            to_plane(near_first(nt - 1 - q), lambda to, slot, _: remote(
                cb, sright_new.at[mine_k], 5, to).start())

        loop(nt, ag2)
    with scope("rs3wait"):
        new, _ = owned(1, 6, la[pl.ds(me * mc, mc), :])
        mult[...] = new
        last[pl.ds(me * mc, mc), :] = new
    with scope("ag3send"):
        def ag3(q):
            to_plane(near_first(q), lambda to, slot, _: remote(
                mult, last.at[pl.ds(me * mc, mc)], 8, to, LAST + my_z).start())

        loop(nt, ag3)
    with scope("ag2wait"):
        wait(sright_new.at[pl.ds(0, half - 1)], recv_sem.at[5])
        part = pl.ds(core * half, half)
        remote(sright_new.at[part], sright_new.at[part], 10, partner, 9 + 6 * nt + 3).start()
    with scope("left3"):
        sums = jnp.zeros((1, r), F32)
        totals = [jnp.zeros((2 * r, r), F32) for _ in range(jl // 2)]
        for h in (core, 1 - core):
            if h is not core:
                wait(sright_new.at[pl.ds(0, half)], recv_sem.at[9 + 6 * nt + 3])
            part = sright_new[pl.ds(h * half, half)].reshape(w, r)
            sums += jnp.sum(part, axis=0, keepdims=True)
            high, low = split(part)
            pair = jnp.concatenate([high, low], axis=1)
            high, low = split(part.T)
            triple = other_three(high, low, 0)
            for g in range(jl // 2):
                joint = mm(sl3[g], triple)
                value = jnp.concatenate(
                    [right_v[:, pl.ds(pl.multiple_of((k * per + h) * w, w), w)]
                     for k in (2 * g, 2 * g + 1)], axis=0)
                qh, ql = split(value * inverse(joint))
                both = mm(qh, pair)
                totals[g] += both[:, :r] + both[:, r:] + mm(ql, pair[:, :r])
        inv_u = 1.0 / sums
        for g in range(jl // 2):
            result = slf[g] * (totals[g] * inv_u)
            outv[:, 2 * g, :] = result[:r]
            outv[:, 2 * g + 1, :] = result[r:]
    with scope("a2asend"):
        to_all(lambda to, slot: remote(outv.at[to], second_out.at[me], 7, to).start())
        own_out = pltpu.make_async_copy(outv.at[me], second_out.at[me], in_sem.at[1])
        own_out.start()
    with scope("ag3wait"):
        def finish(q):
            t, parts = blocks(q)

            @pl.when(q == 0)
            def _():
                wait(last.at[pl.ds(0, (xh * cols - 1) * mc)], recv_sem.at[LAST + t])

            @pl.when(q != 0)
            def _():
                wait(last.at[pl.ds(0, xh * cols * mc)], recv_sem.at[LAST + t])

            for part in parts:
                remote(last.at[part], left_out.at[part], LAST, partner, LASTF).start()
                pltpu.make_async_copy(last.at[part], left_out.at[part], in_sem.at[2]).start()

        loop(nt, finish)
    with scope("a2await"):
        own_out.wait()
        wait(second_out.at[pl.ds(0, d - 1)], recv_sem.at[7])
    with scope("ag3end"):
        wait(left_out.at[pl.ds(0, m // 2)], in_sem.at[2])
        wait(left_out.at[pl.ds(0, m // 2)], recv_sem.at[LASTF])
    with scope("sendwait"):
        wait(sleft_v.at[pl.ds(0, r - rr)], send_sem.at[0])
        wait(sright_v.at[pl.ds(0, cols - 1)], send_sem.at[1])
        wait(rc, send_sem.at[4])
        wait(sq, send_sem.at[4])
        wait(sright_new.at[pl.ds(0, half - 1)], send_sem.at[5])
        wait(sright_new.at[pl.ds(0, half)], send_sem.at[10])
        wait(second_out.at[pl.ds(0, d - 1)], send_sem.at[7])
        for turn, phase in ((0, 2), (1, 6)):
            wait(ra.at[turn, :, pl.ds(0, 10 - turn)], send_sem.at[phase])
            wait(ur.at[turn], send_sem.at[PAIR + turn])
            wait(pr.at[turn, pl.ds(0, half)], send_sem.at[PAIR + turn])
        wait(la.at[pl.ds(0, (half - 1) * mc)], send_sem.at[3])
        wait(la.at[pl.ds(0, half * mc)], send_sem.at[GATHER])
        wait(last.at[pl.ds(0, (half - 1) * mc)], send_sem.at[8])
        wait(last.at[pl.ds(0, half * mc)], send_sem.at[LAST])


def deliver(left, second, left_out, second_out, sem):
    outs = (pltpu.make_async_copy(left, left_out, sem.at[0]),
            pltpu.make_async_copy(second, second_out, sem.at[1]))
    for out in outs:
        out.start()
    for out in outs:
        out.wait()


def solution(mesh):
    rows, cols = mesh.shape["row"], mesh.shape["col"]
    d = rows * cols

    def body(slab, left, right, sleft, sright):
        m, width = slab.shape
        r = left.shape[1]
        depth = sright.shape[1] * cols
        jl = width // depth
        w = depth // 2
        nb = width // w
        mc = m // d
        rt = m // TILES
        own_k = depth // d
        sleft = sleft.reshape(r // rows, d, jl, r)
        sright = sright.T.reshape(d // cols, own_k, r)
        slab, left, right, sleft, sright = (
            pltpu.with_memory_space_constraint(x, pltpu.HBM)
            for x in (slab, left, right, sleft, sright))
        hbm = pl.BlockSpec(memory_space=pl.ANY)
        vmem = pl.BlockSpec(memory_space=pltpu.VMEM)
        left_out, second = pl.pallas_call(
            functools.partial(kernel, (rows, cols, m, r, w, jl, depth)),
            out_shape=(jax.ShapeDtypeStruct((m, r), F32),
                       jax.ShapeDtypeStruct((d, jl, r), F32)),
            in_specs=[hbm] * 5,
            out_specs=(vmem, vmem),
            scratch_shapes=[
                pltpu.VMEM((m, width), F32),
                pltpu.VMEM((m, r), F32),
                pltpu.VMEM((r, width), F32),
                pltpu.VMEM((nb, w, r), F32),
                pltpu.VMEM((r, jl, r), F32),
                pltpu.VMEM((cols, d // cols, own_k, r), F32),
                pltpu.VMEM((d, jl, r), F32),
                pltpu.VMEM((2 * rt, w), F32),
                pltpu.VMEM((TILES, rt, 2 * r), BF16),
                pltpu.VMEM((TILES, 2 * r, rt), BF16),
                pltpu.VMEM((nb, r, w), BF16),
                pltpu.VMEM((nb, w, 2 * r), BF16),
                pltpu.VMEM((nb, r, w), F32),
                pltpu.VMEM((r, 128), F32),
                pltpu.VMEM((8, r), F32),
                pltpu.VMEM((m, r), F32),
                pltpu.VMEM((mc, r), F32),
                pltpu.VMEM((mc, r), F32),
                pltpu.VMEM((m, r), F32),
                pltpu.VMEM((d // 2, own_k, r), F32),
                pltpu.VMEM((d // 2, own_k, r), F32),
                pltpu.VMEM((d // 2, own_k, r), F32),
                pltpu.VMEM((d // 2 - 1, own_k, r), F32),
                pltpu.VMEM((d, own_k, r), F32),
                pltpu.VMEM((own_k, r), F32),
                pltpu.VMEM((d, jl, r), F32),
                pltpu.VMEM((8, r), F32),
                pltpu.VMEM((jl // 2, 2 * r, 3 * r), BF16),
                pltpu.VMEM((jl // 2, 2 * r, 2 * r), BF16),
                pltpu.VMEM((jl // 2, 3 * r, 2 * r), BF16),
                pltpu.VMEM((2, jl // 2, w, 2 * r), F32),
                pltpu.VMEM((jl // 2, 2 * r, r), F32),
                pltpu.VMEM((2, 8, r), F32),
                pltpu.VMEM((2, 8, r), F32),
                pltpu.VMEM((2, d, mc, r), F32),
                pltpu.VMEM((2, d, mc, r), F32),
                pltpu.VMEM((2, d, 16, r), F32),
                pltpu.VMEM((2, d // 2 - 1, 16, r), F32),
                pltpu.SemaphoreType.DMA((nb,)),
                pltpu.SemaphoreType.DMA((5,)),
                pltpu.SemaphoreType.DMA((9 + 6 * TILES,)),
                pltpu.SemaphoreType.DMA((9 + 6 * TILES + 4,)),
            ],
            compiler_params=pltpu.CompilerParams(
                collective_id=0, has_side_effects=True, vmem_limit_bytes=LIMIT),
        )(slab, left, right, sleft, sright)
        second = second.reshape(d * jl, r)
        return pl.pallas_call(
            deliver,
            out_shape=(jax.ShapeDtypeStruct((m, r), F32),
                       jax.ShapeDtypeStruct((d * jl, r), F32)),
            in_specs=[vmem] * 2,
            out_specs=(hbm, hbm),
            scratch_shapes=[pltpu.SemaphoreType.DMA((2,))],
            compiler_params=pltpu.CompilerParams(vmem_limit_bytes=LIMIT),
        )(left_out, second)

    placed = (P(None, ("row", "col")), P(), P(None, ("row", "col")), P("row", None), P(None, "col"))
    return jax.shard_map(
        body, mesh=mesh, in_specs=placed, out_specs=(P(), P(("row", "col"), None)), check_vma=False
    )
```

```python
import contextlib
import functools

import jax
import jax.numpy as jnp
from jax import lax
from jax.experimental import pallas as pl
from jax.experimental.pallas import tpu as pltpu
from jax.sharding import PartitionSpec as P

F32 = jnp.float32
BF16 = jnp.bfloat16
NN = (((1,), (0,)), ((), ()))
NT = (((1,), (1,)), ((), ()))
TILES = 4
AHEAD = 1
CHUNK = 4
SCALE = 1.5
LIMIT = 40 * 1024 * 1024


def scope(_):
    return contextlib.nullcontext()


def mm(a, b, dims=NN):
    return lax.dot_general(a, b, dims, preferred_element_type=F32)


def split(x):
    high = x.astype(BF16)
    low = (x - high.astype(F32)).astype(BF16)
    return high, low


def inverse(x):
    guess = pl.reciprocal(x, approx=True)
    return guess * (2.0 - x * guess)


def three(high, low, axis):
    return jnp.concatenate([high, high, low], axis=axis)


def other_three(high, low, axis):
    return jnp.concatenate([high, low, high], axis=axis)


def kernel(sizes, slab, left, right, sleft, sright, left_out, second_out, *scratch):
    (rows, cols, m, r, w, jl, depth) = sizes
    (slab_v, left_v, right_v, right_t, sleft_v, sright_v, c2_v, noise, left2, left_t, rd, rpair,
     nacc, csum, sums_v, la, lc, mult, last, sp, sq, sc, rc, sright_new, cb, outv, keep,
     sl3, slpair, slt3, inv2, slf, ub, ur, sa, pr, sm, ra,
     slab_sem, in_sem, send_sem, recv_sem) = scratch
    d = rows * cols
    nt = TILES
    rt = m // nt
    nb = rd.shape[0]
    mc = m // d
    dt = d // nt
    xh = dt // (2 * cols)
    own_k = depth // d
    per = depth // w
    rr = r // rows
    half = d // 2
    my_row, my_col = lax.axis_index("row"), lax.axis_index("col")
    me = my_row * cols + my_col
    my_z = lax.div(me, dt)
    my_in = lax.rem(me, dt)
    core = lax.rem(my_row, 2)
    my_x = lax.rem(lax.div(my_row, 2), xh)
    partner = me + cols * (1 - 2 * core)
    PAIR, GATHER, FORWARD, LAST, LASTF = 9, 9 + 2 * nt, 9 + 3 * nt, 9 + 4 * nt, 9 + 5 * nt

    def wait(ref, sem):
        pltpu.make_async_copy(ref, ref, sem).wait()

    def remote(src, dst, phase, to, recv=None):
        return pltpu.make_async_remote_copy(
            src, dst, send_sem.at[phase], recv_sem.at[phase if recv is None else recv],
            device_id=to, device_id_type=pl.DeviceIdType.LOGICAL)

    def near_first(q):
        return lax.rem(my_z + lax.div(q * (q + 1), 2), nt)

    def loop(n, body, start=0, unroll=1):
        def step(k, _):
            body(k)
            return 0

        lax.fori_loop(start, n, step, 0, unroll=unroll)

    def offset(z):
        oz = z - my_z
        return jnp.where(oz < 0, oz + nt, oz)

    def to_whole_plane(z, start, first):
        def one(k):
            i = my_in + k
            start(z * dt + jnp.where(i >= dt, i - dt, i), first + k)

        loop(dt, one, 1, dt - 1)

        @pl.when(z != my_z)
        def _():
            one(0)

    def to_all(start):
        def plane(q):
            z = near_first(nt - 1 - q)
            to_whole_plane(z, start, offset(z) * dt - 1)

        loop(nt, plane)

    def to_plane(z, start, first=0):
        for ox in range(xh):
            x = my_x + ox
            x = jnp.where(x >= xh, x - xh, x)
            base = z * dt + (x * 2 + core) * cols

            def one(k, base=base, ox=ox, x=x):
                c = my_col + k
                c = jnp.where(c >= cols, c - cols, c)
                start(base + c, first + ox * cols + k, (z * xh + x) * cols + c)

            if ox == 0:
                @pl.when(z != my_z)
                def _():
                    one(0)
                loop(cols, one, 1, cols - 1)
            else:
                loop(cols, one, 0, cols)

    with scope("start"):
        left_in = pltpu.make_async_copy(left, left_v, in_sem.at[0])
        left_in.start()
        right_in = pltpu.make_async_copy(right, right_v, in_sem.at[3])
        right_in.start()
        barrier = pltpu.get_barrier_semaphore()

        def greet(k):
            t = me + k
            pl.semaphore_signal(barrier, inc=1, device_id=jnp.where(t >= d, t - d, t),
                                device_id_type=pl.DeviceIdType.LOGICAL)

        for g in range(nt):
            for k in range(max(1, g * dt), (g + 1) * dt):
                greet(k)
            for i in range(g * nb // nt, (g + 1) * nb // nt):
                part = pl.ds(i * w, w)
                pltpu.make_async_copy(slab.at[:, part], slab_v.at[:, part], slab_sem.at[i]).start()
        own_sleft = pltpu.make_async_copy(
            sleft.at[:, me], sleft_v.at[pl.ds(my_row * rr, rr)], in_sem.at[1])
        own_sleft.start()
        own_sright = pltpu.make_async_copy(sright, sright_v.at[my_col], in_sem.at[2])
        own_sright.start()
        c2_in = pltpu.make_async_copy(sleft.at[my_col], c2_v, in_sem.at[4])
        c2_in.start()

    def prepare(source, t):
        value = source[pl.ds(t * rt, rt), :]
        high, low = split(value * (1.0 / SCALE))
        left2[t] = jnp.concatenate([high, low], axis=1)
        turned = value.T
        high, low = split(turned)
        left_t[t] = jnp.concatenate([high, low], axis=0)
        csum[...] += SCALE * jnp.broadcast_to(jnp.sum(turned, axis=1, keepdims=True), csum.shape)

    def dither(i, t):
        at = pl.multiple_of(8 * lax.rem(11 * i + 9 * t + 5 * me, rt // 8), 8)
        return noise[pl.ds(at, rt), :]

    def products(count, one):
        ahead = [one(i) for i in range(AHEAD)]
        for i in range(count):
            if i + AHEAD < count:
                ahead.append(one(i + AHEAD))
            yield i, ahead[i]

    def right_times(i):
        return jnp.concatenate([rd[i], rd[i]], axis=0)

    def new_right(i, total, inv_c):
        cut = pl.ds(i * w, w)
        new = right_v[:, cut] * (total * inv_c)
        right_v[:, cut] = new
        turned = new.T
        right_t[i] = turned
        return new, turned

    def rounded_right(i, new, turned):
        rd[i] = (new * dither(i, 1)[:r]).astype(BF16)
        high, low = split(turned)
        rpair[i] = jnp.concatenate([high, low], axis=1)
        sums_v[0:1] += SCALE * jnp.sum(turned, axis=0, keepdims=True)

    def right_blocks(first, count):
        for g in range(count):
            i = first + g
            wait(slab_v.at[:, pl.ds(0, w)], slab_sem.at[i])
        parts = []
        for n, joint in products(count * nt, lambda n: mm(left2[n % nt], right_times(first + n // nt))):
            i, t = first + n // nt, n % nt
            rows_t, cut = slice(t * rt, (t + 1) * rt), pl.ds(i * w, w)
            top = slab_v[rows_t, cut] * dither(i, t)
            slab_v[rows_t, cut] = top
            parts.append((top * inverse(joint)).astype(BF16))
            if t == nt - 1:
                both = mm(jnp.concatenate([left_t[k] for k in range(nt)], axis=1),
                          jnp.concatenate(parts, axis=0))
                parts = []
                nacc[i] = both[:r] + both[r:]

    def quotients(t):
        part = pl.ds(t * rt, rt)
        lhs = left2[t]
        for i, joint in products(nb, lambda i: mm(lhs, right_times(i))):
            yield i, (slab_v[part, i * w:(i + 1) * w] * inverse(joint)).astype(BF16)

    def right_tile(t, inv_c=None):
        turned = left_t[t]
        for i, quotient in quotients(t):
            both = mm(turned, quotient)
            total = nacc[i] + both[:r] + both[r:]
            if inv_c is None:
                nacc[i] = total
            else:
                new_right(i, total, inv_c)

    def left_tile(t, buffer):
        total = jnp.zeros((rt, r), F32)
        parts = []
        for i, quotient in quotients(t):
            parts.append(quotient)
            if len(parts) == CHUNK:
                both = mm(jnp.concatenate(parts, axis=1),
                          jnp.concatenate([rpair[k] for k in range(i + 1 - CHUNK, i + 1)], axis=0))
                total += both[:, :r] + both[:, r:]
                parts = []
        buffer[pl.ds(t * dt, dt)] = total.reshape(dt, mc, r)

    def left_part(t, c, buffer):
        size = cols * mc
        starts = [(x * 2 + c) * size for x in range(xh)]
        lhs = jnp.concatenate([left2[t, pl.ds(at, size), :] for at in starts], axis=0)
        total = jnp.zeros((xh * size, r), F32)
        parts = []
        for i, joint in products(nb, lambda i: mm(lhs, right_times(i))):
            cut = slice(i * w, (i + 1) * w)
            top = jnp.concatenate([slab_v[pl.ds(t * rt + at, size), cut] for at in starts], axis=0)
            parts.append((top * inverse(joint)).astype(BF16))
            if len(parts) == CHUNK:
                both = mm(jnp.concatenate(parts, axis=1),
                          jnp.concatenate([rpair[k] for k in range(i + 1 - CHUNK, i + 1)], axis=0))
                total += both[:, :r] + both[:, r:]
                parts = []
        for x in range(xh):
            buffer[pl.ds(group(t, x, c), cols)] = total[x * size:(x + 1) * size].reshape(cols, mc, r)

    def reset():
        nacc[...] = jnp.zeros_like(nacc)
        csum[...] = jnp.zeros_like(csum)
        sums_v[...] = jnp.zeros_like(sums_v)

    def group(z, x, c):
        return z * dt + (x * 2 + c) * cols

    def left_sums(turn, phase):
        mine, theirs, message, arrived = sa.at[turn], pr.at[turn], sm.at[turn], ra.at[turn]
        remote(ub.at[turn], ur.at[turn], PAIR + turn, partner, 9 + 6 * nt + turn).start()

        rows_sent = 10 - turn

        def combine(q):
            t = near_first(nt - 1 - q)
            wait(theirs.at[pl.ds(0, xh * cols)], recv_sem.at[PAIR + turn * nt + q])
            for x in range(xh):
                part = pl.ds(group(t, x, core), cols)
                message[part, 0:mc, :] = mine[part] + theirs[part]
                message[part, 8:16, :] = jnp.broadcast_to((ub[turn] + ur[turn])[None], (cols, 8, r))
            to_plane(t, lambda to, slot, _: remote(
                message.at[to, pl.ds(0, rows_sent)], arrived.at[slot, pl.ds(0, rows_sent)],
                phase, to).start(), offset(t) * (xh * cols) - 1)

        def exchange(q):
            for x in range(xh):
                part = pl.ds(group(near_first(nt - 1 - q), x, 1 - core), cols)
                remote(mine.at[part], theirs.at[part], PAIR + turn, partner,
                       PAIR + turn * nt + q).start()

        def tile(q):
            left_tile(near_first(nt - 1 - q), mine)
            exchange(q)

            @pl.when(q == 1)
            def _():
                wait(ur.at[turn], recv_sem.at[9 + 6 * nt + turn])

            @pl.when(q > 0)
            def _():
                combine(q - 1)

        loop(nt - 1, tile)
        left_part(my_z, 1 - core, mine)
        exchange(nt - 1)
        combine(nt - 2)
        left_part(my_z, core, mine)
        combine(nt - 1)

    def owned(turn, phase, old):
        wait(ra.at[turn, :, pl.ds(0, 10 - turn)], recv_sem.at[phase])
        own = sm[turn, me]
        numer = own[:mc] + jnp.sum(ra[turn, :, 0:mc, :], axis=0)
        tail = own[8:10 - turn] + jnp.sum(ra[turn, :, 8:10 - turn, :], axis=0)
        return old * numer / tail[0:1], tail

    with scope("prep"):
        reset()
        down = lax.broadcasted_iota(jnp.int32, noise.shape, 0).astype(F32)
        across = lax.broadcasted_iota(jnp.int32, noise.shape, 1).astype(F32)
        one = down * 0.7548776662 + across * 0.5698402910
        two = down * 0.6710436067 + across * 0.8191725134
        noise[...] = 1.0 + ((one - jnp.floor(one)) + (two - jnp.floor(two)) - 1.0) * (1.0 / 128)
        left_in.wait()

        loop(nt, lambda t: prepare(left_v, t))
        right_in.wait()
        for i in range(nb):
            rd[i] = (right_v[:, i * w:(i + 1) * w] * dither(i, 1)[:r]).astype(BF16)

    line = lax.broadcasted_iota(jnp.int32, (8, r), 0)
    with scope("right1"):
        inv_c = 1.0 / csum[:, 0:1]

        def finish_blocks(first):
            for i in (first, first + 1):
                rounded_right(i, *new_right(i, nacc[i], inv_c))

        right_blocks(0, 2)

        def two_blocks(g):
            right_blocks(2 * g, 2)
            finish_blocks(2 * g - 2)

        loop(nb // 2, two_blocks, 1)
        finish_blocks(nb - 2)
        c2_in.wait()
        part2 = jnp.sum(jnp.sum(c2_v[...], axis=0), axis=0, keepdims=True)
        ub[0] = jnp.where(line == 0, sums_v[0:1], part2)

    with scope("barrier"):
        pl.semaphore_wait(barrier, d - 1)

    with scope("sendin"):
        def send_sleft(k):
            t = lax.rem(my_row + k, rows) * cols + my_col
            remote(sleft.at[:, t], sleft_v.at[pl.ds(my_row * rr, rr)], 0, t).start()

        def send_sright(k):
            t = my_row * cols + lax.rem(my_col + k, cols)
            remote(sright, sright_v.at[my_col], 1, t).start()

    with scope("left1"):
        left_sums(0, 2)

    with scope("sendin"):
        loop(rows, send_sleft, 1)
        loop(cols, send_sright, 1)
        reset()

    with scope("rs1wait"):
        new, tail = owned(0, 2, left_v[pl.ds(me * mc, mc), :])
        keep[...] = jnp.broadcast_to(tail[1:2], (8, r))
        lc[...] = new
        la[pl.ds(me * mc, mc), :] = new
    with scope("ag1send"):
        def share(to, slot, _):
            remote(lc, la.at[pl.ds(me * mc, mc)], 3, to, GATHER + my_z).start()

        loop(nt, lambda q: to_plane(near_first(q), share))

    def blocks(q):
        t = near_first(q)
        return t, [pl.ds(group(t, x, core) * mc, cols * mc) for x in range(xh)]

    with scope("slprep"):
        own_sleft.wait()
        wait(sleft_v.at[pl.ds(0, r - rr)], recv_sem.at[0])
        own_sright.wait()
        wait(sright_v.at[pl.ds(0, cols - 1)], recv_sem.at[1])
        for g in range(jl // 2):
            two = jnp.concatenate([sleft_v[:, 2 * g, :], sleft_v[:, 2 * g + 1, :]], axis=0)
            slf[g] = two
            high, low = split(two)
            sl3[g] = three(high, low, 1)
            slpair[g] = jnp.concatenate([high, low], axis=1)
            high, low = split(two.T)
            slt3[g] = other_three(high, low, 0)
        for h in range(per):
            high, low = split(sright_v[pl.ds(h * (cols // per), cols // per)].reshape(w, r))
            lhs = three(high, low, 1)
            for g in range(jl // 2):
                inv2[h, g] = inverse(mm(lhs, slt3[g]))

    with scope("right2"):
        def forward(q):
            t, parts = blocks(q)

            @pl.when(q == 0)
            def _():
                wait(la.at[pl.ds(0, (xh * cols - 1) * mc)], recv_sem.at[GATHER + t])

            @pl.when(q != 0)
            def _():
                wait(la.at[pl.ds(0, xh * cols * mc)], recv_sem.at[GATHER + t])

            for part in parts:
                remote(la.at[part], la.at[part], GATHER, partner, FORWARD + q).start()

        forward(0)

        def second(q):
            t = near_first(q)
            wait(la.at[pl.ds(0, xh * cols * mc)], recv_sem.at[FORWARD + q])
            prepare(la, t)
            right_tile(t)

            @pl.when(q == 0)
            def _():
                for k in range(1, nt - 1):
                    forward(k)

            @pl.when(q == 1)
            def _():
                forward(nt - 1)

        loop(nt - 1, second)
        t = near_first(nt - 1)
        wait(la.at[pl.ds(0, xh * cols * mc)], recv_sem.at[FORWARD + nt - 1])
        prepare(la, t)
        right_tile(t, 1.0 / csum[:, 0:1])

    chip = (my_z * xh + my_x) * cols + my_col
    mine_k = core * half + chip
    with scope("numer2"):
        def half_numer(h):
            total = jnp.zeros((w, r), F32)
            for g in range(jl // 2):
                value = jnp.concatenate(
                    [right_t[2 * g * per + h], right_t[(2 * g + 1) * per + h]], axis=1)
                qh, ql = split(value * inv2[h, g])
                both = mm(qh, slpair[g])
                total += both[:, :r] + both[:, r:] + mm(ql, slpair[g, :, :r])
            return total.reshape(half, own_k, r)

        sp[...] = half_numer(1 - core)
        remote(sp, sq, 4, partner, 9 + 6 * nt + 2).start()
        own2 = half_numer(core)
        wait(sq, recv_sem.at[9 + 6 * nt + 2])
        sc[...] = own2 + sq[...]
    with scope("rs2send"):
        def rs2(q):
            z = near_first(nt - 1 - q)
            to_plane(z, lambda to, slot, at: remote(sc.at[at], rc.at[slot], 4, to).start(),
                     offset(z) * (xh * cols) - 1)

        loop(nt, rs2)

    with scope("left2"):
        for i in range(nb):
            rounded_right(i, right_v[:, i * w:(i + 1) * w], right_t[i])
        ub[1] = jnp.broadcast_to(sums_v[0:1], (8, r))
        left_sums(1, 6)

    with scope("rs2wait"):
        wait(rc, recv_sem.at[4])
    with scope("rs2sum"):
        numer = sc[chip] + jnp.sum(rc[...], axis=0)
        cb[...] = (sright_v[lax.div(mine_k, d // cols), lax.rem(mine_k, d // cols)]
                   * numer / keep[0:1])
        sright_new[mine_k] = cb[...]
    with scope("ag2send"):
        def ag2(q):
            to_plane(near_first(nt - 1 - q), lambda to, slot, _: remote(
                cb, sright_new.at[mine_k], 5, to).start())

        loop(nt, ag2)
    with scope("rs3wait"):
        new, _ = owned(1, 6, la[pl.ds(me * mc, mc), :])
        mult[...] = new
        last[pl.ds(me * mc, mc), :] = new
    with scope("ag3send"):
        def ag3(q):
            to_plane(near_first(q), lambda to, slot, _: remote(
                mult, last.at[pl.ds(me * mc, mc)], 8, to, LAST + my_z).start())

        loop(nt, ag3)
    with scope("ag2wait"):
        wait(sright_new.at[pl.ds(0, half - 1)], recv_sem.at[5])
        part = pl.ds(core * half, half)
        remote(sright_new.at[part], sright_new.at[part], 10, partner, 9 + 6 * nt + 3).start()
    with scope("left3"):
        sums = jnp.zeros((1, r), F32)
        totals = [jnp.zeros((2 * r, r), F32) for _ in range(jl // 2)]
        for h in (core, 1 - core):
            if h is not core:
                wait(sright_new.at[pl.ds(0, half)], recv_sem.at[9 + 6 * nt + 3])
            part = sright_new[pl.ds(h * half, half)].reshape(w, r)
            sums += jnp.sum(part, axis=0, keepdims=True)
            high, low = split(part)
            pair = jnp.concatenate([high, low], axis=1)
            high, low = split(part.T)
            triple = other_three(high, low, 0)
            for g in range(jl // 2):
                joint = mm(sl3[g], triple)
                value = jnp.concatenate(
                    [right_v[:, pl.ds(pl.multiple_of((k * per + h) * w, w), w)]
                     for k in (2 * g, 2 * g + 1)], axis=0)
                qh, ql = split(value * inverse(joint))
                both = mm(qh, pair)
                totals[g] += both[:, :r] + both[:, r:] + mm(ql, pair[:, :r])
        inv_u = 1.0 / sums
        for g in range(jl // 2):
            result = slf[g] * (totals[g] * inv_u)
            outv[:, 2 * g, :] = result[:r]
            outv[:, 2 * g + 1, :] = result[r:]
    with scope("a2asend"):
        to_all(lambda to, slot: remote(outv.at[to], second_out.at[me], 7, to).start())
        own_out = pltpu.make_async_copy(outv.at[me], second_out.at[me], in_sem.at[1])
        own_out.start()
    with scope("ag3wait"):
        def finish(q):
            t, parts = blocks(q)

            @pl.when(q == 0)
            def _():
                wait(last.at[pl.ds(0, (xh * cols - 1) * mc)], recv_sem.at[LAST + t])

            @pl.when(q != 0)
            def _():
                wait(last.at[pl.ds(0, xh * cols * mc)], recv_sem.at[LAST + t])

            for part in parts:
                remote(last.at[part], left_out.at[part], LAST, partner, LASTF).start()
                pltpu.make_async_copy(last.at[part], left_out.at[part], in_sem.at[2]).start()

        loop(nt, finish)
    with scope("a2await"):
        own_out.wait()
        wait(second_out.at[pl.ds(0, d - 1)], recv_sem.at[7])
    with scope("ag3end"):
        wait(left_out.at[pl.ds(0, m // 2)], in_sem.at[2])
        wait(left_out.at[pl.ds(0, m // 2)], recv_sem.at[LASTF])
    with scope("sendwait"):
        wait(sleft_v.at[pl.ds(0, r - rr)], send_sem.at[0])
        wait(sright_v.at[pl.ds(0, cols - 1)], send_sem.at[1])
        wait(rc, send_sem.at[4])
        wait(sq, send_sem.at[4])
        wait(sright_new.at[pl.ds(0, half - 1)], send_sem.at[5])
        wait(sright_new.at[pl.ds(0, half)], send_sem.at[10])
        wait(second_out.at[pl.ds(0, d - 1)], send_sem.at[7])
        for turn, phase in ((0, 2), (1, 6)):
            wait(ra.at[turn, :, pl.ds(0, 10 - turn)], send_sem.at[phase])
            wait(ur.at[turn], send_sem.at[PAIR + turn])
            wait(pr.at[turn, pl.ds(0, half)], send_sem.at[PAIR + turn])
        wait(la.at[pl.ds(0, (half - 1) * mc)], send_sem.at[3])
        wait(la.at[pl.ds(0, half * mc)], send_sem.at[GATHER])
        wait(last.at[pl.ds(0, (half - 1) * mc)], send_sem.at[8])
        wait(last.at[pl.ds(0, half * mc)], send_sem.at[LAST])


def deliver(left, second, left_out, second_out, sem):
    outs = (pltpu.make_async_copy(left, left_out, sem.at[0]),
            pltpu.make_async_copy(second, second_out, sem.at[1]))
    for out in outs:
        out.start()
    for out in outs:
        out.wait()


def solution(mesh):
    rows, cols = mesh.shape["row"], mesh.shape["col"]
    d = rows * cols

    def body(slab, left, right, sleft, sright):
        m, width = slab.shape
        r = left.shape[1]
        depth = sright.shape[1] * cols
        jl = width // depth
        w = depth // 2
        nb = width // w
        mc = m // d
        rt = m // TILES
        own_k = depth // d
        sleft = sleft.reshape(r // rows, d, jl, r)
        sright = sright.T.reshape(d // cols, own_k, r)
        slab, left, right, sleft, sright = (
            pltpu.with_memory_space_constraint(x, pltpu.HBM)
            for x in (slab, left, right, sleft, sright))
        hbm = pl.BlockSpec(memory_space=pl.ANY)
        vmem = pl.BlockSpec(memory_space=pltpu.VMEM)
        left_out, second = pl.pallas_call(
            functools.partial(kernel, (rows, cols, m, r, w, jl, depth)),
            out_shape=(jax.ShapeDtypeStruct((m, r), F32),
                       jax.ShapeDtypeStruct((d, jl, r), F32)),
            in_specs=[hbm] * 5,
            out_specs=(vmem, vmem),
            scratch_shapes=[
                pltpu.VMEM((m, width), F32),
                pltpu.VMEM((m, r), F32),
                pltpu.VMEM((r, width), F32),
                pltpu.VMEM((nb, w, r), F32),
                pltpu.VMEM((r, jl, r), F32),
                pltpu.VMEM((cols, d // cols, own_k, r), F32),
                pltpu.VMEM((d, jl, r), F32),
                pltpu.VMEM((2 * rt, w), F32),
                pltpu.VMEM((TILES, rt, 2 * r), BF16),
                pltpu.VMEM((TILES, 2 * r, rt), BF16),
                pltpu.VMEM((nb, r, w), BF16),
                pltpu.VMEM((nb, w, 2 * r), BF16),
                pltpu.VMEM((nb, r, w), F32),
                pltpu.VMEM((r, 128), F32),
                pltpu.VMEM((8, r), F32),
                pltpu.VMEM((m, r), F32),
                pltpu.VMEM((mc, r), F32),
                pltpu.VMEM((mc, r), F32),
                pltpu.VMEM((m, r), F32),
                pltpu.VMEM((d // 2, own_k, r), F32),
                pltpu.VMEM((d // 2, own_k, r), F32),
                pltpu.VMEM((d // 2, own_k, r), F32),
                pltpu.VMEM((d // 2 - 1, own_k, r), F32),
                pltpu.VMEM((d, own_k, r), F32),
                pltpu.VMEM((own_k, r), F32),
                pltpu.VMEM((d, jl, r), F32),
                pltpu.VMEM((8, r), F32),
                pltpu.VMEM((jl // 2, 2 * r, 3 * r), BF16),
                pltpu.VMEM((jl // 2, 2 * r, 2 * r), BF16),
                pltpu.VMEM((jl // 2, 3 * r, 2 * r), BF16),
                pltpu.VMEM((2, jl // 2, w, 2 * r), F32),
                pltpu.VMEM((jl // 2, 2 * r, r), F32),
                pltpu.VMEM((2, 8, r), F32),
                pltpu.VMEM((2, 8, r), F32),
                pltpu.VMEM((2, d, mc, r), F32),
                pltpu.VMEM((2, d, mc, r), F32),
                pltpu.VMEM((2, d, 16, r), F32),
                pltpu.VMEM((2, d // 2 - 1, 16, r), F32),
                pltpu.SemaphoreType.DMA((nb,)),
                pltpu.SemaphoreType.DMA((5,)),
                pltpu.SemaphoreType.DMA((9 + 6 * TILES,)),
                pltpu.SemaphoreType.DMA((9 + 6 * TILES + 4,)),
            ],
            compiler_params=pltpu.CompilerParams(
                collective_id=0, has_side_effects=True, vmem_limit_bytes=LIMIT),
        )(slab, left, right, sleft, sright)
        second = second.reshape(d * jl, r)
        return pl.pallas_call(
            deliver,
            out_shape=(jax.ShapeDtypeStruct((m, r), F32),
                       jax.ShapeDtypeStruct((d * jl, r), F32)),
            in_specs=[vmem] * 2,
            out_specs=(hbm, hbm),
            scratch_shapes=[pltpu.SemaphoreType.DMA((2,))],
            compiler_params=pltpu.CompilerParams(vmem_limit_bytes=LIMIT),
        )(left_out, second)

    placed = (P(None, ("row", "col")), P(), P(None, ("row", "col")), P("row", None), P(None, "col"))
    return jax.shard_map(
        body, mesh=mesh, in_specs=placed, out_specs=(P(), P(("row", "col"), None)), check_vma=False
    )
```
